32 devices in a mesh: gx: 4 (over z), gy: 8 (over y, x, core).
Axes of the slice: x: 2, y: 2, z: 4, core: 2. Of those that a mesh axis runs over, the one named last changes fastest.
Arguments:
- gauss_params: float32 [55, 65536], P(None, ('gx', 'gy')), may hold values from -16 to 2064, as said below
- first_moment: float32 [55, 65536], P(None, ('gx', 'gy')), may hold values from -0.3 to 0.3
- second_moment: float32 [55, 65536], P(None, ('gx', 'gy')), may hold values from 0.001 to 0.1
- splat_lists: int32 [2, 512, 512], P(None, ('gx', 'gy')), may hold values from 0 to 65535, as said below
- tile_ids: int32 [2, 512], P(None, ('gx', 'gy')), may hold values from 0 to 2047, as said below
- targets: float32 [2, 512, 3, 256], P(None, ('gx', 'gy')), may hold values from 0 to 1
- camera: float32 [2, 2], replicated, may hold values from -3 to 3
Outputs:
- updated_params: float32 [55, 65536], P(None, ('gx', 'gy'))
- updated_first: float32 [55, 65536], P(None, ('gx', 'gy'))
- updated_second: float32 [55, 65536], P(None, ('gx', 'gy'))
- rendered: float32 [2, 512, 3, 256], P(None, ('gx', 'gy'))
- loss: float32 [2], replicated
The draws below stay inside these ranges and needn't reach their ends.
Inputs may be any that keep to these rules, and one draw needn't show every extreme that they name: `gauss_params`: rows of each column: x and y (positions scaled by depth), depth z in [1, 2], two log scales, an angle, an opacity logit, then 16 harmonic coefficients for red, green and blue in turn. `splat_lists`: gaussian ids; the Gaussians with ids k * 2048 to (k + 1) * 2048 - 1 belong to device k along gx+gy. In each step, the entries of one device's 16 tile slots name Gaussians of one owner at most 512 times, and some owner is named exactly 512 times by every device. `tile_ids`: image tiles numbered row by row over 64 columns; within a step, slots show distinct tiles while 512 <= 2048.
All inputs are finite; a program needn't handle non-finite values.
Results may differ from the reference program's by a relative error of at most 0.0014.
Values sent between devices are 32-bit elements; how exact they have to be, the bound alone decides.
No kernel may reach another device: no remote copies, remote signals or barrier semaphores. Data moves between devices by JAX's collectives and lax.ppermute only.
A program may use at most 64 MiB of HBM per device.

```python
import math
import jax
import jax.numpy as jnp
from jax import lax

SIDE = 16
PIX = 256
K = 512
NCOEF = 16
PROWS = 55
STEPS = 2
IMG_TX = 64
IMG_TY = 32
NT_IMG = 2048
G_DEV = 2048
OWNERS = 32
GAUSS = 65536
TILES = 512
S_DEV = 8192
CAP = 512


depth_levels = 4096


def depth_table(base_key):
    return jax.random.randint(jax.random.fold_in(base_key, 7), (GAUSS,), 0, depth_levels, dtype=jnp.int32)


def list_parts(base_key, step_index):
    step_key = jax.random.fold_in(base_key, 1000 + step_index)
    key_perm, key_heavy, key_weight, key_shuffle, key_near, key_copy = jax.random.split(step_key, 6)
    tile_order = jax.random.permutation(key_perm, NT_IMG).astype(jnp.int32)
    tiles_drawn = tile_order[jnp.arange(TILES, dtype=jnp.int32) % NT_IMG]
    heavy_owner = jax.random.randint(key_heavy, (), 0, OWNERS, dtype=jnp.int32)
    owner_range = jnp.arange(OWNERS, dtype=jnp.int32)
    weights = jax.random.randint(key_weight, (OWNERS, OWNERS), 2, 4, dtype=jnp.int32)
    weights = jnp.where(owner_range[None, :] == heavy_owner, 0, weights)
    running = jnp.cumsum(weights, axis=1)
    ends_at = running * (S_DEV - CAP) // running[:, -1:]
    counts = ends_at - jnp.concatenate([jnp.zeros((OWNERS, 1), jnp.int32), ends_at[:, :-1]], 1)
    counts = counts + jnp.where(owner_range[None, :] == heavy_owner, CAP, 0)
    limits = jnp.cumsum(counts, axis=1)
    slot_index = jnp.arange(S_DEV, dtype=jnp.int32)
    sequence = jax.vmap(lambda limit_row: jnp.searchsorted(limit_row, slot_index, side='right'))(limits).astype(jnp.int32)
    shuffles = jax.vmap(lambda shuffle_key: jax.random.permutation(shuffle_key, S_DEV))(jax.random.split(key_shuffle, OWNERS))
    owner_of = jnp.take_along_axis(sequence, shuffles.astype(jnp.int32), axis=1).reshape(TILES, K)
    tile_x = tiles_drawn % IMG_TX
    tile_y = tiles_drawn // IMG_TX
    nearby = jax.random.randint(key_near, (2, TILES, K), -1, 2, dtype=jnp.int32)
    near_x = jnp.clip(tile_x[:, None] + nearby[0], 0, IMG_TX - 1)
    near_y = jnp.clip(tile_y[:, None] + nearby[1], 0, IMG_TY - 1)
    home_tile = near_y * IMG_TX + near_x
    copy_index = jax.random.randint(key_copy, (TILES, K), 0, G_DEV // NT_IMG, dtype=jnp.int32)
    gauss_id = owner_of * G_DEV + copy_index * NT_IMG + home_tile
    depth_key = depth_table(base_key)[gauss_id]
    scores = depth_key * K + jnp.arange(K, dtype=jnp.int32)[None, :]
    order_in = jnp.argsort(scores, axis=1)
    gauss_id = jnp.take_along_axis(gauss_id, order_in, axis=1)
    return (tiles_drawn.astype(jnp.int32), gauss_id.astype(jnp.int32))


def draw_splat_lists(key, part):
    return jnp.stack([list_parts(key, step_index)[1] for step_index in range(STEPS)])


def draw_tile_ids(key, part):
    return jnp.stack([list_parts(key, step_index)[0] for step_index in range(STEPS)])


def draw_gauss_params(key, part):
    index_all = jnp.arange(GAUSS, dtype=jnp.int32)
    home_tile = index_all % G_DEV % NT_IMG
    centre_x = (home_tile % IMG_TX).astype(jnp.float32) * SIDE + 0.5 * SIDE
    centre_y = (home_tile // IMG_TX).astype(jnp.float32) * SIDE + 0.5 * SIDE
    float_keys = jax.random.split(jax.random.fold_in(key, 23), 7)
    depth_z = 1.0 + (depth_table(key).astype(jnp.float32) + jax.random.uniform(float_keys[0], (GAUSS,))) / depth_levels
    jitter = jnp.clip(6.0 * jax.random.normal(float_keys[1], (2, GAUSS)), -16.0, 16.0)
    spread = jnp.exp(jax.random.uniform(float_keys[2], (2, GAUSS), minval=math.log(3.0), maxval=math.log(10.0)))
    logit_value = jax.random.uniform(float_keys[3], (GAUSS,), minval=-3.5, maxval=-1.0)
    coeffs = jnp.clip(0.25 * jax.random.normal(float_keys[5], (3 * NCOEF, GAUSS)), -1.0, 1.0)
    angle_value = jax.random.uniform(float_keys[6], (GAUSS,), minval=-math.pi, maxval=math.pi)
    geometry = jnp.stack([(centre_x + jitter[0]) * depth_z, (centre_y + jitter[1]) * depth_z, depth_z, jnp.log(spread[0] * depth_z), jnp.log(spread[1] * depth_z), angle_value, logit_value])
    return jnp.concatenate([geometry, coeffs], 0).astype(jnp.float32)


def shard_levels(stream_key, extent, pieces, low, top_value):
    gain = 1.0
    for position, parts in pieces:
        steps = jax.random.uniform(jax.random.fold_in(jax.random.fold_in(stream_key, 6), position), (parts,), jnp.float32, low / len(pieces), top_value / len(pieces))
        gain = gain * jnp.repeat(jnp.exp(steps), extent[position] // parts).reshape((-1,) + (1,) * (len(extent) - 1 - position))
    return gain


def normal_values(rng, shape, scale, reach, shards=(), held_as=jnp.bfloat16):
    factor_of = shard_levels(rng, shape, shards, -0.22, 0.18) if shards else 1.0
    result = jax.random.normal(rng, shape, jnp.float32) * scale * factor_of
    return jnp.minimum(jnp.maximum(result, -reach), reach).astype(held_as)


def setup_inputs(seed: int = 0) -> dict:
    streams_of = jax.random.split(jax.random.key(seed), 8)
    return {
        "gauss_params": draw_gauss_params(jax.random.fold_in(streams_of[7], 71), 0),
        "first_moment": normal_values(streams_of[1], (PROWS, GAUSS), 0.05, 0.3, ((1, 32),), jnp.float32),
        "second_moment": jnp.clip(jnp.exp(math.log(0.1) - 4.6051702 * jax.random.uniform(streams_of[2], (PROWS, GAUSS), jnp.float32) ** shard_levels(streams_of[2], (PROWS, GAUSS), ((1, 32),), -0.2, 0.2)), 0.001, 0.1),
        "splat_lists": draw_splat_lists(jax.random.fold_in(streams_of[7], 71), 0),
        "tile_ids": draw_tile_ids(jax.random.fold_in(streams_of[7], 71), 0),
        "targets": jnp.clip(1.0 * jax.random.uniform(streams_of[5], (STEPS, TILES, 3, PIX), jnp.float32) ** shard_levels(streams_of[5], (STEPS, TILES, 3, PIX), ((1, 32),), -0.2, 0.2), 0.0, 1.0),
        "camera": jnp.clip(jax.random.uniform(streams_of[6], (STEPS, 2), jnp.float32, -3.0, 3.0), -3.0, 3.0),
    }


beta_one = 0.9
beta_two = 0.999
adam_eps = 1e-08
learn_rate = 0.01
adam_start = 1000
splat_fields = 9
band_zero = 0.28209479177387814
band_one = 0.4886025119029199
band_two = (1.0925484305920792, -1.0925484305920792, 0.31539156525252005, -1.0925484305920792, 0.5462742152960396)
band_three = (-0.5900435899266435, 2.890611442640554, -0.4570457994644658, 0.3731763325901154, -0.4570457994644658, 1.445305721320277, -0.5900435899266435)

def harmonics(ray_x, ray_y, ray_z):
    sq_x = ray_x * ray_x
    sq_y = ray_y * ray_y
    sq_z = ray_z * ray_z
    return jnp.stack([band_zero * jnp.ones_like(ray_x), -band_one * ray_y, band_one * ray_z, -band_one * ray_x, band_two[0] * ray_x * ray_y, band_two[1] * ray_y * ray_z, band_two[2] * (2.0 * sq_z - sq_x - sq_y), band_two[3] * ray_x * ray_z, band_two[4] * (sq_x - sq_y), band_three[0] * ray_y * (3.0 * sq_x - sq_y), band_three[1] * ray_x * ray_y * ray_z, band_three[2] * ray_y * (4.0 * sq_z - sq_x - sq_y), band_three[3] * ray_z * (2.0 * sq_z - 3.0 * sq_x - 3.0 * sq_y), band_three[4] * ray_x * (4.0 * sq_z - sq_x - sq_y), band_three[5] * ray_z * (sq_x - sq_y), band_three[6] * ray_x * (sq_x - 3.0 * sq_y)])

def project(gauss_rows, camera_row):
    image_width = 1.0 * SIDE * IMG_TX
    image_height = 1.0 * SIDE * IMG_TY
    depth_z = gauss_rows[2]
    screen_u = (gauss_rows[0] - camera_row[0]) / depth_z
    screen_v = (gauss_rows[1] - camera_row[1]) / depth_z
    inv_one = depth_z * depth_z * jnp.exp(-2.0 * gauss_rows[3])
    inv_two = depth_z * depth_z * jnp.exp(-2.0 * gauss_rows[4])
    cosine = jnp.cos(gauss_rows[5])
    sine_angle = jnp.sin(gauss_rows[5])
    conic_a = cosine * cosine * inv_one + sine_angle * sine_angle * inv_two
    conic_b = cosine * sine_angle * (inv_one - inv_two)
    conic_c = sine_angle * sine_angle * inv_one + cosine * cosine * inv_two
    opacity = 0.99 * jax.nn.sigmoid(gauss_rows[6])
    ray_x = (screen_u - 0.5 * image_width) / image_width
    ray_y = (screen_v - 0.5 * image_height) / image_width
    factor = lax.rsqrt(ray_x * ray_x + ray_y * ray_y + 1.0)
    harmonic_basis = harmonics(ray_x * factor, ray_y * factor, factor)
    coeffs = gauss_rows[7:].reshape(3, NCOEF, gauss_rows.shape[1])
    colour = 0.5 + lax.optimization_barrier(jnp.sum(coeffs * harmonic_basis[None], axis=1))
    geometry = jnp.stack([screen_u, screen_v, conic_a, conic_b, conic_c, opacity])
    return jnp.concatenate([geometry, colour], 0)

def pixel_grid(tile_row):
    cell_index = jnp.arange(SIDE * SIDE, dtype=jnp.int32)
    column = (tile_row % IMG_TX)[:, None] * SIDE + cell_index % SIDE
    row_pix = (tile_row // IMG_TX)[:, None] * SIDE + cell_index // SIDE
    return jnp.stack([column, row_pix], 1).astype(jnp.float32) + 0.5

def render(splat_rows, centres):
    delta_x = centres[0][None, :] - splat_rows[0][:, None]
    delta_y = centres[1][None, :] - splat_rows[1][:, None]
    exponent = -0.5 * (splat_rows[2][:, None] * delta_x * delta_x + 2.0 * splat_rows[3][:, None] * delta_x * delta_y + splat_rows[4][:, None] * delta_y * delta_y)
    opaque = splat_rows[5][:, None] * jnp.exp(exponent)
    log_keep = jnp.log1p(-opaque)
    before = jnp.cumsum(log_keep, axis=0) - log_keep
    weight = jnp.exp(before) * opaque
    return jnp.dot(splat_rows[6:9], weight, precision=lax.Precision.HIGHEST, preferred_element_type=jnp.float32)

def tile_terms(splat_rows, centres, target):
    picture, pullback = jax.vjp(lambda values: render(values, centres), splat_rows)
    residual = picture - target
    return (picture, pullback(residual)[0], 0.5 * jnp.sum(residual * residual))

def adam_update(params, moment_one, second, gradient, step_index):
    step_count = adam_start + step_index + 1
    moment_one = beta_one * moment_one + (1.0 - beta_one) * gradient
    second = beta_two * second + (1.0 - beta_two) * gradient * gradient
    scaled_first = moment_one / (1.0 - beta_one ** step_count)
    scaled_second = second / (1.0 - beta_two ** step_count)
    params = params - learn_rate * scaled_first / (jnp.sqrt(scaled_second) + adam_eps)
    return (params, moment_one, second)

def reference(gauss_params, first_moment, second_moment, splat_lists, tile_ids, targets, camera):
    params, moment_one, moment_two = (gauss_params, first_moment, second_moment)
    pictures = []
    losses = []
    for step_index in range(STEPS):
        camera_row = camera[step_index]
        projected, pullback = jax.vjp(lambda values: project(values, camera_row), params)
        listed = splat_lists[step_index].astype(jnp.int32)
        gathered = jnp.moveaxis(projected[:, listed], 1, 0)
        centres = pixel_grid(tile_ids[step_index].astype(jnp.int32))
        picture, slot_grads, halves = lax.map(lambda tile_parts: tile_terms(tile_parts[0], tile_parts[1], tile_parts[2]), (gathered, centres, targets[step_index]))
        flat_grads = jnp.moveaxis(slot_grads, 0, 1).reshape(splat_fields, -1)
        summed = jnp.zeros_like(projected).at[:, listed.reshape(-1)].add(flat_grads)
        gradient = pullback(summed)[0]
        params, moment_one, moment_two = adam_update(params, moment_one, moment_two, gradient, step_index)
        pictures.append(picture)
        losses.append(jnp.sum(halves) / (3.0 * SIDE * SIDE * TILES))
    return (params, moment_one, moment_two, jnp.stack(pictures), jnp.stack(losses))
```

```python
import functools

import jax
import jax.numpy as jnp
from jax import lax
from jax.experimental import pallas as pl
from jax.experimental.pallas import tpu as pltpu
from jax.sharding import PartitionSpec as P

SIDE = 16
NCOEF = 16
STEPS = 2
IMG_TX = 64
IMG_TY = 32

FIELDS = 9
LANES = 128
ROWSUB = 8
AXES = ("gx", "gy")

beta_one = 0.9
beta_two = 0.999
adam_eps = 1e-08
learn_rate = 0.01
adam_start = 1000
band_zero = 0.28209479177387814
band_one = 0.4886025119029199
band_two = (
    1.0925484305920792,
    -1.0925484305920792,
    0.31539156525252005,
    -1.0925484305920792,
    0.5462742152960396,
)
band_three = (
    -0.5900435899266435,
    2.890611442640554,
    -0.4570457994644658,
    0.3731763325901154,
    -0.4570457994644658,
    1.445305721320277,
    -0.5900435899266435,
)
LOG2E = 1.4426950408889634
LOG_CAP = -0.01005033585350145


def harmonic_rows(ray_x, ray_y, ray_z):
    sq_x = ray_x * ray_x
    sq_y = ray_y * ray_y
    sq_z = ray_z * ray_z
    return [
        band_zero * jnp.ones_like(ray_x),
        -band_one * ray_y,
        band_one * ray_z,
        -band_one * ray_x,
        band_two[0] * ray_x * ray_y,
        band_two[1] * ray_y * ray_z,
        band_two[2] * (2.0 * sq_z - sq_x - sq_y),
        band_two[3] * ray_x * ray_z,
        band_two[4] * (sq_x - sq_y),
        band_three[0] * ray_y * (3.0 * sq_x - sq_y),
        band_three[1] * ray_x * ray_y * ray_z,
        band_three[2] * ray_y * (4.0 * sq_z - sq_x - sq_y),
        band_three[3] * ray_z * (2.0 * sq_z - 3.0 * sq_x - 3.0 * sq_y),
        band_three[4] * ray_x * (4.0 * sq_z - sq_x - sq_y),
        band_three[5] * ray_z * (sq_x - sq_y),
        band_three[6] * ray_x * (sq_x - 3.0 * sq_y),
    ]


def geometry_rows(p0, p1, p2, p3, p4, p5, p6, cam_x, cam_y):
    screen_u = (p0 - cam_x) / p2
    screen_v = (p1 - cam_y) / p2
    inv_one = p2 * p2 * jnp.exp(-2.0 * p3)
    inv_two = p2 * p2 * jnp.exp(-2.0 * p4)
    cosine = jnp.cos(p5)
    sine = jnp.sin(p5)
    conic_a = cosine * cosine * inv_one + sine * sine * inv_two
    conic_b = cosine * sine * (inv_one - inv_two)
    conic_c = sine * sine * inv_one + cosine * cosine * inv_two
    tail = jnp.log(1.0 + jnp.exp(-jnp.abs(p6)))
    log_opacity = LOG_CAP - (jnp.maximum(-p6, 0.0) + tail)
    return screen_u, screen_v, conic_a, conic_b, conic_c, log_opacity


def ray_rows(screen_u, screen_v):
    image_width = 1.0 * SIDE * IMG_TX
    image_height = 1.0 * SIDE * IMG_TY
    ray_x = (screen_u - 0.5 * image_width) / image_width
    ray_y = (screen_v - 0.5 * image_height) / image_width
    factor = lax.rsqrt(ray_x * ray_x + ray_y * ray_y + 1.0)
    return ray_x, ray_y, factor


def project_to(param_ref, cam_x, cam_y, out_ref):
    rows = [param_ref[i : i + 1, :] for i in range(7)]
    geo = geometry_rows(*rows, cam_x, cam_y)
    ray_x, ray_y, factor = ray_rows(geo[0], geo[1])
    basis = jnp.concatenate(harmonic_rows(ray_x * factor, ray_y * factor, factor), 0)
    colours = []
    for ch in range(3):
        coef = param_ref[7 + NCOEF * ch : 7 + NCOEF * (ch + 1), :]
        colours.append(0.5 + jnp.sum(coef * basis, axis=0, keepdims=True))
    fields = jnp.concatenate(list(geo) + colours, 0)
    per_field = fields.shape[1] // LANES
    for k in range(per_field):
        out_ref[pl.ds(k, FIELDS, stride=per_field), :] = fields[:, k * LANES : (k + 1) * LANES]


def project_kernel(cam_ref, param_ref, out_ref, *, step):
    project_to(param_ref, cam_ref[step, 0], cam_ref[step, 1], out_ref)


def gradient_to(param_ref, cam_x, cam_y, grad_ref, full_ref):
    count = param_ref.shape[1]
    per_field = count // LANES
    pieces = [grad_ref[pl.ds(k, FIELDS, stride=per_field), :] for k in range(per_field)]
    grads = jnp.concatenate(pieces, 1)
    g = [grads[i : i + 1, :] for i in range(FIELDS)]
    p0, p1, p2, p3, p4, p5, p6 = [param_ref[i : i + 1, :] for i in range(7)]
    inv_z = 1.0 / p2
    screen_u = (p0 - cam_x) / p2
    screen_v = (p1 - cam_y) / p2
    inv_one = p2 * p2 * jnp.exp(-2.0 * p3)
    inv_two = p2 * p2 * jnp.exp(-2.0 * p4)
    cosine = jnp.cos(p5)
    sine = jnp.sin(p5)
    cc = cosine * cosine
    ss = sine * sine
    cs = cosine * sine
    ray_x, ray_y, factor = ray_rows(screen_u, screen_v)
    nx, ny, nz = ray_x * factor, ray_y * factor, factor
    basis_rows, basis_vjp = jax.vjp(lambda a, b, c: tuple(harmonic_rows(a, b, c)), nx, ny, nz)
    basis = jnp.concatenate(basis_rows, 0)
    d_basis = jnp.zeros_like(basis)
    for ch in range(3):
        coef = param_ref[7 + NCOEF * ch : 7 + NCOEF * (ch + 1), :]
        full_ref[7 + NCOEF * ch : 7 + NCOEF * (ch + 1), :] = g[6 + ch] * basis
        d_basis = d_basis + g[6 + ch] * coef
    d_nx, d_ny, d_nz = basis_vjp(tuple(d_basis[i : i + 1, :] for i in range(NCOEF)))
    dot = d_nx * nx + d_ny * ny + d_nz * nz
    image_width = 1.0 * SIDE * IMG_TX
    d_u = g[0] + factor * (d_nx - nx * dot) / image_width
    d_v = g[1] + factor * (d_ny - ny * dot) / image_width
    d_one = g[2] * cc + g[3] * cs + g[4] * ss
    d_two = g[2] * ss - g[3] * cs + g[4] * cc
    diff = inv_one - inv_two
    d_angle = diff * (2.0 * cs * (g[4] - g[2]) + (cc - ss) * g[3])
    d_x = d_u * inv_z
    d_y = d_v * inv_z
    d_z = 2.0 * (d_one * inv_one + d_two * inv_two) * inv_z - d_x * screen_u - d_y * screen_v
    full_ref[0:1, :] = d_x
    full_ref[1:2, :] = d_y
    full_ref[2:3, :] = d_z
    full_ref[3:4, :] = -2.0 * inv_one * d_one
    full_ref[4:5, :] = -2.0 * inv_two * d_two
    full_ref[5:6, :] = d_angle
    full_ref[6:7, :] = g[5] / (1.0 + jnp.exp(p6))


def update_kernel(
    cam_ref, param_ref, first_ref, second_ref, grad_ref, *refs, step, project_next
):
    if project_next:
        new_param, new_first, new_second, field_ref, full_ref = refs
    else:
        new_param, new_first, new_second, full_ref = refs
    gradient_to(param_ref, cam_ref[step, 0], cam_ref[step, 1], grad_ref, full_ref)
    step_count = adam_start + step + 1
    gradient = full_ref[...]
    first = beta_one * first_ref[...] + (1.0 - beta_one) * gradient
    second = beta_two * second_ref[...] + (1.0 - beta_two) * gradient * gradient
    scaled_first = first / (1.0 - beta_one**step_count)
    scaled_second = second / (1.0 - beta_two**step_count)
    new_first[...] = first
    new_second[...] = second
    new_param[...] = param_ref[...] - learn_rate * scaled_first / (
        jnp.sqrt(scaled_second) + adam_eps
    )
    if project_next:
        project_to(new_param, cam_ref[step + 1, 0], cam_ref[step + 1, 1], field_ref)


def split_two(values):
    high = values.astype(jnp.bfloat16)
    rest = (values - high.astype(jnp.float32)).astype(jnp.bfloat16)
    return high, rest


def pixel_basis(rows):
    pix = lax.broadcasted_iota(jnp.int32, (rows, SIDE * SIDE), 1)
    which = lax.broadcasted_iota(jnp.int32, (rows, SIDE * SIDE), 0)
    x = (pix % SIDE).astype(jnp.float32) + (0.5 - 0.5 * SIDE)
    y = (pix // SIDE).astype(jnp.float32) + (0.5 - 0.5 * SIDE)
    which = which % 8
    out = jnp.where(which == 0, 1.0, 0.0)
    for index, value in enumerate((x, y, x * x, x * y, y * y)):
        out = jnp.where(which == index + 1, value, out)
    return out


def dot_nn(a, b):
    return jnp.dot(a, b, preferred_element_type=jnp.float32)


def dot_nt(a, b):
    return lax.dot_general(
        a, b, (((1,), (1,)), ((), ())), preferred_element_type=jnp.float32
    )


def render_kernel(
    rows_ref,
    group_ref,
    middle_ref,
    target_ref,
    table_in,
    picture_ref,
    grad_out,
    planes,
    entries,
    fields,
    picture_sum,
    residual,
    in_sem,
    out_sem,
    *tables,
    devices,
    per_owner,
    groups,
    depth,
):
    planes_in = FIELDS * per_owner
    planes_out = planes_in + ROWSUB
    halves = per_owner // ROWSUB
    total = groups * ROWSUB * depth
    table = tables[0]
    blocks = depth * ROWSUB // LANES
    per_block = LANES // ROWSUB
    pixels = SIDE * SIDE
    wide = pixels // LANES

    load = pltpu.make_async_copy(table_in, planes.at[pl.ds(0, devices * planes_in)], in_sem)
    load.start()
    load.wait()

    pad = jnp.zeros((LANES - FIELDS * ROWSUB, LANES), jnp.float32)

    def build(owner, carry):
        start = pl.multiple_of(owner * planes_in, 8)
        for half in range(halves):
            parts = [
                planes[pl.ds(start + f * per_owner + half * ROWSUB, ROWSUB), :]
                for f in range(FIELDS)
            ]
            block = jnp.concatenate(parts + [pad], 0)
            at = pl.multiple_of((owner * halves + half) * LANES, LANES)
            table[pl.ds(at, LANES), :] = block.T
        return carry

    lax.fori_loop(0, devices, build, 0)

    unroll = 32

    def gather(index, carry):
        base = pl.multiple_of(index * unroll, unroll)
        for q in range(unroll):
            row = rows_ref[base + q]
            entries[pl.ds(base + q, 1), :] = table[pl.ds(row, 1), :]
        return carry

    lax.fori_loop(0, total // unroll, gather, 0)

    sub = lax.broadcasted_iota(jnp.int32, (ROWSUB, LANES), 0)
    lane = lax.broadcasted_iota(jnp.int32, (ROWSUB, LANES), 1)
    own_tile = sub == lane % ROWSUB
    basis = pixel_basis(32)
    basis_three = jnp.where(
        lax.broadcasted_iota(jnp.int32, (32, pixels), 0) < 24, basis, 0.0
    ).astype(jnp.bfloat16)
    basis_rows = jnp.where(
        lax.broadcasted_iota(jnp.int32, (16, pixels), 0) < 8, pixel_basis(16), 0.0
    ).astype(jnp.bfloat16)

    def field_mask(block):
        return sub == group_ref[pl.ds(block, 1), :]

    def colour_rows(block):
        parts = []
        for ch in range(3):
            row = fields[pl.ds(block * 16 + 6 + ch, 1), :]
            parts.append(jnp.where(own_tile, row, 0.0))
        full = jnp.concatenate(parts, 0)
        high = full.astype(jnp.bfloat16).astype(jnp.float32)
        return high, full - high

    for group in range(groups):
        picture_sum[group] = jnp.zeros((48, pixels), jnp.float32)

    w_base = [h * total for h in range(wide)]
    a_base = [(wide + h) * total for h in range(wide)]

    def forward(step, carry):
        out = []
        for group in range(groups):
            block = group * blocks + step
            at = pl.multiple_of(block * LANES, LANES)
            mask = field_mask(block)
            turned = entries[pl.ds(at, LANES), :].T
            rows = []
            for f in range(FIELDS):
                part = jnp.where(mask, turned[f * ROWSUB : (f + 1) * ROWSUB, :], 0.0)
                rows.append(jnp.sum(part, axis=0, keepdims=True))
            u = rows[0] - middle_ref[2 * group : 2 * group + 1, :]
            v = rows[1] - middle_ref[2 * group + 1 : 2 * group + 2, :]
            rows[0], rows[1] = u, v
            a, b, c = rows[2], rows[3], rows[4]
            for f in range(FIELDS):
                fields[pl.ds(block * 16 + f, 1), :] = rows[f]
            au = a * u + b * v
            bv = b * u + c * v
            coefs = (
                LOG2E * (rows[5] - 0.5 * (u * au + v * bv)),
                LOG2E * au,
                LOG2E * bv,
                (-0.5 * LOG2E) * a,
                -LOG2E * b,
                (-0.5 * LOG2E) * c,
            )
            coef = jnp.zeros((ROWSUB, LANES), jnp.float32)
            for i, row in enumerate(coefs):
                coef = jnp.where(sub == i, row, coef)
            high = coef.astype(jnp.bfloat16).astype(jnp.float32)
            rest = coef - high
            mid = rest.astype(jnp.bfloat16).astype(jnp.float32)
            low = rest - mid
            stacked = jnp.concatenate([high, mid, low, jnp.zeros_like(low)], 0)
            exponent = dot_nn(stacked.T.astype(jnp.bfloat16), basis_three)
            trans = list(carry[group])
            weights = [[] for _ in range(wide)]
            for s in range(per_block):
                for h in range(wide):
                    e = exponent[s * ROWSUB : (s + 1) * ROWSUB, h * LANES : (h + 1) * LANES]
                    alpha = jnp.exp2(jnp.minimum(e, LOG2E * LOG_CAP))
                    w = trans[h] * alpha
                    trans[h] = trans[h] - w
                    planes[pl.ds(a_base[h] + at + s * ROWSUB, ROWSUB), :] = alpha
                    planes[pl.ds(w_base[h] + at + s * ROWSUB, ROWSUB), :] = w
                    weights[h].append(w)
            weight = jnp.concatenate([jnp.concatenate(ws, 0) for ws in weights], 1)
            w_high, w_rest = split_two(weight)
            c_high, c_rest = colour_rows(block)
            both = jnp.concatenate([c_high, c_rest], 0).astype(jnp.bfloat16)
            picture_sum[group] += dot_nn(both, w_high) + dot_nn(both, w_rest)
            out.append(tuple(trans))
        return tuple(out)

    ones = jnp.ones((ROWSUB, LANES), jnp.float32)
    start = tuple(tuple(ones for _ in range(wide)) for _ in range(groups))
    lax.fori_loop(0, blocks, forward, start)

    loss = jnp.zeros((1, 1), jnp.float32)
    for group in range(groups):
        both = picture_sum[group]
        picture = both[:24] + both[24:]
        parts = []
        for ch in range(3):
            pair = []
            for h in range(wide):
                where = pl.ds((group * ROWSUB * 3 + ch) * wide + h, ROWSUB, stride=3 * wide)
                part = picture[ch * ROWSUB : (ch + 1) * ROWSUB, h * LANES : (h + 1) * LANES]
                picture_ref[where, :] = part
                pair.append(part - target_ref[where, :])
            parts.append(jnp.concatenate(pair, 1))
        left = jnp.concatenate(parts, 0)
        square = left * left
        loss = loss + 0.5 * jnp.sum(
            jnp.sum(square, axis=0, keepdims=True), axis=1, keepdims=True
        )
        high = left.astype(jnp.bfloat16).astype(jnp.float32)
        residual[group] = jnp.concatenate([high, left - high] * 2, 0).astype(jnp.bfloat16)

    def backward(index, carry):
        step = blocks - 1 - index
        out = []
        for group in range(groups):
            block = group * blocks + step
            at = pl.multiple_of(block * LANES, LANES)
            mask = field_mask(block)
            c_high, c_rest = colour_rows(block)
            four = jnp.concatenate([c_high, c_high, c_rest, c_rest], 0)
            q = dot_nn(four.T.astype(jnp.bfloat16), residual[group])
            behind = list(carry[group])
            slopes = [[None] * per_block for _ in range(wide)]
            weights = [[None] * per_block for _ in range(wide)]
            for s in reversed(range(per_block)):
                for h in range(wide):
                    w = planes[pl.ds(w_base[h] + at + s * ROWSUB, ROWSUB), :]
                    alpha = planes[pl.ds(a_base[h] + at + s * ROWSUB, ROWSUB), :]
                    d = q[s * ROWSUB : (s + 1) * ROWSUB, h * LANES : (h + 1) * LANES] - behind[h]
                    slopes[h][s] = w * d
                    weights[h][s] = w
                    behind[h] = behind[h] + alpha * d
            slope = jnp.concatenate([jnp.concatenate(ws, 0) for ws in slopes], 1)
            weight = jnp.concatenate([jnp.concatenate(ws, 0) for ws in weights], 1)
            g_high, g_rest = split_two(slope)
            w_high, w_rest = split_two(weight)
            moments = dot_nt(basis_rows, g_high) + dot_nt(basis_rows, g_rest)
            res = residual[group, 0:48, :]
            tone = dot_nt(res, w_high) + dot_nt(res, w_rest)
            tone = tone[:24] + tone[24:]
            m = [moments[i : i + 1, :] for i in range(6)]
            u, v, a, b, c = [fields[pl.ds(block * 16 + f, 1), :] for f in range(5)]
            m_x = m[1] - u * m[0]
            m_y = m[2] - v * m[0]
            rows = [
                a * m_x + b * m_y,
                b * m_x + c * m_y,
                -0.5 * (m[3] - u * (m[1] + m_x)),
                -(m[4] - u * m[2] - v * m_x),
                -0.5 * (m[5] - v * (m[2] + m_y)),
                m[0],
            ]
            for ch in range(3):
                part = jnp.where(own_tile, tone[ch * ROWSUB : (ch + 1) * ROWSUB, :], 0.0)
                rows.append(jnp.sum(part, axis=0, keepdims=True))
            placed = [jnp.where(mask, row, 0.0) for row in rows]
            entries[pl.ds(at, LANES), :] = jnp.concatenate(placed + [pad], 0).T
            out.append(tuple(behind))
        return tuple(out)

    zeros = jnp.zeros((ROWSUB, LANES), jnp.float32)
    start = tuple(tuple(zeros for _ in range(wide)) for _ in range(groups))
    lax.fori_loop(0, blocks, backward, start)

    tall = jnp.zeros((LANES, LANES), jnp.float32)

    def clear(index, carry):
        at = pl.multiple_of(index * LANES, LANES)
        for one in tables:
            one[pl.ds(at, LANES), :] = tall
        return carry

    lax.fori_loop(0, devices * halves, clear, 0)

    def scatter(index, carry):
        base = pl.multiple_of(index * unroll, unroll)
        for q in range(unroll):
            one = tables[q % len(tables)]
            row = rows_ref[base + q]
            one[pl.ds(row, 1), :] = one[pl.ds(row, 1), :] + entries[pl.ds(base + q, 1), :]
        return carry

    lax.fori_loop(0, total // unroll, scatter, 0)

    loss_rows = jnp.broadcast_to(loss, (ROWSUB, LANES))

    def collect(owner, carry):
        start = pl.multiple_of(owner * planes_out, 8)
        for half in range(halves):
            at = pl.multiple_of((owner * halves + half) * LANES, LANES)
            block = tables[0][pl.ds(at, LANES), :]
            for one in tables[1:]:
                block = block + one[pl.ds(at, LANES), :]
            turned = block.T
            for f in range(FIELDS):
                planes[pl.ds(start + f * per_owner + half * ROWSUB, ROWSUB), :] = turned[
                    f * ROWSUB : (f + 1) * ROWSUB, :
                ]
        planes[pl.ds(start + planes_in, ROWSUB), :] = loss_rows
        return carry

    lax.fori_loop(0, devices, collect, 0)

    store = pltpu.make_async_copy(planes.at[pl.ds(0, devices * planes_out)], grad_out, out_sem)
    store.start()
    store.wait()


def exchange_order(gx_size, gy_size):
    gx_bits = gx_size.bit_length() - 1
    gy_bits = gy_size.bit_length() - 1
    order = [("gx", gx_size, 1 << b, gy_bits + b) for b in range(gx_bits)]
    order += [("gy", gy_size, 1 << b, b) for b in reversed(range(gy_bits))]
    return order


def swap(values, phase):
    axis, size, flip, _ = phase
    return lax.ppermute(values, axis, [(i, i ^ flip) for i in range(size)])


def spread(values, order):
    for phase in order:
        values = jnp.concatenate([values, swap(values, phase)], 0)
    return values


def fold(values, order):
    for phase in reversed(order):
        half = values.shape[0] // 2
        values = values[:half] + swap(values[half:], phase)
    return values


def per_device(gauss_params, first_moment, second_moment, splat_lists, tile_ids, targets, camera):
    gx_size = lax.axis_size("gx")
    gy_size = lax.axis_size("gy")
    devices = gx_size * gy_size
    order = exchange_order(gx_size, gy_size)
    params_rows, count = gauss_params.shape
    tiles, depth = splat_lists.shape[1:]
    per_owner = count // LANES
    groups = tiles // ROWSUB
    planes_in = FIELDS * per_owner
    planes_out = planes_in + ROWSUB
    total = tiles * depth
    pixels = SIDE * SIDE

    me = lax.axis_index("gx") * gy_size + lax.axis_index("gy")
    apart = (splat_lists // count) ^ me
    local = splat_lists % count
    place = jnp.zeros_like(apart)
    for bit, phase in enumerate(order):
        place = place + (((apart >> phase[3]) & 1) << bit)
    rows = place * (count // ROWSUB) + (local // (ROWSUB * LANES)) * LANES + local % LANES
    which = (local // LANES) % ROWSUB

    def interleave(values):
        return (
            values.reshape(STEPS, groups, ROWSUB, depth)
            .transpose(0, 1, 3, 2)
            .reshape(STEPS, total)
        )

    rows = interleave(rows)
    which = interleave(which).reshape(STEPS, total // LANES, LANES)
    middle_x = (tile_ids % IMG_TX * SIDE + SIDE // 2).astype(jnp.float32)
    middle_y = (tile_ids // IMG_TX * SIDE + SIDE // 2).astype(jnp.float32)
    middle = jnp.stack([middle_x, middle_y], 1).reshape(STEPS, 2, groups, ROWSUB)
    middle = middle.transpose(0, 2, 1, 3).reshape(STEPS, 2 * groups, ROWSUB)
    middle = jnp.tile(middle, (1, 1, LANES // ROWSUB))
    target_rows = targets.reshape(STEPS, tiles * 3 * pixels // LANES, LANES)

    vmem = pl.BlockSpec(memory_space=pltpu.VMEM)
    smem = pl.BlockSpec(memory_space=pltpu.SMEM)
    hbm = pl.BlockSpec(memory_space=pl.ANY)
    f32 = jnp.float32
    state = jax.ShapeDtypeStruct((params_rows, count), f32)
    field_shape = jax.ShapeDtypeStruct((planes_in, LANES), f32)

    table_bytes = devices * count // ROWSUB * LANES * 4
    copies = max(1, min(4, (24 << 20) // table_bytes))
    render = pl.pallas_call(
        functools.partial(
            render_kernel, devices=devices, per_owner=per_owner, groups=groups, depth=depth
        ),
        out_shape=(
            jax.ShapeDtypeStruct((tiles * 3 * pixels // LANES, LANES), f32),
            jax.ShapeDtypeStruct((devices * planes_out, LANES), f32),
        ),
        in_specs=[smem, vmem, vmem, vmem, hbm],
        out_specs=(vmem, hbm),
        scratch_shapes=[
            pltpu.VMEM((max(2 * pixels // LANES * total, devices * planes_out), LANES), f32),
            pltpu.VMEM((total, LANES), f32),
            pltpu.VMEM((total // LANES * 16, LANES), f32),
            pltpu.VMEM((groups, 48, pixels), f32),
            pltpu.VMEM((groups, 96, pixels), jnp.bfloat16),
            pltpu.SemaphoreType.DMA(()),
            pltpu.SemaphoreType.DMA(()),
        ]
        + [pltpu.VMEM((devices * count // ROWSUB, LANES), f32)] * copies,
        compiler_params=pltpu.CompilerParams(vmem_limit_bytes=60 << 20),
        name="render",
    )

    params, first, second = gauss_params, first_moment, second_moment
    fields = pl.pallas_call(
        functools.partial(project_kernel, step=0),
        out_shape=field_shape,
        in_specs=[smem, vmem],
        out_specs=vmem,
        name="project",
    )(camera, params)
    pictures = []
    losses = []
    for step in range(STEPS):
        table = spread(fields, order)
        picture, grads = render(
            rows[step], which[step], middle[step], target_rows[step], table
        )
        pictures.append(picture)
        summed = fold(grads, order)
        losses.append(summed[planes_in, 0])
        more = step + 1 < STEPS
        result = pl.pallas_call(
            functools.partial(update_kernel, step=step, project_next=more),
            out_shape=(state, state, state) + ((field_shape,) if more else ()),
            in_specs=[smem, vmem, vmem, vmem, vmem],
            out_specs=(vmem,) * (4 if more else 3),
            scratch_shapes=[pltpu.VMEM((params_rows, count), f32)],
            name="update",
        )(camera, params, first, second, summed)
        params, first, second = result[:3]
        if more:
            fields = result[3]
    rendered = jnp.stack(pictures).reshape(STEPS, tiles, 3, pixels)
    loss = jnp.stack(losses) / (3.0 * pixels * tiles * devices)
    return params, first, second, rendered, loss


def solution(mesh):
    along = P(None, AXES)
    lists = P(None, AXES, None)
    frames = P(None, AXES, None, None)
    return jax.shard_map(
        per_device,
        mesh=mesh,
        in_specs=(along, along, along, lists, along, frames, P()),
        out_specs=(along, along, along, frames, P()),
        check_vma=False,
    )
```

```python
import functools

import jax
import jax.numpy as jnp
from jax import lax
from jax.experimental import pallas as pl
from jax.experimental.pallas import tpu as pltpu
from jax.sharding import PartitionSpec as P

SIDE = 16
NCOEF = 16
STEPS = 2
IMG_TX = 64
IMG_TY = 32

FIELDS = 9
LANES = 128
ROWSUB = 8
AXES = ("gx", "gy")

beta_one = 0.9
beta_two = 0.999
adam_eps = 1e-08
learn_rate = 0.01
adam_start = 1000
band_zero = 0.28209479177387814
band_one = 0.4886025119029199
band_two = (
    1.0925484305920792,
    -1.0925484305920792,
    0.31539156525252005,
    -1.0925484305920792,
    0.5462742152960396,
)
band_three = (
    -0.5900435899266435,
    2.890611442640554,
    -0.4570457994644658,
    0.3731763325901154,
    -0.4570457994644658,
    1.445305721320277,
    -0.5900435899266435,
)
LOG2E = 1.4426950408889634
LOG_CAP = -0.01005033585350145


def harmonic_rows(ray_x, ray_y, ray_z):
    sq_x = ray_x * ray_x
    sq_y = ray_y * ray_y
    sq_z = ray_z * ray_z
    return [
        band_zero * jnp.ones_like(ray_x),
        -band_one * ray_y,
        band_one * ray_z,
        -band_one * ray_x,
        band_two[0] * ray_x * ray_y,
        band_two[1] * ray_y * ray_z,
        band_two[2] * (2.0 * sq_z - sq_x - sq_y),
        band_two[3] * ray_x * ray_z,
        band_two[4] * (sq_x - sq_y),
        band_three[0] * ray_y * (3.0 * sq_x - sq_y),
        band_three[1] * ray_x * ray_y * ray_z,
        band_three[2] * ray_y * (4.0 * sq_z - sq_x - sq_y),
        band_three[3] * ray_z * (2.0 * sq_z - 3.0 * sq_x - 3.0 * sq_y),
        band_three[4] * ray_x * (4.0 * sq_z - sq_x - sq_y),
        band_three[5] * ray_z * (sq_x - sq_y),
        band_three[6] * ray_x * (sq_x - 3.0 * sq_y),
    ]


def geometry_rows(p0, p1, p2, p3, p4, p5, p6, cam_x, cam_y):
    screen_u = (p0 - cam_x) / p2
    screen_v = (p1 - cam_y) / p2
    inv_one = p2 * p2 * jnp.exp(-2.0 * p3)
    inv_two = p2 * p2 * jnp.exp(-2.0 * p4)
    cosine = jnp.cos(p5)
    sine = jnp.sin(p5)
    conic_a = cosine * cosine * inv_one + sine * sine * inv_two
    conic_b = cosine * sine * (inv_one - inv_two)
    conic_c = sine * sine * inv_one + cosine * cosine * inv_two
    tail = jnp.log(1.0 + jnp.exp(-jnp.abs(p6)))
    log_opacity = LOG_CAP - (jnp.maximum(-p6, 0.0) + tail)
    return screen_u, screen_v, conic_a, conic_b, conic_c, log_opacity


def ray_rows(screen_u, screen_v):
    image_width = 1.0 * SIDE * IMG_TX
    image_height = 1.0 * SIDE * IMG_TY
    ray_x = (screen_u - 0.5 * image_width) / image_width
    ray_y = (screen_v - 0.5 * image_height) / image_width
    factor = lax.rsqrt(ray_x * ray_x + ray_y * ray_y + 1.0)
    return ray_x, ray_y, factor


def project_to(param_ref, cam_x, cam_y, out_ref):
    rows = [param_ref[i : i + 1, :] for i in range(7)]
    geo = geometry_rows(*rows, cam_x, cam_y)
    ray_x, ray_y, factor = ray_rows(geo[0], geo[1])
    basis = jnp.concatenate(harmonic_rows(ray_x * factor, ray_y * factor, factor), 0)
    colours = []
    for ch in range(3):
        coef = param_ref[7 + NCOEF * ch : 7 + NCOEF * (ch + 1), :]
        colours.append(0.5 + jnp.sum(coef * basis, axis=0, keepdims=True))
    fields = jnp.concatenate(list(geo) + colours, 0)
    per_field = fields.shape[1] // LANES
    for k in range(per_field):
        out_ref[pl.ds(k, FIELDS, stride=per_field), :] = fields[:, k * LANES : (k + 1) * LANES]


def project_kernel(cam_ref, param_ref, out_ref, *, step):
    project_to(param_ref, cam_ref[step, 0], cam_ref[step, 1], out_ref)


def gradient_to(param_ref, cam_x, cam_y, grad_ref, full_ref):
    count = param_ref.shape[1]
    per_field = count // LANES
    pieces = [grad_ref[pl.ds(k, FIELDS, stride=per_field), :] for k in range(per_field)]
    grads = jnp.concatenate(pieces, 1)
    g = [grads[i : i + 1, :] for i in range(FIELDS)]
    p0, p1, p2, p3, p4, p5, p6 = [param_ref[i : i + 1, :] for i in range(7)]
    inv_z = 1.0 / p2
    screen_u = (p0 - cam_x) / p2
    screen_v = (p1 - cam_y) / p2
    inv_one = p2 * p2 * jnp.exp(-2.0 * p3)
    inv_two = p2 * p2 * jnp.exp(-2.0 * p4)
    cosine = jnp.cos(p5)
    sine = jnp.sin(p5)
    cc = cosine * cosine
    ss = sine * sine
    cs = cosine * sine
    ray_x, ray_y, factor = ray_rows(screen_u, screen_v)
    nx, ny, nz = ray_x * factor, ray_y * factor, factor
    basis_rows, basis_vjp = jax.vjp(lambda a, b, c: tuple(harmonic_rows(a, b, c)), nx, ny, nz)
    basis = jnp.concatenate(basis_rows, 0)
    d_basis = jnp.zeros_like(basis)
    for ch in range(3):
        coef = param_ref[7 + NCOEF * ch : 7 + NCOEF * (ch + 1), :]
        full_ref[7 + NCOEF * ch : 7 + NCOEF * (ch + 1), :] = g[6 + ch] * basis
        d_basis = d_basis + g[6 + ch] * coef
    d_nx, d_ny, d_nz = basis_vjp(tuple(d_basis[i : i + 1, :] for i in range(NCOEF)))
    dot = d_nx * nx + d_ny * ny + d_nz * nz
    image_width = 1.0 * SIDE * IMG_TX
    d_u = g[0] + factor * (d_nx - nx * dot) / image_width
    d_v = g[1] + factor * (d_ny - ny * dot) / image_width
    d_one = g[2] * cc + g[3] * cs + g[4] * ss
    d_two = g[2] * ss - g[3] * cs + g[4] * cc
    diff = inv_one - inv_two
    d_angle = diff * (2.0 * cs * (g[4] - g[2]) + (cc - ss) * g[3])
    d_x = d_u * inv_z
    d_y = d_v * inv_z
    d_z = 2.0 * (d_one * inv_one + d_two * inv_two) * inv_z - d_x * screen_u - d_y * screen_v
    full_ref[0:1, :] = d_x
    full_ref[1:2, :] = d_y
    full_ref[2:3, :] = d_z
    full_ref[3:4, :] = -2.0 * inv_one * d_one
    full_ref[4:5, :] = -2.0 * inv_two * d_two
    full_ref[5:6, :] = d_angle
    full_ref[6:7, :] = g[5] / (1.0 + jnp.exp(p6))


def update_kernel(
    cam_ref, param_ref, first_ref, second_ref, grad_ref, *refs, step, project_next
):
    if project_next:
        new_param, new_first, new_second, field_ref, full_ref = refs
    else:
        new_param, new_first, new_second, full_ref = refs
    gradient_to(param_ref, cam_ref[step, 0], cam_ref[step, 1], grad_ref, full_ref)
    step_count = adam_start + step + 1
    gradient = full_ref[...]
    first = beta_one * first_ref[...] + (1.0 - beta_one) * gradient
    second = beta_two * second_ref[...] + (1.0 - beta_two) * gradient * gradient
    scaled_first = first / (1.0 - beta_one**step_count)
    scaled_second = second / (1.0 - beta_two**step_count)
    new_first[...] = first
    new_second[...] = second
    new_param[...] = param_ref[...] - learn_rate * scaled_first / (
        jnp.sqrt(scaled_second) + adam_eps
    )
    if project_next:
        project_to(new_param, cam_ref[step + 1, 0], cam_ref[step + 1, 1], field_ref)


def split_two(values):
    high = values.astype(jnp.bfloat16)
    rest = (values - high.astype(jnp.float32)).astype(jnp.bfloat16)
    return high, rest


def pixel_basis(rows):
    pix = lax.broadcasted_iota(jnp.int32, (rows, SIDE * SIDE), 1)
    which = lax.broadcasted_iota(jnp.int32, (rows, SIDE * SIDE), 0)
    x = (pix % SIDE).astype(jnp.float32) + (0.5 - 0.5 * SIDE)
    y = (pix // SIDE).astype(jnp.float32) + (0.5 - 0.5 * SIDE)
    which = which % 8
    out = jnp.where(which == 0, 1.0, 0.0)
    for index, value in enumerate((x, y, x * x, x * y, y * y)):
        out = jnp.where(which == index + 1, value, out)
    return out


def dot_nn(a, b):
    return jnp.dot(a, b, preferred_element_type=jnp.float32)


def dot_tn(a, b):
    return lax.dot_general(
        a, b, (((0,), (0,)), ((), ())), preferred_element_type=jnp.float32
    )


def dot_nt(a, b):
    return lax.dot_general(
        a, b, (((1,), (1,)), ((), ())), preferred_element_type=jnp.float32
    )


def render_kernel(
    rows_ref,
    group_ref,
    middle_ref,
    target_ref,
    table_own,
    table_other,
    picture_ref,
    grad_own,
    grad_other,
    planes,
    entries,
    fields,
    factors,
    picture_sum,
    residual,
    in_sem,
    out_sem,
    *tables,
    devices,
    per_owner,
    groups,
    depth,
):
    planes_in = FIELDS * per_owner
    planes_out = planes_in + ROWSUB
    halves = per_owner // ROWSUB
    total = groups * ROWSUB * depth
    table = tables[0]
    blocks = depth * ROWSUB // LANES
    per_block = LANES // ROWSUB
    pixels = SIDE * SIDE
    wide = pixels // LANES
    near = devices // 2

    loads = [
        pltpu.make_async_copy(
            ref, planes.at[pl.ds(i * near * planes_in, near * planes_in)], in_sem.at[i]
        )
        for i, ref in enumerate((table_own, table_other))
    ]
    for load in loads:
        load.start()
    for load in loads:
        load.wait()

    pad = jnp.zeros((LANES - FIELDS * ROWSUB, LANES), jnp.float32)

    def build(owner, carry):
        start = pl.multiple_of(owner * planes_in, 8)
        for half in range(halves):
            parts = [
                planes[pl.ds(start + f * per_owner + half * ROWSUB, ROWSUB), :]
                for f in range(FIELDS)
            ]
            block = jnp.concatenate(parts + [pad], 0)
            at = pl.multiple_of((owner * halves + half) * LANES, LANES)
            table[pl.ds(at, LANES), :] = block.T
        return carry

    lax.fori_loop(0, devices, build, 0, unroll=2)

    unroll = 32

    def gather(index, carry):
        base = pl.multiple_of(index * unroll, unroll)
        for q in range(unroll):
            row = rows_ref[base + q]
            entries[pl.ds(base + q, 1), :] = table[pl.ds(row, 1), :]
        return carry

    lax.fori_loop(0, total // unroll, gather, 0)

    sub = lax.broadcasted_iota(jnp.int32, (ROWSUB, LANES), 0)
    lane = lax.broadcasted_iota(jnp.int32, (ROWSUB, LANES), 1)
    own_tile = sub == lane % ROWSUB
    basis_three = jnp.where(
        lax.broadcasted_iota(jnp.int32, (LANES, pixels), 0) < 24, pixel_basis(LANES), 0.0
    ).astype(jnp.bfloat16)
    basis_rows = jnp.where(
        lax.broadcasted_iota(jnp.int32, (16, pixels), 0) < 8, pixel_basis(16), 0.0
    ).astype(jnp.bfloat16)
    w_base = [h * total for h in range(wide)]
    a_base = [(wide + h) * total for h in range(wide)]

    def field_mask(block):
        return sub == group_ref[pl.ds(block, 1), :]

    def prepare(block, carry):
        at = pl.multiple_of(block * LANES, LANES)
        group = block // blocks
        mask = field_mask(block)
        turned = entries[pl.ds(at, LANES), :].T
        rows = []
        for f in range(FIELDS):
            part = jnp.where(mask, turned[f * ROWSUB : (f + 1) * ROWSUB, :], 0.0)
            rows.append(jnp.sum(part, axis=0, keepdims=True))
        u = rows[0] - middle_ref[pl.ds(2 * group, 1), :]
        v = rows[1] - middle_ref[pl.ds(2 * group + 1, 1), :]
        rows[0], rows[1] = u, v
        a, b, c = rows[2], rows[3], rows[4]
        for f in range(5):
            fields[pl.ds(block * ROWSUB + f, 1), :] = rows[f]
        au = a * u + b * v
        bv = b * u + c * v
        coefs = (
            LOG2E * (rows[5] - 0.5 * (u * au + v * bv)),
            LOG2E * au,
            LOG2E * bv,
            (-0.5 * LOG2E) * a,
            -LOG2E * b,
            (-0.5 * LOG2E) * c,
        )
        coef = jnp.zeros((ROWSUB, LANES), jnp.float32)
        for i, row in enumerate(coefs):
            coef = jnp.where(sub == i, row, coef)
        high = coef.astype(jnp.bfloat16).astype(jnp.float32)
        rest = coef - high
        mid = rest.astype(jnp.bfloat16).astype(jnp.float32)
        low = rest - mid
        full = [jnp.where(own_tile, rows[6 + ch], 0.0) for ch in range(3)]
        c_high = [part.astype(jnp.bfloat16).astype(jnp.float32) for part in full]
        c_rest = [part - top for part, top in zip(full, c_high)]
        stacked = jnp.concatenate(
            [high, mid, low, jnp.zeros_like(low)] + c_high + c_high + c_rest + c_rest, 0
        )
        factors[pl.ds(at, LANES), :] = stacked.T.astype(jnp.bfloat16)
        return carry

    lax.fori_loop(0, groups * blocks, prepare, 0, unroll=2)

    def forward(step, carry):
        out = []
        for group in range(groups):
            at = pl.multiple_of((group * blocks + step) * LANES, LANES)
            exponent = dot_nn(factors[pl.ds(at, LANES), :], basis_three)
            trans = list(carry[group])
            for s in range(per_block):
                for h in range(wide):
                    e = exponent[s * ROWSUB : (s + 1) * ROWSUB, h * LANES : (h + 1) * LANES]
                    alpha = jnp.exp2(jnp.minimum(e, LOG2E * LOG_CAP))
                    w = trans[h] * alpha
                    trans[h] = trans[h] - w
                    planes[pl.ds(a_base[h] + at + s * ROWSUB, ROWSUB), :] = alpha
                    planes[pl.ds(w_base[h] + at + s * ROWSUB, ROWSUB), :] = w
            out.append(tuple(trans))
        return tuple(out)

    ones = jnp.ones((ROWSUB, LANES), jnp.float32)
    start = tuple(tuple(ones for _ in range(wide)) for _ in range(groups))
    lax.fori_loop(0, blocks, forward, start)

    def wide_block(bases, at):
        return jnp.concatenate([planes[pl.ds(base + at, LANES), :] for base in bases], 1)

    for group in range(groups):
        picture_sum[group] = jnp.zeros((LANES, pixels), jnp.float32)

    def paint(step, carry):
        for group in range(groups):
            at = pl.multiple_of((group * blocks + step) * LANES, LANES)
            w_high, w_rest = split_two(wide_block(w_base, at))
            left = factors[pl.ds(at, LANES), :]
            picture_sum[group] += dot_tn(left, w_high) + dot_tn(left, w_rest)
        return carry

    lax.fori_loop(0, blocks, paint, 0)

    loss = jnp.zeros((1, 1), jnp.float32)
    for group in range(groups):
        picture = picture_sum[group, 32:56, :] + picture_sum[group, 80:104, :]
        parts = []
        for ch in range(3):
            pair = []
            for h in range(wide):
                where = pl.ds((group * ROWSUB * 3 + ch) * wide + h, ROWSUB, stride=3 * wide)
                part = picture[ch * ROWSUB : (ch + 1) * ROWSUB, h * LANES : (h + 1) * LANES]
                picture_ref[where, :] = part
                pair.append(part - target_ref[where, :])
            parts.append(jnp.concatenate(pair, 1))
        left = jnp.concatenate(parts, 0)
        square = left * left
        loss = loss + 0.5 * jnp.sum(
            jnp.sum(square, axis=0, keepdims=True), axis=1, keepdims=True
        )
        high = left.astype(jnp.bfloat16).astype(jnp.float32)
        rest = left - high
        none = jnp.zeros((32, pixels), jnp.float32)
        residual[group] = jnp.concatenate([none, high, rest, high, rest], 0).astype(jnp.bfloat16)

    def backward(index, carry):
        step = blocks - 1 - index
        out = []
        for group in range(groups):
            at = pl.multiple_of((group * blocks + step) * LANES, LANES)
            q = dot_nn(factors[pl.ds(at, LANES), :], residual[group])
            behind = list(carry[group])
            for s in reversed(range(per_block)):
                for h in range(wide):
                    w = planes[pl.ds(w_base[h] + at + s * ROWSUB, ROWSUB), :]
                    alpha = planes[pl.ds(a_base[h] + at + s * ROWSUB, ROWSUB), :]
                    d = q[s * ROWSUB : (s + 1) * ROWSUB, h * LANES : (h + 1) * LANES] - behind[h]
                    planes[pl.ds(a_base[h] + at + s * ROWSUB, ROWSUB), :] = w * d
                    behind[h] = behind[h] + alpha * d
            out.append(tuple(behind))
        return tuple(out)

    zeros = jnp.zeros((ROWSUB, LANES), jnp.float32)
    start = tuple(tuple(zeros for _ in range(wide)) for _ in range(groups))
    lax.fori_loop(0, blocks, backward, start)

    def slopes(step, carry):
        for group in range(groups):
            block = group * blocks + step
            at = pl.multiple_of(block * LANES, LANES)
            mask = field_mask(block)
            g_high, g_rest = split_two(wide_block(a_base, at))
            w_high, w_rest = split_two(wide_block(w_base, at))
            moments = dot_nt(basis_rows, g_high) + dot_nt(basis_rows, g_rest)
            res = residual[group, 32:80, :]
            tone = dot_nt(res, w_high) + dot_nt(res, w_rest)
            tone = tone[:24] + tone[24:]
            m = [moments[i : i + 1, :] for i in range(6)]
            u, v, a, b, c = [fields[pl.ds(block * ROWSUB + f, 1), :] for f in range(5)]
            m_x = m[1] - u * m[0]
            m_y = m[2] - v * m[0]
            rows = [
                a * m_x + b * m_y,
                b * m_x + c * m_y,
                -0.5 * (m[3] - u * (m[1] + m_x)),
                -(m[4] - u * m[2] - v * m_x),
                -0.5 * (m[5] - v * (m[2] + m_y)),
                m[0],
            ]
            for ch in range(3):
                part = jnp.where(own_tile, tone[ch * ROWSUB : (ch + 1) * ROWSUB, :], 0.0)
                rows.append(jnp.sum(part, axis=0, keepdims=True))
            placed = [jnp.where(mask, row, 0.0) for row in rows]
            entries[pl.ds(at, LANES), :] = jnp.concatenate(placed + [pad], 0).T
        return carry

    lax.fori_loop(0, blocks, slopes, 0)

    tall = jnp.zeros((LANES, LANES), jnp.float32)

    def clear(index, carry):
        at = pl.multiple_of(index * LANES, LANES)
        for one in tables:
            one[pl.ds(at, LANES), :] = tall
        return carry

    lax.fori_loop(0, devices * halves, clear, 0)

    def scatter(index, carry):
        base = pl.multiple_of(index * unroll, unroll)
        for q in range(unroll):
            one = tables[q % len(tables)]
            row = rows_ref[base + q]
            one[pl.ds(row, 1), :] = one[pl.ds(row, 1), :] + entries[pl.ds(base + q, 1), :]
        return carry

    lax.fori_loop(0, total // unroll, scatter, 0)

    loss_rows = jnp.broadcast_to(loss, (ROWSUB, LANES))

    def collect(owner, carry):
        start = pl.multiple_of(owner * planes_out, 8)
        for half in range(halves):
            at = pl.multiple_of((owner * halves + half) * LANES, LANES)
            block = tables[0][pl.ds(at, LANES), :]
            for one in tables[1:]:
                block = block + one[pl.ds(at, LANES), :]
            turned = block.T
            for f in range(FIELDS):
                planes[pl.ds(start + f * per_owner + half * ROWSUB, ROWSUB), :] = turned[
                    f * ROWSUB : (f + 1) * ROWSUB, :
                ]
        planes[pl.ds(start + planes_in, ROWSUB), :] = loss_rows
        return carry

    stores = [
        pltpu.make_async_copy(
            planes.at[pl.ds(i * near * planes_out, near * planes_out)], ref, out_sem.at[i]
        )
        for i, ref in enumerate((grad_own, grad_other))
    ]
    lax.fori_loop(near, devices, collect, 0, unroll=2)
    stores[1].start()
    lax.fori_loop(0, near, collect, 0, unroll=2)
    stores[0].start()
    for store in stores:
        store.wait()


def exchange_orders(gx_size, gy_size):
    gx_bits = [gy_size.bit_length() - 1 + b for b in range(gx_size.bit_length() - 1)]
    gy_bits = list(range(1, gy_size.bit_length() - 1))
    cut = (len(gy_bits) + 1) // 2
    low, high = gy_bits[:cut], gy_bits[cut:]
    return gx_bits[::-1] + low + high, gx_bits + high + low


def swap(values, devices, flips):
    pairs = [(i, i ^ flips[i & 1]) for i in range(devices)]
    return lax.ppermute(values, AXES, pairs)


def spread(values, devices, orders):
    for bits in zip(*orders):
        flips = [1 << bit for bit in bits]
        values = jnp.concatenate([values, swap(values, devices, flips)], 0)
    return values, swap(values, devices, (1, 1))


def fold(own, other, devices, orders):
    values = own + swap(other, devices, (1, 1))
    for bits in reversed(list(zip(*orders))):
        flips = [1 << bit for bit in bits]
        half = values.shape[0] // 2
        values = values[:half] + swap(values[half:], devices, flips)
    return values


def per_device(gauss_params, first_moment, second_moment, splat_lists, tile_ids, targets, camera):
    gx_size = lax.axis_size("gx")
    gy_size = lax.axis_size("gy")
    devices = gx_size * gy_size
    orders = exchange_orders(gx_size, gy_size)
    params_rows, count = gauss_params.shape
    tiles, depth = splat_lists.shape[1:]
    per_owner = count // LANES
    groups = tiles // ROWSUB
    planes_in = FIELDS * per_owner
    planes_out = planes_in + ROWSUB
    total = tiles * depth
    pixels = SIDE * SIDE

    me = lax.axis_index("gx") * gy_size + lax.axis_index("gy")
    owner = splat_lists // count
    apart = owner ^ me
    local = splat_lists % count
    place = (apart & 1) << len(orders[0])
    for bit, (even, odd) in enumerate(zip(*orders)):
        taken = jnp.where(owner & 1 == 0, apart >> even, apart >> odd)
        place = place + ((taken & 1) << bit)
    rows = place * (count // ROWSUB) + (local // (ROWSUB * LANES)) * LANES + local % LANES
    which = (local // LANES) % ROWSUB

    def interleave(values):
        return (
            values.reshape(STEPS, groups, ROWSUB, depth)
            .transpose(0, 1, 3, 2)
            .reshape(STEPS, total)
        )

    rows = interleave(rows)
    which = interleave(which).reshape(STEPS, total // LANES, LANES)
    middle_x = (tile_ids % IMG_TX * SIDE + SIDE // 2).astype(jnp.float32)
    middle_y = (tile_ids // IMG_TX * SIDE + SIDE // 2).astype(jnp.float32)
    middle = jnp.stack([middle_x, middle_y], 1).reshape(STEPS, 2, groups, ROWSUB)
    middle = middle.transpose(0, 2, 1, 3).reshape(STEPS, 2 * groups, ROWSUB)
    middle = jnp.tile(middle, (1, 1, LANES // ROWSUB))
    target_rows = targets.reshape(STEPS, tiles * 3 * pixels // LANES, LANES)

    vmem = pl.BlockSpec(memory_space=pltpu.VMEM)
    smem = pl.BlockSpec(memory_space=pltpu.SMEM)
    hbm = pl.BlockSpec(memory_space=pl.ANY)
    f32 = jnp.float32
    state = jax.ShapeDtypeStruct((params_rows, count), f32)
    field_shape = jax.ShapeDtypeStruct((planes_in, LANES), f32)

    table_bytes = devices * count // ROWSUB * LANES * 4
    copies = max(1, min(4, (24 << 20) // table_bytes))
    render = pl.pallas_call(
        functools.partial(
            render_kernel, devices=devices, per_owner=per_owner, groups=groups, depth=depth
        ),
        out_shape=(
            jax.ShapeDtypeStruct((tiles * 3 * pixels // LANES, LANES), f32),
            jax.ShapeDtypeStruct((devices // 2 * planes_out, LANES), f32),
            jax.ShapeDtypeStruct((devices // 2 * planes_out, LANES), f32),
        ),
        in_specs=[smem, vmem, vmem, vmem, hbm, hbm],
        out_specs=(vmem, hbm, hbm),
        scratch_shapes=[
            pltpu.VMEM((max(2 * pixels // LANES * total, devices * planes_out), LANES), f32),
            pltpu.VMEM((total, LANES), f32),
            pltpu.VMEM((total // LANES * ROWSUB, LANES), f32),
            pltpu.VMEM((total, LANES), jnp.bfloat16),
            pltpu.VMEM((groups, LANES, pixels), f32),
            pltpu.VMEM((groups, LANES, pixels), jnp.bfloat16),
            pltpu.SemaphoreType.DMA((2,)),
            pltpu.SemaphoreType.DMA((2,)),
        ]
        + [pltpu.VMEM((devices * count // ROWSUB, LANES), f32)] * copies,
        compiler_params=pltpu.CompilerParams(vmem_limit_bytes=60 << 20),
        name="render",
    )

    params, first, second = gauss_params, first_moment, second_moment
    fields = pl.pallas_call(
        functools.partial(project_kernel, step=0),
        out_shape=field_shape,
        in_specs=[smem, vmem],
        out_specs=vmem,
        name="project",
    )(camera, params)
    pictures = []
    losses = []
    for step in range(STEPS):
        near, far = spread(fields, devices, orders)
        picture, own, other = render(
            rows[step], which[step], middle[step], target_rows[step], near, far
        )
        pictures.append(picture)
        summed = fold(own, other, devices, orders)
        losses.append(summed[planes_in, 0])
        more = step + 1 < STEPS
        result = pl.pallas_call(
            functools.partial(update_kernel, step=step, project_next=more),
            out_shape=(state, state, state) + ((field_shape,) if more else ()),
            in_specs=[smem, vmem, vmem, vmem, vmem],
            out_specs=(vmem,) * (4 if more else 3),
            scratch_shapes=[pltpu.VMEM((params_rows, count), f32)],
            name="update",
        )(camera, params, first, second, summed)
        params, first, second = result[:3]
        if more:
            fields = result[3]
    rendered = jnp.stack(pictures).reshape(STEPS, tiles, 3, pixels)
    loss = jnp.stack(losses) / (3.0 * pixels * tiles * devices)
    return params, first, second, rendered, loss


def solution(mesh):
    along = P(None, AXES)
    lists = P(None, AXES, None)
    frames = P(None, AXES, None, None)
    return jax.shard_map(
        per_device,
        mesh=mesh,
        in_specs=(along, along, along, lists, along, frames, P()),
        out_specs=(along, along, along, frames, P()),
        check_vma=False,
    )
```

```python
import functools

import jax
import jax.numpy as jnp
from jax import lax
from jax.experimental import pallas as pl
from jax.experimental.pallas import tpu as pltpu
from jax.sharding import PartitionSpec as P

SIDE = 16
NCOEF = 16
STEPS = 2
IMG_TX = 64
IMG_TY = 32

FIELDS = 9
LANES = 128
ROWSUB = 8
AXES = ("gx", "gy")

beta_one = 0.9
beta_two = 0.999
adam_eps = 1e-08
learn_rate = 0.01
adam_start = 1000
band_zero = 0.28209479177387814
band_one = 0.4886025119029199
band_two = (
    1.0925484305920792,
    -1.0925484305920792,
    0.31539156525252005,
    -1.0925484305920792,
    0.5462742152960396,
)
band_three = (
    -0.5900435899266435,
    2.890611442640554,
    -0.4570457994644658,
    0.3731763325901154,
    -0.4570457994644658,
    1.445305721320277,
    -0.5900435899266435,
)
LOG2E = 1.4426950408889634
LOG_CAP = -0.01005033585350145


def harmonic_rows(ray_x, ray_y, ray_z):
    sq_x = ray_x * ray_x
    sq_y = ray_y * ray_y
    sq_z = ray_z * ray_z
    return [
        band_zero * jnp.ones_like(ray_x),
        -band_one * ray_y,
        band_one * ray_z,
        -band_one * ray_x,
        band_two[0] * ray_x * ray_y,
        band_two[1] * ray_y * ray_z,
        band_two[2] * (2.0 * sq_z - sq_x - sq_y),
        band_two[3] * ray_x * ray_z,
        band_two[4] * (sq_x - sq_y),
        band_three[0] * ray_y * (3.0 * sq_x - sq_y),
        band_three[1] * ray_x * ray_y * ray_z,
        band_three[2] * ray_y * (4.0 * sq_z - sq_x - sq_y),
        band_three[3] * ray_z * (2.0 * sq_z - 3.0 * sq_x - 3.0 * sq_y),
        band_three[4] * ray_x * (4.0 * sq_z - sq_x - sq_y),
        band_three[5] * ray_z * (sq_x - sq_y),
        band_three[6] * ray_x * (sq_x - 3.0 * sq_y),
    ]


def geometry_rows(p0, p1, p2, p3, p4, p5, p6, cam_x, cam_y):
    screen_u = (p0 - cam_x) / p2
    screen_v = (p1 - cam_y) / p2
    inv_one = p2 * p2 * jnp.exp(-2.0 * p3)
    inv_two = p2 * p2 * jnp.exp(-2.0 * p4)
    cosine = jnp.cos(p5)
    sine = jnp.sin(p5)
    conic_a = cosine * cosine * inv_one + sine * sine * inv_two
    conic_b = cosine * sine * (inv_one - inv_two)
    conic_c = sine * sine * inv_one + cosine * cosine * inv_two
    tail = jnp.log(1.0 + jnp.exp(-jnp.abs(p6)))
    log_opacity = LOG_CAP - (jnp.maximum(-p6, 0.0) + tail)
    return screen_u, screen_v, conic_a, conic_b, conic_c, log_opacity


def ray_rows(screen_u, screen_v):
    image_width = 1.0 * SIDE * IMG_TX
    image_height = 1.0 * SIDE * IMG_TY
    ray_x = (screen_u - 0.5 * image_width) / image_width
    ray_y = (screen_v - 0.5 * image_height) / image_width
    factor = lax.rsqrt(ray_x * ray_x + ray_y * ray_y + 1.0)
    return ray_x, ray_y, factor


def project_to(param_ref, cam_x, cam_y, out_ref):
    rows = [param_ref[i : i + 1, :] for i in range(7)]
    geo = geometry_rows(*rows, cam_x, cam_y)
    ray_x, ray_y, factor = ray_rows(geo[0], geo[1])
    basis = jnp.concatenate(harmonic_rows(ray_x * factor, ray_y * factor, factor), 0)
    colours = []
    for ch in range(3):
        coef = param_ref[7 + NCOEF * ch : 7 + NCOEF * (ch + 1), :]
        colours.append(0.5 + jnp.sum(coef * basis, axis=0, keepdims=True))
    fields = jnp.concatenate(list(geo) + colours, 0)
    per_field = fields.shape[1] // LANES
    for k in range(per_field):
        out_ref[pl.ds(k, FIELDS, stride=per_field), :] = fields[:, k * LANES : (k + 1) * LANES]


def project_kernel(cam_ref, param_ref, out_ref, *, step):
    project_to(param_ref, cam_ref[step, 0], cam_ref[step, 1], out_ref)


def gradient_to(param_ref, cam_x, cam_y, grad_ref, full_ref):
    count = param_ref.shape[1]
    per_field = count // LANES
    pieces = [grad_ref[pl.ds(k, FIELDS, stride=per_field), :] for k in range(per_field)]
    grads = jnp.concatenate(pieces, 1)
    g = [grads[i : i + 1, :] for i in range(FIELDS)]
    p0, p1, p2, p3, p4, p5, p6 = [param_ref[i : i + 1, :] for i in range(7)]
    inv_z = 1.0 / p2
    screen_u = (p0 - cam_x) / p2
    screen_v = (p1 - cam_y) / p2
    inv_one = p2 * p2 * jnp.exp(-2.0 * p3)
    inv_two = p2 * p2 * jnp.exp(-2.0 * p4)
    cosine = jnp.cos(p5)
    sine = jnp.sin(p5)
    cc = cosine * cosine
    ss = sine * sine
    cs = cosine * sine
    ray_x, ray_y, factor = ray_rows(screen_u, screen_v)
    nx, ny, nz = ray_x * factor, ray_y * factor, factor
    basis_rows, basis_vjp = jax.vjp(lambda a, b, c: tuple(harmonic_rows(a, b, c)), nx, ny, nz)
    basis = jnp.concatenate(basis_rows, 0)
    d_basis = jnp.zeros_like(basis)
    for ch in range(3):
        coef = param_ref[7 + NCOEF * ch : 7 + NCOEF * (ch + 1), :]
        full_ref[7 + NCOEF * ch : 7 + NCOEF * (ch + 1), :] = g[6 + ch] * basis
        d_basis = d_basis + g[6 + ch] * coef
    d_nx, d_ny, d_nz = basis_vjp(tuple(d_basis[i : i + 1, :] for i in range(NCOEF)))
    dot = d_nx * nx + d_ny * ny + d_nz * nz
    image_width = 1.0 * SIDE * IMG_TX
    d_u = g[0] + factor * (d_nx - nx * dot) / image_width
    d_v = g[1] + factor * (d_ny - ny * dot) / image_width
    d_one = g[2] * cc + g[3] * cs + g[4] * ss
    d_two = g[2] * ss - g[3] * cs + g[4] * cc
    diff = inv_one - inv_two
    d_angle = diff * (2.0 * cs * (g[4] - g[2]) + (cc - ss) * g[3])
    d_x = d_u * inv_z
    d_y = d_v * inv_z
    d_z = 2.0 * (d_one * inv_one + d_two * inv_two) * inv_z - d_x * screen_u - d_y * screen_v
    full_ref[0:1, :] = d_x
    full_ref[1:2, :] = d_y
    full_ref[2:3, :] = d_z
    full_ref[3:4, :] = -2.0 * inv_one * d_one
    full_ref[4:5, :] = -2.0 * inv_two * d_two
    full_ref[5:6, :] = d_angle
    full_ref[6:7, :] = g[5] / (1.0 + jnp.exp(p6))


def update_kernel(
    cam_ref, param_ref, first_ref, second_ref, grad_ref, *refs, step, project_next
):
    if project_next:
        new_param, new_first, new_second, field_ref, full_ref = refs
    else:
        new_param, new_first, new_second, full_ref = refs
    gradient_to(param_ref, cam_ref[step, 0], cam_ref[step, 1], grad_ref, full_ref)
    step_count = adam_start + step + 1
    gradient = full_ref[...]
    first = beta_one * first_ref[...] + (1.0 - beta_one) * gradient
    second = beta_two * second_ref[...] + (1.0 - beta_two) * gradient * gradient
    scaled_first = first / (1.0 - beta_one**step_count)
    scaled_second = second / (1.0 - beta_two**step_count)
    new_first[...] = first
    new_second[...] = second
    new_param[...] = param_ref[...] - learn_rate * scaled_first / (
        jnp.sqrt(scaled_second) + adam_eps
    )
    if project_next:
        project_to(new_param, cam_ref[step + 1, 0], cam_ref[step + 1, 1], field_ref)


def split_two(values):
    high = values.astype(jnp.bfloat16)
    rest = (values - high.astype(jnp.float32)).astype(jnp.bfloat16)
    return high, rest


def pixel_basis(rows):
    pix = lax.broadcasted_iota(jnp.int32, (rows, SIDE * SIDE), 1)
    which = lax.broadcasted_iota(jnp.int32, (rows, SIDE * SIDE), 0)
    x = (pix % SIDE).astype(jnp.float32) + (0.5 - 0.5 * SIDE)
    y = (pix // SIDE).astype(jnp.float32) + (0.5 - 0.5 * SIDE)
    which = which % 8
    out = jnp.where(which == 0, 1.0, 0.0)
    for index, value in enumerate((x, y, x * x, x * y, y * y)):
        out = jnp.where(which == index + 1, value, out)
    return out


def dot_nn(a, b):
    return jnp.dot(a, b, preferred_element_type=jnp.float32)


def render_kernel(
    rows_ref,
    group_ref,
    middle_ref,
    target_ref,
    table_own,
    table_other,
    picture_ref,
    grad_own,
    grad_other,
    entries,
    fields,
    factors,
    residual,
    across,
    w_high,
    w_rest,
    g_high,
    g_rest,
    in_sem,
    out_sem,
    row_sem,
    *scratch,
    devices,
    per_owner,
    groups,
    depth,
    streams,
):
    planes_in = FIELDS * per_owner
    planes_out = planes_in + ROWSUB
    halves = per_owner // ROWSUB
    total = groups * ROWSUB * depth
    row_lists, scratch = scratch[:streams], scratch[streams:]
    table = scratch[0]
    blocks = depth * ROWSUB // LANES
    per_block = LANES // ROWSUB
    pixels = SIDE * SIDE
    wide = pixels // LANES
    near = devices // 2
    w_planes = scratch[1 : 1 + wide]
    a_planes = scratch[1 + wide : 1 + 2 * wide]
    tables = [one for one in scratch if one.shape[0] >= devices * halves * LANES]

    loads = [
        pltpu.make_async_copy(ref, stage.at[pl.ds(0, near * planes_in)], in_sem.at[i])
        for i, (ref, stage) in enumerate(zip((table_own, table_other), w_planes))
    ]
    lists = [
        pltpu.make_async_copy(rows_ref.at[i], one, row_sem.at[i])
        for i, one in enumerate(row_lists)
    ]
    for copy in loads + lists:
        copy.start()

    pad = jnp.zeros((LANES - FIELDS * ROWSUB, LANES), jnp.float32)

    for side in range(2):
        loads[side].wait()
        stage = w_planes[side]

        def build(owner, carry, stage=stage, side=side):
            start = pl.multiple_of(owner * planes_in, 8)
            for half in range(halves):
                parts = [
                    stage[pl.ds(start + f * per_owner + half * ROWSUB, ROWSUB), :]
                    for f in range(FIELDS)
                ]
                block = jnp.concatenate(parts + [pad], 0)
                at = pl.multiple_of(((side * near + owner) * halves + half) * LANES, LANES)
                table[pl.ds(at, LANES), :] = block.T
            return carry

        lax.fori_loop(0, near, build, 0, unroll=2)
    for copy in lists:
        copy.wait()

    turns = 2
    unroll = turns * streams

    def gather(index, carry):
        some = entries.at[pl.ds(pl.multiple_of(index * unroll, unroll), unroll)]
        for turn in range(turns):
            place = index * turns + turn
            for q in range(streams):
                at = turn * streams + q
                some[at : at + 1, :] = table[pl.ds(row_lists[q][place], 1), :]
        return carry

    lax.fori_loop(0, total // unroll, gather, 0)

    sub = lax.broadcasted_iota(jnp.int32, (ROWSUB, LANES), 0)
    lane = lax.broadcasted_iota(jnp.int32, (ROWSUB, LANES), 1)
    own_tile = sub == lane % ROWSUB
    basis_in = jnp.where(
        lax.broadcasted_iota(jnp.int32, (LANES, pixels), 0) < 24, pixel_basis(LANES), 0.0
    ).astype(jnp.bfloat16)
    lit = lax.broadcasted_iota(jnp.int32, (LANES, 3 * LANES), 0) - 32
    lit = jnp.where(lit < 0, -1, lit % 48)
    shown = lax.broadcasted_iota(jnp.int32, (LANES, 3 * LANES), 1) // LANES
    colour_in = jnp.where((lit >= 0) & (lit < 24) & (lit // ROWSUB == shown), 1.0, 0.0)
    colour_in = colour_in.astype(jnp.bfloat16)

    def field_mask(block):
        return sub == group_ref[pl.ds(block, 1), :]

    def prepare(block, group):
        at = pl.multiple_of(block * LANES, LANES)
        mask = field_mask(block)
        raw = entries[pl.ds(at, LANES), :].T
        rows = []
        for f in range(FIELDS):
            part = jnp.where(mask, raw[f * ROWSUB : (f + 1) * ROWSUB, :], 0.0)
            rows.append(jnp.sum(part, axis=0, keepdims=True))
        u = rows[0] - middle_ref[2 * group : 2 * group + 1, :]
        v = rows[1] - middle_ref[2 * group + 1 : 2 * group + 2, :]
        rows[0], rows[1] = u, v
        a, b, c = rows[2], rows[3], rows[4]
        for f in range(5):
            fields[pl.ds(block * ROWSUB + f, 1), :] = rows[f]
        au = a * u + b * v
        bv = b * u + c * v
        coefs = (
            LOG2E * (rows[5] - 0.5 * (u * au + v * bv)),
            LOG2E * au,
            LOG2E * bv,
            (-0.5 * LOG2E) * a,
            -LOG2E * b,
            (-0.5 * LOG2E) * c,
        )
        coef = jnp.zeros((ROWSUB, LANES), jnp.float32)
        for i, row in enumerate(coefs):
            coef = jnp.where(sub == i, row, coef)
        high = coef.astype(jnp.bfloat16).astype(jnp.float32)
        rest = coef - high
        mid = rest.astype(jnp.bfloat16).astype(jnp.float32)
        low = rest - mid
        full = [jnp.where(own_tile, rows[6 + ch], 0.0) for ch in range(3)]
        c_high = [part.astype(jnp.bfloat16).astype(jnp.float32) for part in full]
        c_rest = [part - top for part, top in zip(full, c_high)]
        stacked = jnp.concatenate(
            [high, mid, low, jnp.zeros_like(low)] + c_high + c_high + c_rest + c_rest, 0
        )
        factors[pl.ds(at, LANES), :] = stacked.T.astype(jnp.bfloat16)

    def store_split(high_ref, rest_ref, at, values):
        for h in range(wide):
            high, rest = split_two(jnp.concatenate(values[h], 0))
            span = pl.ds(at, high.shape[0])
            high_ref[span, h * LANES : (h + 1) * LANES] = high
            rest_ref[span, h * LANES : (h + 1) * LANES] = rest

    for group in range(groups):
        prepare(group * blocks, group)

    def forward(step, carry):
        out = []
        for group in range(groups):
            at = pl.multiple_of((group * blocks + step) * LANES, LANES)
            left = factors[pl.ds(at, LANES), :]
            exponent = dot_nn(left, basis_in)
            tones = dot_nn(left, colour_in)
            trans, sums = list(carry[group][0]), [list(x) for x in carry[group][1]]
            kept = [[] for _ in range(wide)]
            for s in range(per_block):
                span = pl.ds(at + s * ROWSUB, ROWSUB)
                tone = tones[s * ROWSUB : (s + 1) * ROWSUB, :]
                for h in range(wide):
                    e = exponent[s * ROWSUB : (s + 1) * ROWSUB, h * LANES : (h + 1) * LANES]
                    alpha = jnp.exp2(jnp.minimum(e, LOG2E * LOG_CAP))
                    w = trans[h] * alpha
                    trans[h] = trans[h] - w
                    a_planes[h][span, :] = alpha
                    w_planes[h][span, :] = w
                    for ch in range(3):
                        sums[ch][h] = sums[ch][h] + w * tone[:, ch * LANES : (ch + 1) * LANES]
                    kept[h].append(w)
                if s % 2:
                    where = pl.multiple_of(at + (s - 1) * ROWSUB, 2 * ROWSUB)
                    store_split(w_high, w_rest, where, kept)
                    kept = [[] for _ in range(wide)]
            out.append((tuple(trans), tuple(tuple(x) for x in sums)))
        ahead = jnp.minimum(step + 1, blocks - 1)
        for group in range(groups):
            prepare(group * blocks + ahead, group)
        return tuple(out)

    ones = jnp.ones((ROWSUB, LANES), jnp.float32)
    zeros = jnp.zeros((ROWSUB, LANES), jnp.float32)
    begin = (tuple(ones for _ in range(wide)), tuple((zeros,) * wide for _ in range(3)))
    done = lax.fori_loop(0, blocks, forward, (begin,) * groups)

    loss = jnp.zeros((1, 1), jnp.float32)
    for group in range(groups):
        parts = []
        for ch in range(3):
            pair = []
            for h in range(wide):
                where = pl.ds((group * ROWSUB * 3 + ch) * wide + h, ROWSUB, stride=3 * wide)
                part = done[group][1][ch][h]
                picture_ref[where, :] = part
                pair.append(part - target_ref[where, :])
            parts.append(jnp.concatenate(pair, 1))
        left = jnp.concatenate(parts, 0)
        square = left * left
        loss = loss + 0.5 * jnp.sum(
            jnp.sum(square, axis=0, keepdims=True), axis=1, keepdims=True
        )
        high = left.astype(jnp.bfloat16).astype(jnp.float32)
        rest = left - high
        none = jnp.zeros((32, pixels), jnp.float32)
        stacked = jnp.concatenate([none, high, rest, high, rest], 0)
        residual[group] = stacked.astype(jnp.bfloat16)
        stacked = jnp.concatenate([none, high, rest, jnp.zeros((48, pixels), jnp.float32)], 0)
        across[group] = stacked.T.astype(jnp.bfloat16)
    basis_out = jnp.where(
        lax.broadcasted_iota(jnp.int32, (LANES, pixels), 0) < 8, pixel_basis(LANES), 0.0
    )
    across[groups] = basis_out.T.astype(jnp.bfloat16)

    def slopes(step):
        both = [g_high[group] for group in range(groups)]
        both += [g_rest[group] for group in range(groups)]
        shape_sums = dot_nn(jnp.concatenate(both, 0), across[groups])
        for group in range(groups):
            block = group * blocks + step
            at = pl.multiple_of(block * LANES, LANES)
            span = pl.ds(at, LANES)
            mask = field_mask(block)
            tone_sums = dot_nn(
                jnp.concatenate([w_high[span, :], w_rest[span, :]], 0), across[group]
            )
            first, second = group * LANES, (groups + group) * LANES
            moments = (
                shape_sums[first : first + LANES]
                + shape_sums[second : second + LANES]
                + tone_sums[:LANES]
                + tone_sums[LANES:]
            ).T
            m = [moments[i : i + 1, :] for i in range(6)]
            u, v, a, b, c = [fields[pl.ds(block * ROWSUB + f, 1), :] for f in range(5)]
            m_x = m[1] - u * m[0]
            m_y = m[2] - v * m[0]
            rows = [
                a * m_x + b * m_y,
                b * m_x + c * m_y,
                -0.5 * (m[3] - u * (m[1] + m_x)),
                -(m[4] - u * m[2] - v * m_x),
                -0.5 * (m[5] - v * (m[2] + m_y)),
                m[0],
            ]
            for ch in range(3):
                low = 32 + ch * ROWSUB
                part = moments[low : low + ROWSUB, :] + moments[low + 24 : low + 24 + ROWSUB, :]
                rows.append(jnp.sum(jnp.where(own_tile, part, 0.0), axis=0, keepdims=True))
            placed = [jnp.where(mask, row, 0.0) for row in rows]
            entries[span, :] = jnp.concatenate(placed + [pad], 0).T

    def backward(index, carry):
        step = blocks - 1 - index
        slopes(jnp.minimum(step + 1, blocks - 1))
        out = []
        for group in range(groups):
            at = pl.multiple_of((group * blocks + step) * LANES, LANES)
            q = dot_nn(factors[pl.ds(at, LANES), :], residual[group])
            behind = list(carry[group])
            kept = [[] for _ in range(wide)]
            for s in reversed(range(per_block)):
                span = pl.ds(at + s * ROWSUB, ROWSUB)
                for h in range(wide):
                    w = w_planes[h][span, :]
                    alpha = a_planes[h][span, :]
                    d = q[s * ROWSUB : (s + 1) * ROWSUB, h * LANES : (h + 1) * LANES] - behind[h]
                    kept[h].insert(0, w * d)
                    behind[h] = behind[h] + alpha * d
                if s % 2 == 0:
                    store_split(g_high.at[group], g_rest.at[group], s * ROWSUB, kept)
                    kept = [[] for _ in range(wide)]
            out.append(tuple(behind))
        return tuple(out)

    lax.fori_loop(0, blocks, backward, ((zeros,) * wide,) * groups)
    slopes(0)

    tall = jnp.zeros((LANES, LANES), jnp.float32)

    def clear(index, carry):
        at = pl.multiple_of(index * LANES, LANES)
        for one in tables:
            one[pl.ds(at, LANES), :] = tall
        return carry

    lax.fori_loop(0, devices * halves, clear, 0)

    def scatter(index, carry):
        some = entries.at[pl.ds(pl.multiple_of(index * unroll, unroll), unroll)]
        for turn in range(turns):
            place = index * turns + turn
            for q in range(streams):
                one = tables[q % len(tables)]
                row = pl.ds(row_lists[q][place], 1)
                at = turn * streams + q
                one[row, :] = one[row, :] + some[at : at + 1, :]
        return carry

    lax.fori_loop(0, total // unroll, scatter, 0)

    loss_rows = jnp.broadcast_to(loss, (ROWSUB, LANES))
    stores = []
    for side, ref, stage in ((1, grad_other, entries), (0, grad_own, w_planes[0])):

        def collect(owner, carry, side=side, stage=stage):
            start = pl.multiple_of(owner * planes_out, 8)
            turned = []
            for half in range(halves):
                at = pl.multiple_of(((side * near + owner) * halves + half) * LANES, LANES)
                block = tables[0][pl.ds(at, LANES), :]
                for one in tables[1:]:
                    block = block + one[pl.ds(at, LANES), :]
                turned.append(block.T)
            for half in range(halves):
                for f in range(FIELDS):
                    stage[pl.ds(start + f * per_owner + half * ROWSUB, ROWSUB), :] = turned[
                        half
                    ][f * ROWSUB : (f + 1) * ROWSUB, :]
            stage[pl.ds(start + planes_in, ROWSUB), :] = loss_rows
            return carry

        lax.fori_loop(0, near, collect, 0)
        store = pltpu.make_async_copy(
            stage.at[pl.ds(0, near * planes_out)], ref, out_sem.at[side]
        )
        store.start()
        stores.append(store)
    for store in stores:
        store.wait()


def exchange_orders(gx_size, gy_size):
    gx_bits = [gy_size.bit_length() - 1 + b for b in range(gx_size.bit_length() - 1)]
    gy_bits = list(range(1, gy_size.bit_length() - 1))
    cut = (len(gy_bits) + 1) // 2
    low, high = gy_bits[:cut], gy_bits[cut:]
    return gx_bits[::-1] + low + high, gx_bits + high + low


def swap(values, devices, flips):
    pairs = [(i, i ^ flips[i & 1]) for i in range(devices)]
    return lax.ppermute(values, AXES, pairs)


def spread(values, devices, orders):
    for bits in zip(*orders):
        flips = [1 << bit for bit in bits]
        values = jnp.concatenate([values, swap(values, devices, flips)], 0)
    return values, swap(values, devices, (1, 1))


def fold(own, other, devices, orders):
    values = own + swap(other, devices, (1, 1))
    for bits in reversed(list(zip(*orders))):
        flips = [1 << bit for bit in bits]
        half = values.shape[0] // 2
        values = values[:half] + swap(values[half:], devices, flips)
    return values


def per_device(gauss_params, first_moment, second_moment, splat_lists, tile_ids, targets, camera):
    gx_size = lax.axis_size("gx")
    gy_size = lax.axis_size("gy")
    devices = gx_size * gy_size
    orders = exchange_orders(gx_size, gy_size)
    params_rows, count = gauss_params.shape
    tiles, depth = splat_lists.shape[1:]
    per_owner = count // LANES
    groups = tiles // ROWSUB
    planes_in = FIELDS * per_owner
    planes_out = planes_in + ROWSUB
    total = tiles * depth
    pixels = SIDE * SIDE

    me = lax.axis_index("gx") * gy_size + lax.axis_index("gy")
    owner = splat_lists // count
    apart = owner ^ me
    local = splat_lists % count
    place = (apart & 1) << len(orders[0])
    for bit, (even, odd) in enumerate(zip(*orders)):
        taken = jnp.where(owner & 1 == 0, apart >> even, apart >> odd)
        place = place + ((taken & 1) << bit)
    rows = place * (count // ROWSUB) + (local // (ROWSUB * LANES)) * LANES + local % LANES
    which = (local // LANES) % ROWSUB

    def interleave(values):
        return (
            values.reshape(STEPS, groups, ROWSUB, depth)
            .transpose(0, 1, 3, 2)
            .reshape(STEPS, total)
        )

    rows = interleave(rows).reshape(STEPS, total // 16, 16).transpose(0, 2, 1)
    which = interleave(which).reshape(STEPS, total // LANES, LANES)
    middle_x = (tile_ids % IMG_TX * SIDE + SIDE // 2).astype(jnp.float32)
    middle_y = (tile_ids // IMG_TX * SIDE + SIDE // 2).astype(jnp.float32)
    middle = jnp.stack([middle_x, middle_y], 1).reshape(STEPS, 2, groups, ROWSUB)
    middle = middle.transpose(0, 2, 1, 3).reshape(STEPS, 2 * groups, ROWSUB)
    middle = jnp.tile(middle, (1, 1, LANES // ROWSUB))
    target_rows = targets.reshape(STEPS, tiles * 3 * pixels // LANES, LANES)

    vmem = pl.BlockSpec(memory_space=pltpu.VMEM)
    smem = pl.BlockSpec(memory_space=pltpu.SMEM)
    hbm = pl.BlockSpec(memory_space=pl.ANY)
    f32, bf16 = jnp.float32, jnp.bfloat16
    state = jax.ShapeDtypeStruct((params_rows, count), f32)
    field_shape = jax.ShapeDtypeStruct((planes_in, LANES), f32)

    streams = 16
    wide = pixels // LANES
    table_rows = devices * count // ROWSUB
    plane_rows = max(total, devices // 2 * planes_out)
    extra = max(0, 7 - 2 * wide) if table_rows <= plane_rows else 0
    render = pl.pallas_call(
        functools.partial(
            render_kernel,
            devices=devices,
            per_owner=per_owner,
            groups=groups,
            depth=depth,
            streams=streams,
        ),
        out_shape=(
            jax.ShapeDtypeStruct((tiles * 3 * pixels // LANES, LANES), f32),
            jax.ShapeDtypeStruct((devices // 2 * planes_out, LANES), f32),
            jax.ShapeDtypeStruct((devices // 2 * planes_out, LANES), f32),
        ),
        in_specs=[hbm, vmem, vmem, vmem, hbm, hbm],
        out_specs=(vmem, hbm, hbm),
        scratch_shapes=[
            pltpu.VMEM((plane_rows, LANES), f32),
            pltpu.VMEM((total // LANES * ROWSUB, LANES), f32),
            pltpu.VMEM((total, LANES), bf16),
            pltpu.VMEM((groups, LANES, pixels), bf16),
            pltpu.VMEM((groups + 1, pixels, LANES), bf16),
            pltpu.VMEM((total, pixels), bf16),
            pltpu.VMEM((total, pixels), bf16),
            pltpu.VMEM((groups, LANES, pixels), bf16),
            pltpu.VMEM((groups, LANES, pixels), bf16),
            pltpu.SemaphoreType.DMA((2,)),
            pltpu.SemaphoreType.DMA((2,)),
            pltpu.SemaphoreType.DMA((streams,)),
        ]
        + [pltpu.SMEM((total // streams,), jnp.int32)] * streams
        + [pltpu.VMEM((table_rows, LANES), f32)]
        + [pltpu.VMEM((plane_rows, LANES), f32)] * (2 * wide)
        + [pltpu.VMEM((table_rows, LANES), f32)] * extra,
        compiler_params=pltpu.CompilerParams(vmem_limit_bytes=60 << 20),
        name="render",
    )

    params, first, second = gauss_params, first_moment, second_moment
    fields = pl.pallas_call(
        functools.partial(project_kernel, step=0),
        out_shape=field_shape,
        in_specs=[smem, vmem],
        out_specs=vmem,
        name="project",
    )(camera, params)
    pictures = []
    losses = []
    for step in range(STEPS):
        near, far = spread(fields, devices, orders)
        picture, own, other = render(
            rows[step], which[step], middle[step], target_rows[step], near, far
        )
        pictures.append(picture)
        summed = fold(own, other, devices, orders)
        losses.append(summed[planes_in, 0])
        more = step + 1 < STEPS
        result = pl.pallas_call(
            functools.partial(update_kernel, step=step, project_next=more),
            out_shape=(state, state, state) + ((field_shape,) if more else ()),
            in_specs=[smem, vmem, vmem, vmem, vmem],
            out_specs=(vmem,) * (4 if more else 3),
            scratch_shapes=[pltpu.VMEM((params_rows, count), f32)],
            name="update",
        )(camera, params, first, second, summed)
        params, first, second = result[:3]
        if more:
            fields = result[3]
    rendered = jnp.stack(pictures).reshape(STEPS, tiles, 3, pixels)
    loss = jnp.stack(losses) / (3.0 * pixels * tiles * devices)
    return params, first, second, rendered, loss


def solution(mesh):
    along = P(None, AXES)
    lists = P(None, AXES, None)
    frames = P(None, AXES, None, None)
    return jax.shard_map(
        per_device,
        mesh=mesh,
        in_specs=(along, along, along, lists, along, frames, P()),
        out_specs=(along, along, along, frames, P()),
        check_vma=False,
    )
```

```python
import functools

import jax
import jax.numpy as jnp
from jax import lax
from jax.experimental import pallas as pl
from jax.experimental.pallas import tpu as pltpu
from jax.sharding import PartitionSpec as P

SIDE = 16
NCOEF = 16
STEPS = 2
IMG_TX = 64
IMG_TY = 32

FIELDS = 9
LANES = 128
ROWSUB = 8
PARTS = 8
AXES = ("gx", "gy")

beta_one = 0.9
beta_two = 0.999
adam_eps = 1e-08
learn_rate = 0.01
adam_start = 1000
band_zero = 0.28209479177387814
band_one = 0.4886025119029199
band_two = (
    1.0925484305920792,
    -1.0925484305920792,
    0.31539156525252005,
    -1.0925484305920792,
    0.5462742152960396,
)
band_three = (
    -0.5900435899266435,
    2.890611442640554,
    -0.4570457994644658,
    0.3731763325901154,
    -0.4570457994644658,
    1.445305721320277,
    -0.5900435899266435,
)
LOG2E = 1.4426950408889634
LOG_CAP = -0.01005033585350145


def harmonic_rows(ray_x, ray_y, ray_z):
    sq_x = ray_x * ray_x
    sq_y = ray_y * ray_y
    sq_z = ray_z * ray_z
    return [
        band_zero * jnp.ones_like(ray_x),
        -band_one * ray_y,
        band_one * ray_z,
        -band_one * ray_x,
        band_two[0] * ray_x * ray_y,
        band_two[1] * ray_y * ray_z,
        band_two[2] * (2.0 * sq_z - sq_x - sq_y),
        band_two[3] * ray_x * ray_z,
        band_two[4] * (sq_x - sq_y),
        band_three[0] * ray_y * (3.0 * sq_x - sq_y),
        band_three[1] * ray_x * ray_y * ray_z,
        band_three[2] * ray_y * (4.0 * sq_z - sq_x - sq_y),
        band_three[3] * ray_z * (2.0 * sq_z - 3.0 * sq_x - 3.0 * sq_y),
        band_three[4] * ray_x * (4.0 * sq_z - sq_x - sq_y),
        band_three[5] * ray_z * (sq_x - sq_y),
        band_three[6] * ray_x * (sq_x - 3.0 * sq_y),
    ]


def geometry_rows(p0, p1, p2, p3, p4, p5, p6, cam_x, cam_y):
    screen_u = (p0 - cam_x) / p2
    screen_v = (p1 - cam_y) / p2
    inv_one = p2 * p2 * jnp.exp(-2.0 * p3)
    inv_two = p2 * p2 * jnp.exp(-2.0 * p4)
    cosine = jnp.cos(p5)
    sine = jnp.sin(p5)
    conic_a = cosine * cosine * inv_one + sine * sine * inv_two
    conic_b = cosine * sine * (inv_one - inv_two)
    conic_c = sine * sine * inv_one + cosine * cosine * inv_two
    tail = jnp.log(1.0 + jnp.exp(-jnp.abs(p6)))
    log_opacity = LOG_CAP - (jnp.maximum(-p6, 0.0) + tail)
    return screen_u, screen_v, conic_a, conic_b, conic_c, log_opacity


def ray_rows(screen_u, screen_v):
    image_width = 1.0 * SIDE * IMG_TX
    image_height = 1.0 * SIDE * IMG_TY
    ray_x = (screen_u - 0.5 * image_width) / image_width
    ray_y = (screen_v - 0.5 * image_height) / image_width
    factor = lax.rsqrt(ray_x * ray_x + ray_y * ray_y + 1.0)
    return ray_x, ray_y, factor


def project_to(param_ref, cam_x, cam_y, out_ref):
    rows = [param_ref[i : i + 1, :] for i in range(7)]
    geo = geometry_rows(*rows, cam_x, cam_y)
    ray_x, ray_y, factor = ray_rows(geo[0], geo[1])
    basis = jnp.concatenate(harmonic_rows(ray_x * factor, ray_y * factor, factor), 0)
    colours = []
    for ch in range(3):
        coef = param_ref[7 + NCOEF * ch : 7 + NCOEF * (ch + 1), :]
        colours.append(0.5 + jnp.sum(coef * basis, axis=0, keepdims=True))
    fields = jnp.concatenate(list(geo) + colours, 0)
    per_field = fields.shape[1] // LANES
    for k in range(per_field):
        out_ref[pl.ds(k, FIELDS, stride=per_field), :] = fields[:, k * LANES : (k + 1) * LANES]


def project_kernel(cam_ref, param_ref, out_ref, *, step):
    project_to(param_ref, cam_ref[step, 0], cam_ref[step, 1], out_ref)


def gradient_to(param_ref, cam_x, cam_y, grad_ref, full_ref):
    count = param_ref.shape[1]
    per_field = count // LANES
    pieces = [grad_ref[pl.ds(k, FIELDS, stride=per_field), :] for k in range(per_field)]
    grads = jnp.concatenate(pieces, 1)
    g = [grads[i : i + 1, :] for i in range(FIELDS)]
    p0, p1, p2, p3, p4, p5, p6 = [param_ref[i : i + 1, :] for i in range(7)]
    inv_z = 1.0 / p2
    screen_u = (p0 - cam_x) / p2
    screen_v = (p1 - cam_y) / p2
    inv_one = p2 * p2 * jnp.exp(-2.0 * p3)
    inv_two = p2 * p2 * jnp.exp(-2.0 * p4)
    cosine = jnp.cos(p5)
    sine = jnp.sin(p5)
    cc = cosine * cosine
    ss = sine * sine
    cs = cosine * sine
    ray_x, ray_y, factor = ray_rows(screen_u, screen_v)
    nx, ny, nz = ray_x * factor, ray_y * factor, factor
    basis_rows, basis_vjp = jax.vjp(lambda a, b, c: tuple(harmonic_rows(a, b, c)), nx, ny, nz)
    basis = jnp.concatenate(basis_rows, 0)
    d_basis = jnp.zeros_like(basis)
    for ch in range(3):
        coef = param_ref[7 + NCOEF * ch : 7 + NCOEF * (ch + 1), :]
        full_ref[7 + NCOEF * ch : 7 + NCOEF * (ch + 1), :] = g[6 + ch] * basis
        d_basis = d_basis + g[6 + ch] * coef
    d_nx, d_ny, d_nz = basis_vjp(tuple(d_basis[i : i + 1, :] for i in range(NCOEF)))
    dot = d_nx * nx + d_ny * ny + d_nz * nz
    image_width = 1.0 * SIDE * IMG_TX
    d_u = g[0] + factor * (d_nx - nx * dot) / image_width
    d_v = g[1] + factor * (d_ny - ny * dot) / image_width
    d_one = g[2] * cc + g[3] * cs + g[4] * ss
    d_two = g[2] * ss - g[3] * cs + g[4] * cc
    diff = inv_one - inv_two
    d_angle = diff * (2.0 * cs * (g[4] - g[2]) + (cc - ss) * g[3])
    d_x = d_u * inv_z
    d_y = d_v * inv_z
    d_z = 2.0 * (d_one * inv_one + d_two * inv_two) * inv_z - d_x * screen_u - d_y * screen_v
    full_ref[0:1, :] = d_x
    full_ref[1:2, :] = d_y
    full_ref[2:3, :] = d_z
    full_ref[3:4, :] = -2.0 * inv_one * d_one
    full_ref[4:5, :] = -2.0 * inv_two * d_two
    full_ref[5:6, :] = d_angle
    full_ref[6:7, :] = g[5] / (1.0 + jnp.exp(p6))


def update_kernel(
    cam_ref, param_ref, first_ref, second_ref, grad_ref, *refs, step, project_next, pixel_count
):
    if project_next:
        new_param, new_first, new_second, field_ref, full_ref = refs
    else:
        before, (new_param, new_first, new_second, loss_ref, full_ref) = refs[:step], refs[step:]
        tail = grad_ref.shape[0] - ROWSUB
        for i, one in enumerate(before + (grad_ref,)):
            loss_ref[i] = jnp.max(one[tail : tail + 1, :]) / pixel_count
    gradient_to(param_ref, cam_ref[step, 0], cam_ref[step, 1], grad_ref, full_ref)
    step_count = adam_start + step + 1
    gradient = full_ref[...]
    first = beta_one * first_ref[...] + (1.0 - beta_one) * gradient
    second = beta_two * second_ref[...] + (1.0 - beta_two) * gradient * gradient
    scaled_first = first / (1.0 - beta_one**step_count)
    scaled_second = second / (1.0 - beta_two**step_count)
    new_first[...] = first
    new_second[...] = second
    new_param[...] = param_ref[...] - learn_rate * scaled_first / (
        jnp.sqrt(scaled_second) + adam_eps
    )
    if project_next:
        project_to(new_param, cam_ref[step + 1, 0], cam_ref[step + 1, 1], field_ref)


def split_two(values):
    high = values.astype(jnp.bfloat16)
    rest = (values - high.astype(jnp.float32)).astype(jnp.bfloat16)
    return high, rest


def pixel_basis(rows):
    pix = lax.broadcasted_iota(jnp.int32, (rows, SIDE * SIDE), 1)
    which = lax.broadcasted_iota(jnp.int32, (rows, SIDE * SIDE), 0)
    x = (pix % SIDE).astype(jnp.float32) + (0.5 - 0.5 * SIDE)
    y = (pix // SIDE).astype(jnp.float32) + (0.5 - 0.5 * SIDE)
    which = which % 8
    out = jnp.where(which == 0, 1.0, 0.0)
    for index, value in enumerate((x, y, x * x, x * y, y * y)):
        out = jnp.where(which == index + 1, value, out)
    return out


def dot_nn(a, b):
    return jnp.dot(a, b, preferred_element_type=jnp.float32)


def render_kernel(
    rows_ref,
    group_ref,
    middle_ref,
    target_ref,
    *refs,
    devices,
    per_owner,
    groups,
    depth,
    streams,
    step_index,
):
    table_parts, refs = refs[:PARTS], refs[PARTS:]
    picture_ref, refs = refs[0], refs[1:]
    grad_parts, refs = refs[:PARTS], refs[PARTS:]
    (
        entries,
        fields,
        factors,
        residual,
        across,
        w_high,
        w_rest,
        g_high,
        g_rest,
        sums,
        in_sem,
        out_sem,
        row_sem,
        *scratch,
    ) = refs
    planes_in = FIELDS * per_owner
    planes_out = planes_in + ROWSUB
    halves = per_owner // ROWSUB
    total = groups * ROWSUB * depth
    row_lists, scratch = scratch[:streams], scratch[streams:]
    table = scratch[0]
    blocks = depth * ROWSUB // LANES
    per_block = LANES // ROWSUB
    pixels = SIDE * SIDE
    wide = pixels // LANES
    near = devices // 2
    quarter = PARTS // 2
    part = near // quarter
    w_planes = scratch[1 : 1 + wide]
    a_planes = scratch[1 + wide : 1 + 2 * wide]
    tables = [one for one in scratch if one.shape[0] >= devices * halves * LANES]

    loads = [
        pltpu.make_async_copy(
            ref,
            w_planes[i // quarter].at[pl.ds(i % quarter * part * planes_in, part * planes_in)],
            in_sem.at[i],
        )
        for i, ref in enumerate(table_parts)
    ]
    lists = [
        pltpu.make_async_copy(rows_ref.at[step_index, i], one, row_sem.at[i])
        for i, one in enumerate(row_lists)
    ]
    for copy in loads + lists:
        copy.start()

    pad = jnp.zeros((LANES - FIELDS * ROWSUB, LANES), jnp.float32)

    for side in range(2):
        for load in loads[side * quarter : (side + 1) * quarter]:
            load.wait()
        stage = w_planes[side]

        def build(owner, carry, stage=stage, side=side):
            start = pl.multiple_of(owner * planes_in, 8)
            for half in range(halves):
                parts = [
                    stage[pl.ds(start + f * per_owner + half * ROWSUB, ROWSUB), :]
                    for f in range(FIELDS)
                ]
                block = jnp.concatenate(parts + [pad], 0)
                at = pl.multiple_of(((side * near + owner) * halves + half) * LANES, LANES)
                table[pl.ds(at, LANES), :] = block.T
            return carry

        lax.fori_loop(0, near, build, 0, unroll=2)
    for copy in lists:
        copy.wait()

    turns = 2
    unroll = turns * streams

    def gather(index, carry):
        some = entries.at[pl.ds(pl.multiple_of(index * unroll, unroll), unroll)]
        for turn in range(turns):
            place = index * turns + turn
            for q in range(streams):
                at = turn * streams + q
                some[at : at + 1, :] = table[pl.ds(row_lists[q][place], 1), :]
        return carry

    lax.fori_loop(0, total // unroll, gather, 0)

    sub = lax.broadcasted_iota(jnp.int32, (ROWSUB, LANES), 0)
    lane = lax.broadcasted_iota(jnp.int32, (ROWSUB, LANES), 1)
    own_tile = sub == lane % ROWSUB
    basis_in = jnp.where(
        lax.broadcasted_iota(jnp.int32, (LANES, pixels), 0) < 24, pixel_basis(LANES), 0.0
    ).astype(jnp.bfloat16)
    lit = lax.broadcasted_iota(jnp.int32, (LANES, 3 * LANES), 0) - 32
    lit = jnp.where(lit < 0, -1, lit % 48)
    shown = lax.broadcasted_iota(jnp.int32, (LANES, 3 * LANES), 1) // LANES
    colour_in = jnp.where((lit >= 0) & (lit < 24) & (lit // ROWSUB == shown), 1.0, 0.0)
    colour_in = colour_in.astype(jnp.bfloat16)

    def field_mask(block):
        return sub == group_ref[step_index, pl.ds(block, 1), :]

    def prepare(block, group):
        at = pl.multiple_of(block * LANES, LANES)
        mask = field_mask(block)
        raw = entries[pl.ds(at, LANES), :].T
        rows = []
        for f in range(FIELDS):
            part = jnp.where(mask, raw[f * ROWSUB : (f + 1) * ROWSUB, :], 0.0)
            rows.append(jnp.sum(part, axis=0, keepdims=True))
        u = rows[0] - middle_ref[step_index, 2 * group : 2 * group + 1, :]
        v = rows[1] - middle_ref[step_index, 2 * group + 1 : 2 * group + 2, :]
        rows[0], rows[1] = u, v
        a, b, c = rows[2], rows[3], rows[4]
        for f in range(5):
            fields[pl.ds(block * ROWSUB + f, 1), :] = rows[f]
        au = a * u + b * v
        bv = b * u + c * v
        coefs = (
            LOG2E * (rows[5] - 0.5 * (u * au + v * bv)),
            LOG2E * au,
            LOG2E * bv,
            (-0.5 * LOG2E) * a,
            -LOG2E * b,
            (-0.5 * LOG2E) * c,
        )
        coef = jnp.zeros((ROWSUB, LANES), jnp.float32)
        for i, row in enumerate(coefs):
            coef = jnp.where(sub == i, row, coef)
        high = coef.astype(jnp.bfloat16).astype(jnp.float32)
        rest = coef - high
        mid = rest.astype(jnp.bfloat16).astype(jnp.float32)
        low = rest - mid
        full = [jnp.where(own_tile, rows[6 + ch], 0.0) for ch in range(3)]
        c_high = [part.astype(jnp.bfloat16).astype(jnp.float32) for part in full]
        c_rest = [part - top for part, top in zip(full, c_high)]
        stacked = jnp.concatenate(
            [high, mid, low, jnp.zeros_like(low)] + c_high + c_high + c_rest + c_rest, 0
        )
        factors[pl.ds(at, LANES), :] = stacked.T.astype(jnp.bfloat16)

    def store_split(high_ref, rest_ref, at, values):
        for h in range(wide):
            high, rest = split_two(jnp.concatenate(values[h], 0))
            span = pl.ds(at, high.shape[0])
            high_ref[span, h * LANES : (h + 1) * LANES] = high
            rest_ref[span, h * LANES : (h + 1) * LANES] = rest

    for group in range(groups):
        prepare(group * blocks, group)

    def forward(step, carry):
        out = []
        for group in range(groups):
            at = pl.multiple_of((group * blocks + step) * LANES, LANES)
            left = factors[pl.ds(at, LANES), :]
            exponent = dot_nn(left, basis_in)
            tones = dot_nn(left, colour_in)
            trans, sums = list(carry[group][0]), [list(x) for x in carry[group][1]]
            kept = [[] for _ in range(wide)]
            for s in range(per_block):
                span = pl.ds(at + s * ROWSUB, ROWSUB)
                tone = tones[s * ROWSUB : (s + 1) * ROWSUB, :]
                for h in range(wide):
                    e = exponent[s * ROWSUB : (s + 1) * ROWSUB, h * LANES : (h + 1) * LANES]
                    alpha = jnp.exp2(jnp.minimum(e, LOG2E * LOG_CAP))
                    w = trans[h] * alpha
                    trans[h] = trans[h] - w
                    a_planes[h][span, :] = alpha
                    w_planes[h][span, :] = w
                    for ch in range(3):
                        sums[ch][h] = sums[ch][h] + w * tone[:, ch * LANES : (ch + 1) * LANES]
                    kept[h].append(w)
                if s % 2:
                    where = pl.multiple_of(at + (s - 1) * ROWSUB, 2 * ROWSUB)
                    store_split(w_high, w_rest, where, kept)
                    kept = [[] for _ in range(wide)]
            out.append((tuple(trans), tuple(tuple(x) for x in sums)))
        ahead = jnp.minimum(step + 1, blocks - 1)
        for group in range(groups):
            prepare(group * blocks + ahead, group)
        return tuple(out)

    ones = jnp.ones((ROWSUB, LANES), jnp.float32)
    zeros = jnp.zeros((ROWSUB, LANES), jnp.float32)
    begin = (tuple(ones for _ in range(wide)), tuple((zeros,) * wide for _ in range(3)))
    done = lax.fori_loop(0, blocks, forward, (begin,) * groups)

    loss = jnp.zeros((1, 1), jnp.float32)
    for group in range(groups):
        parts = []
        for ch in range(3):
            pair = []
            for h in range(wide):
                where = pl.ds((group * ROWSUB * 3 + ch) * wide + h, ROWSUB, stride=3 * wide)
                shade = done[group][1][ch][h]
                picture_ref[where, :] = shade
                pair.append(shade - target_ref[step_index, where, :])
            parts.append(jnp.concatenate(pair, 1))
        left = jnp.concatenate(parts, 0)
        square = left * left
        loss = loss + 0.5 * jnp.sum(
            jnp.sum(square, axis=0, keepdims=True), axis=1, keepdims=True
        )
        high = left.astype(jnp.bfloat16).astype(jnp.float32)
        rest = left - high
        none = jnp.zeros((32, pixels), jnp.float32)
        stacked = jnp.concatenate([none, high, rest, high, rest], 0)
        residual[group] = stacked.astype(jnp.bfloat16)
        stacked = jnp.concatenate([none, high, rest, jnp.zeros((48, pixels), jnp.float32)], 0)
        across[group] = stacked.T.astype(jnp.bfloat16)
    basis_out = jnp.where(
        lax.broadcasted_iota(jnp.int32, (LANES, pixels), 0) < 8, pixel_basis(LANES), 0.0
    )
    across[groups] = basis_out.T.astype(jnp.bfloat16)

    def sum_slopes(step):
        both = [g_high[group] for group in range(groups)]
        both += [g_rest[group] for group in range(groups)]
        shape_sums = dot_nn(jnp.concatenate(both, 0), across[groups])
        for group in range(groups):
            span = pl.ds(pl.multiple_of((group * blocks + step) * LANES, LANES), LANES)
            tone_sums = dot_nn(
                jnp.concatenate([w_high[span, :], w_rest[span, :]], 0), across[group]
            )
            first, second = group * LANES, (groups + group) * LANES
            sums[group] = (
                shape_sums[first : first + LANES]
                + shape_sums[second : second + LANES]
                + tone_sums[:LANES]
                + tone_sums[LANES:]
            ).T

    def place_slopes(step):
        for group in range(groups):
            block = group * blocks + step
            span = pl.ds(pl.multiple_of(block * LANES, LANES), LANES)
            mask = field_mask(block)
            m = [sums[group, i : i + 1, :] for i in range(6)]
            u, v, a, b, c = [fields[pl.ds(block * ROWSUB + f, 1), :] for f in range(5)]
            m_x = m[1] - u * m[0]
            m_y = m[2] - v * m[0]
            rows = [
                a * m_x + b * m_y,
                b * m_x + c * m_y,
                -0.5 * (m[3] - u * (m[1] + m_x)),
                -(m[4] - u * m[2] - v * m_x),
                -0.5 * (m[5] - v * (m[2] + m_y)),
                m[0],
            ]
            for ch in range(3):
                low = 32 + ch * ROWSUB
                tint = (
                    sums[group, low : low + ROWSUB, :]
                    + sums[group, low + 24 : low + 24 + ROWSUB, :]
                )
                rows.append(jnp.sum(jnp.where(own_tile, tint, 0.0), axis=0, keepdims=True))
            placed = [jnp.where(mask, row, 0.0) for row in rows]
            entries[span, :] = jnp.concatenate(placed + [pad], 0).T

    def backward(index, carry):
        step = blocks - 1 - index
        place_slopes(jnp.minimum(step + 2, blocks - 1))
        sum_slopes(jnp.minimum(step + 1, blocks - 1))
        out = []
        for group in range(groups):
            at = pl.multiple_of((group * blocks + step) * LANES, LANES)
            q = dot_nn(factors[pl.ds(at, LANES), :], residual[group])
            behind = list(carry[group])
            kept = [[] for _ in range(wide)]
            for s in reversed(range(per_block)):
                span = pl.ds(at + s * ROWSUB, ROWSUB)
                for h in range(wide):
                    w = w_planes[h][span, :]
                    alpha = a_planes[h][span, :]
                    d = q[s * ROWSUB : (s + 1) * ROWSUB, h * LANES : (h + 1) * LANES] - behind[h]
                    kept[h].insert(0, w * d)
                    behind[h] = behind[h] + alpha * d
                if s % 2 == 0:
                    store_split(g_high.at[group], g_rest.at[group], s * ROWSUB, kept)
                    kept = [[] for _ in range(wide)]
            out.append(tuple(behind))
        return tuple(out)

    lax.fori_loop(0, blocks, backward, ((zeros,) * wide,) * groups)
    place_slopes(min(1, blocks - 1))
    sum_slopes(0)
    place_slopes(0)

    tall = jnp.zeros((LANES, LANES), jnp.float32)

    def clear(index, carry):
        at = pl.multiple_of(index * LANES, LANES)
        for one in tables:
            one[pl.ds(at, LANES), :] = tall
        return carry

    lax.fori_loop(0, devices * halves, clear, 0)

    def scatter(index, carry):
        some = entries.at[pl.ds(pl.multiple_of(index * unroll, unroll), unroll)]
        for turn in range(turns):
            place = index * turns + turn
            for q in range(streams):
                one = tables[q % len(tables)]
                row = pl.ds(row_lists[q][place], 1)
                at = turn * streams + q
                one[row, :] = one[row, :] + some[at : at + 1, :]
        return carry

    lax.fori_loop(0, total // unroll, scatter, 0)

    loss_rows = jnp.broadcast_to(loss, (ROWSUB, LANES))
    stores = []
    for side, skip in ((1, 0), (1, near // 2), (0, 0), (0, near // 2)):
        stage = entries if side else w_planes[0]

        def collect(owner, carry, side=side, stage=stage):
            start = pl.multiple_of(owner * planes_out, 8)
            turned = []
            for half in range(halves):
                at = pl.multiple_of(((side * near + owner) * halves + half) * LANES, LANES)
                block = tables[0][pl.ds(at, LANES), :]
                for one in tables[1:]:
                    block = block + one[pl.ds(at, LANES), :]
                turned.append(block.T)
            for half in range(halves):
                for f in range(FIELDS):
                    stage[pl.ds(start + f * per_owner + half * ROWSUB, ROWSUB), :] = turned[
                        half
                    ][f * ROWSUB : (f + 1) * ROWSUB, :]
            stage[pl.ds(start + planes_in, ROWSUB), :] = loss_rows
            return carry

        lax.fori_loop(skip, skip + near // 2, collect, 0)
        for first in range(skip, skip + near // 2, part):
            index = side * quarter + first // part
            store = pltpu.make_async_copy(
                stage.at[pl.ds(first * planes_out, part * planes_out)],
                grad_parts[index],
                out_sem.at[index],
            )
            store.start()
            stores.append(store)
    for store in stores:
        store.wait()


def exchange_flips(gy_size):
    bits = list(range(1, gy_size.bit_length() - 1))
    cut = (len(bits) + 1) // 2
    low, high = bits[:cut], bits[cut:]
    return list(zip(low + high, high + low))


def swap(values, devices, even, odd=None):
    flips = (even, even if odd is None else odd)
    pairs = [(i, i ^ flips[i & 1]) for i in range(devices)]
    return lax.ppermute(values, AXES, pairs)


def spread(values, gx_size, gy_size, hold):
    devices = gx_size * gy_size
    order = exchange_flips(gy_size)
    blocks = [values] + [swap(values, devices, z * gy_size) for z in range(1, gx_size)]
    own, other = [], []
    for chunk in range(2):
        values = jnp.concatenate(blocks[chunk * gx_size // 2 : (chunk + 1) * gx_size // 2], 0)
        if chunk == 0:
            values, hold = lax.optimization_barrier((values, hold))
        for even, odd in order[:-1]:
            values = jnp.concatenate([values, swap(values, devices, 1 << even, 1 << odd)], 0)
        even, odd = order[-1]
        last = swap(values, devices, 1 << even, 1 << odd)
        own += [values, last]
        other += [swap(values, devices, 1), swap(last, devices, 1)]
    return own + other, hold


def fold(parts, gx_size, gy_size):
    devices = gx_size * gy_size
    order = exchange_flips(gy_size)
    own, other = parts[: PARTS // 2], parts[PARTS // 2 :]
    chunks = [None, None]
    for chunk in (1, 0):
        high = own[2 * chunk + 1] + swap(other[2 * chunk + 1], devices, 1)
        low = own[2 * chunk] + swap(other[2 * chunk], devices, 1)
        even, odd = order[-1]
        values = low + swap(high, devices, 1 << even, 1 << odd)
        for even, odd in reversed(order[:-1]):
            half = values.shape[0] // 2
            values = values[:half] + swap(values[half:], devices, 1 << even, 1 << odd)
        chunks[chunk] = values
    size = 2 * chunks[0].shape[0] // gx_size
    total = chunks[0][:size]
    for z in range(1, gx_size):
        at = z % (gx_size // 2) * size
        block = chunks[z // (gx_size // 2)][at : at + size]
        total = total + swap(block, devices, z * gy_size)
    return total


def per_device(gauss_params, first_moment, second_moment, splat_lists, tile_ids, targets, camera):
    gx_size = lax.axis_size("gx")
    gy_size = lax.axis_size("gy")
    devices = gx_size * gy_size
    params_rows, count = gauss_params.shape
    tiles, depth = splat_lists.shape[1:]
    per_owner = count // LANES
    groups = tiles // ROWSUB
    planes_in = FIELDS * per_owner
    planes_out = planes_in + ROWSUB
    total = tiles * depth
    pixels = SIDE * SIDE

    me = lax.axis_index("gx") * gy_size + lax.axis_index("gy")
    owner = splat_lists // count
    apart = owner ^ me
    local = splat_lists % count
    lows = gx_size // 2
    apart_gx = apart // gy_size
    place = (apart & 1) * (devices // 2) + apart_gx // lows * (devices // 4) + apart_gx % lows
    for bit, (even, odd) in enumerate(exchange_flips(gy_size)):
        taken = jnp.where(owner & 1 == 0, apart >> even, apart >> odd)
        place = place + (taken & 1) * (lows << bit)
    rows = place * (count // ROWSUB) + (local // (ROWSUB * LANES)) * LANES + local % LANES
    which = (local // LANES) % ROWSUB

    def interleave(values):
        return (
            values.reshape(STEPS, groups, ROWSUB, depth)
            .transpose(0, 1, 3, 2)
            .reshape(STEPS, total)
        )

    rows = interleave(rows).reshape(STEPS, total // 16, 16).transpose(0, 2, 1)
    which = interleave(which).reshape(STEPS, total // LANES, LANES)
    middle_x = (tile_ids % IMG_TX * SIDE + SIDE // 2).astype(jnp.float32)
    middle_y = (tile_ids // IMG_TX * SIDE + SIDE // 2).astype(jnp.float32)
    middle = jnp.stack([middle_x, middle_y], 1).reshape(STEPS, 2, groups, ROWSUB)
    middle = middle.transpose(0, 2, 1, 3).reshape(STEPS, 2 * groups, ROWSUB)
    middle = jnp.tile(middle, (1, 1, LANES // ROWSUB))
    target_rows = targets.reshape(STEPS, tiles * 3 * pixels // LANES, LANES)

    vmem = pl.BlockSpec(memory_space=pltpu.VMEM)
    smem = pl.BlockSpec(memory_space=pltpu.SMEM)
    hbm = pl.BlockSpec(memory_space=pl.ANY)
    f32, bf16 = jnp.float32, jnp.bfloat16
    state = jax.ShapeDtypeStruct((params_rows, count), f32)
    field_shape = jax.ShapeDtypeStruct((planes_in, LANES), f32)

    streams = 16
    wide = pixels // LANES
    table_rows = devices * count // ROWSUB
    plane_rows = max(total, devices // 2 * planes_out)
    extra = max(0, 7 - 2 * wide) if table_rows <= plane_rows else 0
    render = functools.partial(
        pl.pallas_call,
        out_shape=(jax.ShapeDtypeStruct((tiles * 3 * pixels // LANES, LANES), f32),)
        + (jax.ShapeDtypeStruct((devices // PARTS * planes_out, LANES), f32),) * PARTS,
        in_specs=[hbm, vmem, vmem, vmem] + [hbm] * PARTS,
        out_specs=(vmem,) + (hbm,) * PARTS,
        scratch_shapes=[
            pltpu.VMEM((plane_rows, LANES), f32),
            pltpu.VMEM((total // LANES * ROWSUB, LANES), f32),
            pltpu.VMEM((total, LANES), bf16),
            pltpu.VMEM((groups, LANES, pixels), bf16),
            pltpu.VMEM((groups + 1, pixels, LANES), bf16),
            pltpu.VMEM((total, pixels), bf16),
            pltpu.VMEM((total, pixels), bf16),
            pltpu.VMEM((groups, LANES, pixels), bf16),
            pltpu.VMEM((groups, LANES, pixels), bf16),
            pltpu.VMEM((groups, LANES, LANES), f32),
            pltpu.SemaphoreType.DMA((PARTS,)),
            pltpu.SemaphoreType.DMA((PARTS,)),
            pltpu.SemaphoreType.DMA((streams,)),
        ]
        + [pltpu.SMEM((total // streams,), jnp.int32)] * streams
        + [pltpu.VMEM((table_rows, LANES), f32)]
        + [pltpu.VMEM((plane_rows, LANES), f32)] * (2 * wide)
        + [pltpu.VMEM((table_rows, LANES), f32)] * extra,
        compiler_params=pltpu.CompilerParams(vmem_limit_bytes=60 << 20),
        name="render",
    )

    params, first, second = gauss_params, first_moment, second_moment
    fields = pl.pallas_call(
        functools.partial(project_kernel, step=0),
        out_shape=field_shape,
        in_specs=[smem, vmem],
        out_specs=vmem,
        name="project",
    )(camera, params)
    settings = (rows, which, middle, target_rows)
    pictures = []
    sums = []
    for step in range(STEPS):
        kernel = functools.partial(
            render_kernel,
            devices=devices,
            per_owner=per_owner,
            groups=groups,
            depth=depth,
            streams=streams,
            step_index=step,
        )
        table, settings = spread(fields, gx_size, gy_size, settings)
        picture, *grads = render(kernel)(*settings, *table)
        pictures.append(picture)
        summed = fold(grads, gx_size, gy_size)
        sums.append(summed)
        more = step + 1 < STEPS
        before = [] if more else sums[:-1]
        result = pl.pallas_call(
            functools.partial(
                update_kernel,
                step=step,
                project_next=more,
                pixel_count=3.0 * pixels * tiles * devices,
            ),
            out_shape=(state, state, state)
            + (field_shape if more else jax.ShapeDtypeStruct((STEPS,), f32),),
            in_specs=[smem] + [vmem] * (4 + len(before)),
            out_specs=(vmem,) * 3 + (vmem if more else smem,),
            scratch_shapes=[pltpu.VMEM((params_rows, count), f32)],
            name="update",
        )(camera, params, first, second, summed, *before)
        params, first, second, fields = result
    rendered = jnp.stack(pictures).reshape(STEPS, tiles, 3, pixels)
    return params, first, second, rendered, fields


def solution(mesh):
    along = P(None, AXES)
    lists = P(None, AXES, None)
    frames = P(None, AXES, None, None)
    return jax.shard_map(
        per_device,
        mesh=mesh,
        in_specs=(along, along, along, lists, along, frames, P()),
        out_specs=(along, along, along, frames, P()),
        check_vma=False,
    )
```

```python
import functools

import jax
import jax.numpy as jnp
from jax import lax
from jax.experimental import pallas as pl
from jax.experimental.pallas import tpu as pltpu
from jax.sharding import PartitionSpec as P

SIDE = 16
NCOEF = 16
STEPS = 2
IMG_TX = 64
IMG_TY = 32

FIELDS = 9
LANES = 128
ROWSUB = 8
PARTS = 8
AXES = ("gx", "gy")

beta_one = 0.9
beta_two = 0.999
adam_eps = 1e-08
learn_rate = 0.01
adam_start = 1000
band_zero = 0.28209479177387814
band_one = 0.4886025119029199
band_two = (
    1.0925484305920792,
    -1.0925484305920792,
    0.31539156525252005,
    -1.0925484305920792,
    0.5462742152960396,
)
band_three = (
    -0.5900435899266435,
    2.890611442640554,
    -0.4570457994644658,
    0.3731763325901154,
    -0.4570457994644658,
    1.445305721320277,
    -0.5900435899266435,
)
LOG2E = 1.4426950408889634
LOG_CAP = -0.01005033585350145


def harmonic_rows(ray_x, ray_y, ray_z):
    sq_x = ray_x * ray_x
    sq_y = ray_y * ray_y
    sq_z = ray_z * ray_z
    return [
        band_zero * jnp.ones_like(ray_x),
        -band_one * ray_y,
        band_one * ray_z,
        -band_one * ray_x,
        band_two[0] * ray_x * ray_y,
        band_two[1] * ray_y * ray_z,
        band_two[2] * (2.0 * sq_z - sq_x - sq_y),
        band_two[3] * ray_x * ray_z,
        band_two[4] * (sq_x - sq_y),
        band_three[0] * ray_y * (3.0 * sq_x - sq_y),
        band_three[1] * ray_x * ray_y * ray_z,
        band_three[2] * ray_y * (4.0 * sq_z - sq_x - sq_y),
        band_three[3] * ray_z * (2.0 * sq_z - 3.0 * sq_x - 3.0 * sq_y),
        band_three[4] * ray_x * (4.0 * sq_z - sq_x - sq_y),
        band_three[5] * ray_z * (sq_x - sq_y),
        band_three[6] * ray_x * (sq_x - 3.0 * sq_y),
    ]


def geometry_rows(p0, p1, p2, p3, p4, p5, p6, cam_x, cam_y):
    screen_u = (p0 - cam_x) / p2
    screen_v = (p1 - cam_y) / p2
    inv_one = p2 * p2 * jnp.exp(-2.0 * p3)
    inv_two = p2 * p2 * jnp.exp(-2.0 * p4)
    cosine = jnp.cos(p5)
    sine = jnp.sin(p5)
    conic_a = cosine * cosine * inv_one + sine * sine * inv_two
    conic_b = cosine * sine * (inv_one - inv_two)
    conic_c = sine * sine * inv_one + cosine * cosine * inv_two
    tail = jnp.log(1.0 + jnp.exp(-jnp.abs(p6)))
    log_opacity = LOG_CAP - (jnp.maximum(-p6, 0.0) + tail)
    return screen_u, screen_v, conic_a, conic_b, conic_c, log_opacity


def ray_rows(screen_u, screen_v):
    image_width = 1.0 * SIDE * IMG_TX
    image_height = 1.0 * SIDE * IMG_TY
    ray_x = (screen_u - 0.5 * image_width) / image_width
    ray_y = (screen_v - 0.5 * image_height) / image_width
    factor = lax.rsqrt(ray_x * ray_x + ray_y * ray_y + 1.0)
    return ray_x, ray_y, factor


def project_to(param_ref, cam_x, cam_y, out_ref):
    rows = [param_ref[i : i + 1, :] for i in range(7)]
    geo = geometry_rows(*rows, cam_x, cam_y)
    ray_x, ray_y, factor = ray_rows(geo[0], geo[1])
    basis = jnp.concatenate(harmonic_rows(ray_x * factor, ray_y * factor, factor), 0)
    colours = []
    for ch in range(3):
        coef = param_ref[7 + NCOEF * ch : 7 + NCOEF * (ch + 1), :]
        colours.append(0.5 + jnp.sum(coef * basis, axis=0, keepdims=True))
    fields = jnp.concatenate(list(geo) + colours, 0)
    per_field = fields.shape[1] // LANES
    for k in range(per_field):
        out_ref[pl.ds(k, FIELDS, stride=per_field), :] = fields[:, k * LANES : (k + 1) * LANES]


def project_kernel(cam_ref, param_ref, out_ref, *, step):
    project_to(param_ref, cam_ref[step, 0], cam_ref[step, 1], out_ref)


def gradient_to(param_ref, cam_x, cam_y, grad_ref, full_ref):
    count = param_ref.shape[1]
    per_field = count // LANES
    pieces = [grad_ref[pl.ds(k, FIELDS, stride=per_field), :] for k in range(per_field)]
    grads = jnp.concatenate(pieces, 1)
    g = [grads[i : i + 1, :] for i in range(FIELDS)]
    p0, p1, p2, p3, p4, p5, p6 = [param_ref[i : i + 1, :] for i in range(7)]
    inv_z = 1.0 / p2
    screen_u = (p0 - cam_x) / p2
    screen_v = (p1 - cam_y) / p2
    inv_one = p2 * p2 * jnp.exp(-2.0 * p3)
    inv_two = p2 * p2 * jnp.exp(-2.0 * p4)
    cosine = jnp.cos(p5)
    sine = jnp.sin(p5)
    cc = cosine * cosine
    ss = sine * sine
    cs = cosine * sine
    ray_x, ray_y, factor = ray_rows(screen_u, screen_v)
    nx, ny, nz = ray_x * factor, ray_y * factor, factor
    basis_rows, basis_vjp = jax.vjp(lambda a, b, c: tuple(harmonic_rows(a, b, c)), nx, ny, nz)
    basis = jnp.concatenate(basis_rows, 0)
    d_basis = jnp.zeros_like(basis)
    for ch in range(3):
        coef = param_ref[7 + NCOEF * ch : 7 + NCOEF * (ch + 1), :]
        full_ref[7 + NCOEF * ch : 7 + NCOEF * (ch + 1), :] = g[6 + ch] * basis
        d_basis = d_basis + g[6 + ch] * coef
    d_nx, d_ny, d_nz = basis_vjp(tuple(d_basis[i : i + 1, :] for i in range(NCOEF)))
    dot = d_nx * nx + d_ny * ny + d_nz * nz
    image_width = 1.0 * SIDE * IMG_TX
    d_u = g[0] + factor * (d_nx - nx * dot) / image_width
    d_v = g[1] + factor * (d_ny - ny * dot) / image_width
    d_one = g[2] * cc + g[3] * cs + g[4] * ss
    d_two = g[2] * ss - g[3] * cs + g[4] * cc
    diff = inv_one - inv_two
    d_angle = diff * (2.0 * cs * (g[4] - g[2]) + (cc - ss) * g[3])
    d_x = d_u * inv_z
    d_y = d_v * inv_z
    d_z = 2.0 * (d_one * inv_one + d_two * inv_two) * inv_z - d_x * screen_u - d_y * screen_v
    full_ref[0:1, :] = d_x
    full_ref[1:2, :] = d_y
    full_ref[2:3, :] = d_z
    full_ref[3:4, :] = -2.0 * inv_one * d_one
    full_ref[4:5, :] = -2.0 * inv_two * d_two
    full_ref[5:6, :] = d_angle
    full_ref[6:7, :] = g[5] / (1.0 + jnp.exp(p6))


def update_kernel(
    cam_ref, param_ref, first_ref, second_ref, grad_ref, *refs, step, project_next, pixel_count
):
    if project_next:
        new_param, new_first, new_second, field_ref, full_ref = refs
    else:
        before, (new_param, new_first, new_second, loss_ref, full_ref) = refs[:step], refs[step:]
        tail = grad_ref.shape[0] - ROWSUB
        for i, one in enumerate(before + (grad_ref,)):
            loss_ref[i] = jnp.max(one[tail : tail + 1, :]) / pixel_count
    gradient_to(param_ref, cam_ref[step, 0], cam_ref[step, 1], grad_ref, full_ref)
    step_count = adam_start + step + 1
    gradient = full_ref[...]
    first = beta_one * first_ref[...] + (1.0 - beta_one) * gradient
    second = beta_two * second_ref[...] + (1.0 - beta_two) * gradient * gradient
    scaled_first = first / (1.0 - beta_one**step_count)
    scaled_second = second / (1.0 - beta_two**step_count)
    new_first[...] = first
    new_second[...] = second
    new_param[...] = param_ref[...] - learn_rate * scaled_first / (
        jnp.sqrt(scaled_second) + adam_eps
    )
    if project_next:
        project_to(new_param, cam_ref[step + 1, 0], cam_ref[step + 1, 1], field_ref)


def split_two(values):
    high = values.astype(jnp.bfloat16)
    rest = (values - high.astype(jnp.float32)).astype(jnp.bfloat16)
    return high, rest


def pixel_basis(rows):
    pix = lax.broadcasted_iota(jnp.int32, (rows, SIDE * SIDE), 1)
    which = lax.broadcasted_iota(jnp.int32, (rows, SIDE * SIDE), 0)
    x = (pix % SIDE).astype(jnp.float32) + (0.5 - 0.5 * SIDE)
    y = (pix // SIDE).astype(jnp.float32) + (0.5 - 0.5 * SIDE)
    which = which % 8
    out = jnp.where(which == 0, 1.0, 0.0)
    for index, value in enumerate((x, y, x * x, x * y, y * y)):
        out = jnp.where(which == index + 1, value, out)
    return out


def dot_nn(a, b):
    return jnp.dot(a, b, preferred_element_type=jnp.float32)


def render_kernel(
    rows_ref,
    group_ref,
    middle_ref,
    target_ref,
    *refs,
    devices,
    per_owner,
    groups,
    depth,
    streams,
    step_index,
):
    table_parts, refs = refs[:PARTS], refs[PARTS:]
    picture_ref, refs = refs[0], refs[1:]
    grad_parts, refs = refs[:PARTS], refs[PARTS:]
    (
        fresh,
        placed,
        fields,
        factors,
        residual,
        across,
        w_high,
        w_rest,
        g_high,
        g_rest,
        sums,
        in_sem,
        out_sem,
        row_sem,
        *scratch,
    ) = refs
    planes_in = FIELDS * per_owner
    planes_out = planes_in + ROWSUB
    halves = per_owner // ROWSUB
    total = groups * ROWSUB * depth
    row_lists, scratch = scratch[:streams], scratch[streams:]
    blocks = depth * ROWSUB // LANES
    per_block = LANES // ROWSUB
    pixels = SIDE * SIDE
    wide = pixels // LANES
    near = devices // 2
    quarter = PARTS // 2
    part = near // quarter
    w_planes, a_planes, tables = scratch[:wide], scratch[wide : 2 * wide], scratch[2 * wide :]
    table = tables[0]

    loads = [
        pltpu.make_async_copy(
            ref,
            w_planes[i // quarter].at[pl.ds(i % quarter * part * planes_in, part * planes_in)],
            in_sem.at[i],
        )
        for i, ref in enumerate(table_parts)
    ]
    lists = [
        pltpu.make_async_copy(rows_ref.at[step_index, i], one, row_sem.at[i])
        for i, one in enumerate(row_lists)
    ]
    for copy in loads + lists:
        copy.start()

    pad = jnp.zeros((LANES - FIELDS * ROWSUB, LANES), jnp.float32)

    for side in range(2):
        for load in loads[side * quarter : (side + 1) * quarter]:
            load.wait()
        stage = w_planes[side]

        def build(owner, carry, stage=stage, side=side):
            start = pl.multiple_of(owner * planes_in, 8)
            for half in range(halves):
                parts = [
                    stage[pl.ds(start + f * per_owner + half * ROWSUB, ROWSUB), :]
                    for f in range(FIELDS)
                ]
                block = jnp.concatenate(parts + [pad], 0)
                at = pl.multiple_of(((side * near + owner) * halves + half) * LANES, LANES)
                table[pl.ds(at, LANES), :] = block.T
            return carry

        lax.fori_loop(0, near, build, 0, unroll=2)
    for copy in lists:
        copy.wait()

    turns = LANES // streams

    def gather(step):
        for group in range(groups):
            for turn in range(turns):
                place = (group * blocks + step) * turns + turn
                for q in range(streams):
                    at = group * LANES + turn * streams + q
                    fresh[at : at + 1, :] = table[pl.ds(row_lists[q][place], 1), :]

    def scatter(step):
        for group in range(groups):
            for turn in range(turns):
                place = (group * blocks + step) * turns + turn
                for q in range(streams):
                    at = group * LANES + turn * streams + q
                    one = tables[at % len(tables)]
                    row = pl.ds(row_lists[q][place], 1)
                    one[row, :] = one[row, :] + placed[at : at + 1, :]

    sub = lax.broadcasted_iota(jnp.int32, (ROWSUB, LANES), 0)
    lane = lax.broadcasted_iota(jnp.int32, (ROWSUB, LANES), 1)
    own_tile = sub == lane % ROWSUB
    basis_in = jnp.where(
        lax.broadcasted_iota(jnp.int32, (LANES, pixels), 0) < 24, pixel_basis(LANES), 0.0
    ).astype(jnp.bfloat16)
    lit = lax.broadcasted_iota(jnp.int32, (LANES, 3 * LANES), 0) - 32
    lit = jnp.where(lit < 0, -1, lit % 48)
    shown = lax.broadcasted_iota(jnp.int32, (LANES, 3 * LANES), 1) // LANES
    colour_in = jnp.where((lit >= 0) & (lit < 24) & (lit // ROWSUB == shown), 1.0, 0.0)
    colour_in = colour_in.astype(jnp.bfloat16)

    def field_mask(block):
        return sub == group_ref[step_index, pl.ds(block, 1), :]

    def prepare(block, group):
        at = pl.multiple_of(block * LANES, LANES)
        mask = field_mask(block)
        raw = fresh[group * LANES : (group + 1) * LANES, :].T
        rows = []
        for f in range(FIELDS):
            part = jnp.where(mask, raw[f * ROWSUB : (f + 1) * ROWSUB, :], 0.0)
            rows.append(jnp.sum(part, axis=0, keepdims=True))
        u = rows[0] - middle_ref[step_index, 2 * group : 2 * group + 1, :]
        v = rows[1] - middle_ref[step_index, 2 * group + 1 : 2 * group + 2, :]
        rows[0], rows[1] = u, v
        a, b, c = rows[2], rows[3], rows[4]
        for f in range(5):
            fields[pl.ds(block * ROWSUB + f, 1), :] = rows[f]
        au = a * u + b * v
        bv = b * u + c * v
        coefs = (
            LOG2E * (rows[5] - 0.5 * (u * au + v * bv)),
            LOG2E * au,
            LOG2E * bv,
            (-0.5 * LOG2E) * a,
            -LOG2E * b,
            (-0.5 * LOG2E) * c,
        )
        coef = jnp.zeros((ROWSUB, LANES), jnp.float32)
        for i, row in enumerate(coefs):
            coef = jnp.where(sub == i, row, coef)
        high = coef.astype(jnp.bfloat16).astype(jnp.float32)
        rest = coef - high
        mid = rest.astype(jnp.bfloat16).astype(jnp.float32)
        low = rest - mid
        full = [jnp.where(own_tile, rows[6 + ch], 0.0) for ch in range(3)]
        c_high = [part.astype(jnp.bfloat16).astype(jnp.float32) for part in full]
        c_rest = [part - top for part, top in zip(full, c_high)]
        stacked = jnp.concatenate(
            [high, mid, low, jnp.zeros_like(low)] + c_high + c_high + c_rest + c_rest, 0
        )
        factors[pl.ds(at, LANES), :] = stacked.T.astype(jnp.bfloat16)

    def store_split(high_ref, rest_ref, at, values):
        for h in range(wide):
            high, rest = split_two(jnp.concatenate(values[h], 0))
            span = pl.ds(at, high.shape[0])
            high_ref[span, h * LANES : (h + 1) * LANES] = high
            rest_ref[span, h * LANES : (h + 1) * LANES] = rest

    gather(0)
    for group in range(groups):
        prepare(group * blocks, group)
    gather(min(1, blocks - 1))

    def forward(step, carry):
        out = []
        for group in range(groups):
            at = pl.multiple_of((group * blocks + step) * LANES, LANES)
            left = factors[pl.ds(at, LANES), :]
            exponent = dot_nn(left, basis_in)
            tones = dot_nn(left, colour_in)
            trans, sums = list(carry[group][0]), [list(x) for x in carry[group][1]]
            kept = [[] for _ in range(wide)]
            for s in range(per_block):
                span = pl.ds(at + s * ROWSUB, ROWSUB)
                tone = tones[s * ROWSUB : (s + 1) * ROWSUB, :]
                for h in range(wide):
                    e = exponent[s * ROWSUB : (s + 1) * ROWSUB, h * LANES : (h + 1) * LANES]
                    alpha = jnp.exp2(jnp.minimum(e, LOG2E * LOG_CAP))
                    w = trans[h] * alpha
                    trans[h] = trans[h] - w
                    a_planes[h][span, :] = alpha
                    w_planes[h][span, :] = w
                    for ch in range(3):
                        sums[ch][h] = sums[ch][h] + w * tone[:, ch * LANES : (ch + 1) * LANES]
                    kept[h].append(w)
                if s % 2:
                    where = pl.multiple_of(at + (s - 1) * ROWSUB, 2 * ROWSUB)
                    store_split(w_high, w_rest, where, kept)
                    kept = [[] for _ in range(wide)]
            out.append((tuple(trans), tuple(tuple(x) for x in sums)))
        ahead = jnp.minimum(step + 1, blocks - 1)
        for group in range(groups):
            prepare(group * blocks + ahead, group)
        gather(jnp.minimum(step + 2, blocks - 1))
        return tuple(out)

    ones = jnp.ones((ROWSUB, LANES), jnp.float32)
    zeros = jnp.zeros((ROWSUB, LANES), jnp.float32)
    begin = (tuple(ones for _ in range(wide)), tuple((zeros,) * wide for _ in range(3)))
    done = lax.fori_loop(0, blocks, forward, (begin,) * groups)

    loss = jnp.zeros((1, 1), jnp.float32)
    for group in range(groups):
        parts = []
        for ch in range(3):
            pair = []
            for h in range(wide):
                where = pl.ds((group * ROWSUB * 3 + ch) * wide + h, ROWSUB, stride=3 * wide)
                shade = done[group][1][ch][h]
                picture_ref[where, :] = shade
                pair.append(shade - target_ref[step_index, where, :])
            parts.append(jnp.concatenate(pair, 1))
        left = jnp.concatenate(parts, 0)
        square = left * left
        loss = loss + 0.5 * jnp.sum(
            jnp.sum(square, axis=0, keepdims=True), axis=1, keepdims=True
        )
        high = left.astype(jnp.bfloat16).astype(jnp.float32)
        rest = left - high
        none = jnp.zeros((32, pixels), jnp.float32)
        stacked = jnp.concatenate([none, high, rest, high, rest], 0)
        residual[group] = stacked.astype(jnp.bfloat16)
        stacked = jnp.concatenate([none, high, rest, jnp.zeros((48, pixels), jnp.float32)], 0)
        across[group] = stacked.T.astype(jnp.bfloat16)
    basis_out = jnp.where(
        lax.broadcasted_iota(jnp.int32, (LANES, pixels), 0) < 8, pixel_basis(LANES), 0.0
    )
    across[groups] = basis_out.T.astype(jnp.bfloat16)

    def sum_slopes(step):
        both = [g_high[group] for group in range(groups)]
        both += [g_rest[group] for group in range(groups)]
        shape_sums = dot_nn(jnp.concatenate(both, 0), across[groups])
        for group in range(groups):
            span = pl.ds(pl.multiple_of((group * blocks + step) * LANES, LANES), LANES)
            tone_sums = dot_nn(
                jnp.concatenate([w_high[span, :], w_rest[span, :]], 0), across[group]
            )
            first, second = group * LANES, (groups + group) * LANES
            sums[group] = (
                shape_sums[first : first + LANES]
                + shape_sums[second : second + LANES]
                + tone_sums[:LANES]
                + tone_sums[LANES:]
            ).T

    def place_slopes(step, skip):
        for group in range(groups):
            block = group * blocks + step
            mask = sub == group_ref[step_index, pl.ds(block, 1), :] + skip
            m = [sums[group, i : i + 1, :] for i in range(6)]
            u, v, a, b, c = [fields[pl.ds(block * ROWSUB + f, 1), :] for f in range(5)]
            m_x = m[1] - u * m[0]
            m_y = m[2] - v * m[0]
            rows = [
                a * m_x + b * m_y,
                b * m_x + c * m_y,
                -0.5 * (m[3] - u * (m[1] + m_x)),
                -(m[4] - u * m[2] - v * m_x),
                -0.5 * (m[5] - v * (m[2] + m_y)),
                m[0],
            ]
            for ch in range(3):
                low = 32 + ch * ROWSUB
                tint = (
                    sums[group, low : low + ROWSUB, :]
                    + sums[group, low + 24 : low + 24 + ROWSUB, :]
                )
                rows.append(jnp.sum(jnp.where(own_tile, tint, 0.0), axis=0, keepdims=True))
            rows = [jnp.where(mask, row, 0.0) for row in rows] + [pad]
            placed[group * LANES : (group + 1) * LANES, :] = jnp.concatenate(rows, 0).T

    tall = jnp.zeros((LANES, LANES), jnp.float32)
    for group in range(groups):
        placed[group * LANES : (group + 1) * LANES, :] = tall

    def clear(index, carry):
        at = pl.multiple_of(index * LANES, LANES)
        for one in tables:
            one[pl.ds(at, LANES), :] = tall
        return carry

    lax.fori_loop(0, devices * halves, clear, 0)

    def backward(index, carry):
        newest = blocks - 1 - index
        later = [jnp.clip(newest + i, 0, blocks - 1) for i in range(4)]
        step = later[0]
        scatter(later[3])
        place_slopes(later[2], jnp.where(newest + 2 < blocks, 0, ROWSUB))
        sum_slopes(later[1])
        out = []
        for group in range(groups):
            at = pl.multiple_of((group * blocks + step) * LANES, LANES)
            q = dot_nn(factors[pl.ds(at, LANES), :], residual[group])
            behind = list(carry[group])
            kept = [[] for _ in range(wide)]
            for s in reversed(range(per_block)):
                span = pl.ds(at + s * ROWSUB, ROWSUB)
                for h in range(wide):
                    w = w_planes[h][span, :]
                    alpha = a_planes[h][span, :]
                    d = q[s * ROWSUB : (s + 1) * ROWSUB, h * LANES : (h + 1) * LANES] - behind[h]
                    kept[h].insert(0, w * d)
                    behind[h] = behind[h] + alpha * d
                if s % 2 == 0:
                    store_split(g_high.at[group], g_rest.at[group], s * ROWSUB, kept)
                    kept = [[] for _ in range(wide)]
            out.append(tuple(behind))
        return tuple(out)

    lax.fori_loop(0, blocks + 3, backward, ((zeros,) * wide,) * groups)

    loss_rows = jnp.broadcast_to(loss, (ROWSUB, LANES))
    stores = []
    for side, skip in ((1, 0), (1, near // 2), (0, 0), (0, near // 2)):
        stage = w_planes[side]

        def collect(owner, carry, side=side, stage=stage):
            start = pl.multiple_of(owner * planes_out, 8)
            turned = []
            for half in range(halves):
                at = pl.multiple_of(((side * near + owner) * halves + half) * LANES, LANES)
                block = tables[0][pl.ds(at, LANES), :]
                for one in tables[1:]:
                    block = block + one[pl.ds(at, LANES), :]
                turned.append(block.T)
            for half in range(halves):
                for f in range(FIELDS):
                    stage[pl.ds(start + f * per_owner + half * ROWSUB, ROWSUB), :] = turned[
                        half
                    ][f * ROWSUB : (f + 1) * ROWSUB, :]
            stage[pl.ds(start + planes_in, ROWSUB), :] = loss_rows
            return carry

        lax.fori_loop(skip, skip + near // 2, collect, 0)
        for first in range(skip, skip + near // 2, part):
            index = side * quarter + first // part
            store = pltpu.make_async_copy(
                stage.at[pl.ds(first * planes_out, part * planes_out)],
                grad_parts[index],
                out_sem.at[index],
            )
            store.start()
            stores.append(store)
    for store in stores:
        store.wait()


def exchange_flips(gy_size):
    bits = list(range(1, gy_size.bit_length() - 1))
    cut = (len(bits) + 1) // 2
    low, high = bits[:cut], bits[cut:]
    return list(zip(low + high, high + low))


def swap(values, devices, even, odd=None):
    flips = (even, even if odd is None else odd)
    pairs = [(i, i ^ flips[i & 1]) for i in range(devices)]
    return lax.ppermute(values, AXES, pairs)


def spread(values, gx_size, gy_size, hold):
    devices = gx_size * gy_size
    order = exchange_flips(gy_size)
    blocks = [values] + [swap(values, devices, z * gy_size) for z in range(1, gx_size)]
    own, other = [], []
    for chunk in range(2):
        values = jnp.concatenate(blocks[chunk * gx_size // 2 : (chunk + 1) * gx_size // 2], 0)
        if chunk == 0:
            values, hold = lax.optimization_barrier((values, hold))
        for even, odd in order[:-1]:
            values = jnp.concatenate([values, swap(values, devices, 1 << even, 1 << odd)], 0)
        even, odd = order[-1]
        last = swap(values, devices, 1 << even, 1 << odd)
        own += [values, last]
        other += [swap(values, devices, 1), swap(last, devices, 1)]
    return own + other, hold


def fold(parts, gx_size, gy_size):
    devices = gx_size * gy_size
    order = exchange_flips(gy_size)
    own, other = parts[: PARTS // 2], parts[PARTS // 2 :]
    chunks = [None, None]
    for chunk in (1, 0):
        high = own[2 * chunk + 1] + swap(other[2 * chunk + 1], devices, 1)
        low = own[2 * chunk] + swap(other[2 * chunk], devices, 1)
        even, odd = order[-1]
        values = low + swap(high, devices, 1 << even, 1 << odd)
        for even, odd in reversed(order[:-1]):
            half = values.shape[0] // 2
            values = values[:half] + swap(values[half:], devices, 1 << even, 1 << odd)
        chunks[chunk] = values
    size = 2 * chunks[0].shape[0] // gx_size
    total = chunks[0][:size]
    for z in range(1, gx_size):
        at = z % (gx_size // 2) * size
        block = chunks[z // (gx_size // 2)][at : at + size]
        total = total + swap(block, devices, z * gy_size)
    return total


def per_device(gauss_params, first_moment, second_moment, splat_lists, tile_ids, targets, camera):
    gx_size = lax.axis_size("gx")
    gy_size = lax.axis_size("gy")
    devices = gx_size * gy_size
    params_rows, count = gauss_params.shape
    tiles, depth = splat_lists.shape[1:]
    per_owner = count // LANES
    groups = tiles // ROWSUB
    planes_in = FIELDS * per_owner
    planes_out = planes_in + ROWSUB
    total = tiles * depth
    pixels = SIDE * SIDE

    me = lax.axis_index("gx") * gy_size + lax.axis_index("gy")
    owner = splat_lists // count
    apart = owner ^ me
    local = splat_lists % count
    lows = gx_size // 2
    apart_gx = apart // gy_size
    place = (apart & 1) * (devices // 2) + apart_gx // lows * (devices // 4) + apart_gx % lows
    for bit, (even, odd) in enumerate(exchange_flips(gy_size)):
        taken = jnp.where(owner & 1 == 0, apart >> even, apart >> odd)
        place = place + (taken & 1) * (lows << bit)
    rows = place * (count // ROWSUB) + (local // (ROWSUB * LANES)) * LANES + local % LANES
    which = (local // LANES) % ROWSUB

    def interleave(values):
        return (
            values.reshape(STEPS, groups, ROWSUB, depth)
            .transpose(0, 1, 3, 2)
            .reshape(STEPS, total)
        )

    rows = interleave(rows).reshape(STEPS, total // 16, 16).transpose(0, 2, 1)
    which = interleave(which).reshape(STEPS, total // LANES, LANES)
    middle_x = (tile_ids % IMG_TX * SIDE + SIDE // 2).astype(jnp.float32)
    middle_y = (tile_ids // IMG_TX * SIDE + SIDE // 2).astype(jnp.float32)
    middle = jnp.stack([middle_x, middle_y], 1).reshape(STEPS, 2, groups, ROWSUB)
    middle = middle.transpose(0, 2, 1, 3).reshape(STEPS, 2 * groups, ROWSUB)
    middle = jnp.tile(middle, (1, 1, LANES // ROWSUB))
    target_rows = targets.reshape(STEPS, tiles * 3 * pixels // LANES, LANES)

    vmem = pl.BlockSpec(memory_space=pltpu.VMEM)
    smem = pl.BlockSpec(memory_space=pltpu.SMEM)
    hbm = pl.BlockSpec(memory_space=pl.ANY)
    f32, bf16 = jnp.float32, jnp.bfloat16
    state = jax.ShapeDtypeStruct((params_rows, count), f32)
    field_shape = jax.ShapeDtypeStruct((planes_in, LANES), f32)

    streams = 16
    wide = pixels // LANES
    table_rows = devices * count // ROWSUB
    plane_rows = max(total, devices // 2 * planes_out)
    copies = max(1, min(6, (26 << 20) // (table_rows * LANES * 4)))
    render = functools.partial(
        pl.pallas_call,
        out_shape=(jax.ShapeDtypeStruct((tiles * 3 * pixels // LANES, LANES), f32),)
        + (jax.ShapeDtypeStruct((devices // PARTS * planes_out, LANES), f32),) * PARTS,
        in_specs=[hbm, vmem, vmem, vmem] + [hbm] * PARTS,
        out_specs=(vmem,) + (hbm,) * PARTS,
        scratch_shapes=[
            pltpu.VMEM((groups * LANES, LANES), f32),
            pltpu.VMEM((groups * LANES, LANES), f32),
            pltpu.VMEM((total // LANES * ROWSUB, LANES), f32),
            pltpu.VMEM((total, LANES), bf16),
            pltpu.VMEM((groups, LANES, pixels), bf16),
            pltpu.VMEM((groups + 1, pixels, LANES), bf16),
            pltpu.VMEM((total, pixels), bf16),
            pltpu.VMEM((total, pixels), bf16),
            pltpu.VMEM((groups, LANES, pixels), bf16),
            pltpu.VMEM((groups, LANES, pixels), bf16),
            pltpu.VMEM((groups, LANES, LANES), f32),
            pltpu.SemaphoreType.DMA((PARTS,)),
            pltpu.SemaphoreType.DMA((PARTS,)),
            pltpu.SemaphoreType.DMA((streams,)),
        ]
        + [pltpu.SMEM((total // streams,), jnp.int32)] * streams
        + [pltpu.VMEM((plane_rows, LANES), f32)] * (2 * wide)
        + [pltpu.VMEM((table_rows, LANES), f32)] * copies,
        compiler_params=pltpu.CompilerParams(vmem_limit_bytes=60 << 20),
        name="render",
    )

    params, first, second = gauss_params, first_moment, second_moment
    fields = pl.pallas_call(
        functools.partial(project_kernel, step=0),
        out_shape=field_shape,
        in_specs=[smem, vmem],
        out_specs=vmem,
        name="project",
    )(camera, params)
    settings = (rows, which, middle, target_rows)
    pictures = []
    sums = []
    for step in range(STEPS):
        kernel = functools.partial(
            render_kernel,
            devices=devices,
            per_owner=per_owner,
            groups=groups,
            depth=depth,
            streams=streams,
            step_index=step,
        )
        table, settings = spread(fields, gx_size, gy_size, settings)
        picture, *grads = render(kernel)(*settings, *table)
        pictures.append(picture)
        summed = fold(grads, gx_size, gy_size)
        sums.append(summed)
        more = step + 1 < STEPS
        before = [] if more else sums[:-1]
        result = pl.pallas_call(
            functools.partial(
                update_kernel,
                step=step,
                project_next=more,
                pixel_count=3.0 * pixels * tiles * devices,
            ),
            out_shape=(state, state, state)
            + (field_shape if more else jax.ShapeDtypeStruct((STEPS,), f32),),
            in_specs=[smem] + [vmem] * (4 + len(before)),
            out_specs=(vmem,) * 3 + (vmem if more else smem,),
            scratch_shapes=[pltpu.VMEM((params_rows, count), f32)],
            name="update",
        )(camera, params, first, second, summed, *before)
        params, first, second, fields = result
    rendered = jnp.stack(pictures).reshape(STEPS, tiles, 3, pixels)
    return params, first, second, rendered, fields


def solution(mesh):
    along = P(None, AXES)
    lists = P(None, AXES, None)
    frames = P(None, AXES, None, None)
    return jax.shard_map(
        per_device,
        mesh=mesh,
        in_specs=(along, along, along, lists, along, frames, P()),
        out_specs=(along, along, along, frames, P()),
        check_vma=False,
    )
```

```python
import functools

import jax
import jax.numpy as jnp
from jax import lax
from jax.experimental import pallas as pl
from jax.experimental.pallas import tpu as pltpu
from jax.sharding import PartitionSpec as P

SIDE = 16
NCOEF = 16
STEPS = 2
IMG_TX = 64
IMG_TY = 32

FIELDS = 9
LANES = 128
ROWSUB = 8
PARTS = 8
AXES = ("gx", "gy")

beta_one = 0.9
beta_two = 0.999
adam_eps = 1e-08
learn_rate = 0.01
adam_start = 1000
band_zero = 0.28209479177387814
band_one = 0.4886025119029199
band_two = (
    1.0925484305920792,
    -1.0925484305920792,
    0.31539156525252005,
    -1.0925484305920792,
    0.5462742152960396,
)
band_three = (
    -0.5900435899266435,
    2.890611442640554,
    -0.4570457994644658,
    0.3731763325901154,
    -0.4570457994644658,
    1.445305721320277,
    -0.5900435899266435,
)
LOG2E = 1.4426950408889634
LOG_CAP = -0.01005033585350145


def harmonic_rows(ray_x, ray_y, ray_z):
    sq_x = ray_x * ray_x
    sq_y = ray_y * ray_y
    sq_z = ray_z * ray_z
    return [
        band_zero * jnp.ones_like(ray_x),
        -band_one * ray_y,
        band_one * ray_z,
        -band_one * ray_x,
        band_two[0] * ray_x * ray_y,
        band_two[1] * ray_y * ray_z,
        band_two[2] * (2.0 * sq_z - sq_x - sq_y),
        band_two[3] * ray_x * ray_z,
        band_two[4] * (sq_x - sq_y),
        band_three[0] * ray_y * (3.0 * sq_x - sq_y),
        band_three[1] * ray_x * ray_y * ray_z,
        band_three[2] * ray_y * (4.0 * sq_z - sq_x - sq_y),
        band_three[3] * ray_z * (2.0 * sq_z - 3.0 * sq_x - 3.0 * sq_y),
        band_three[4] * ray_x * (4.0 * sq_z - sq_x - sq_y),
        band_three[5] * ray_z * (sq_x - sq_y),
        band_three[6] * ray_x * (sq_x - 3.0 * sq_y),
    ]


def geometry_rows(p0, p1, p2, p3, p4, p5, p6, cam_x, cam_y):
    screen_u = (p0 - cam_x) / p2
    screen_v = (p1 - cam_y) / p2
    inv_one = p2 * p2 * jnp.exp(-2.0 * p3)
    inv_two = p2 * p2 * jnp.exp(-2.0 * p4)
    cosine = jnp.cos(p5)
    sine = jnp.sin(p5)
    conic_a = cosine * cosine * inv_one + sine * sine * inv_two
    conic_b = cosine * sine * (inv_one - inv_two)
    conic_c = sine * sine * inv_one + cosine * cosine * inv_two
    tail = jnp.log(1.0 + jnp.exp(-jnp.abs(p6)))
    log_opacity = LOG_CAP - (jnp.maximum(-p6, 0.0) + tail)
    return screen_u, screen_v, conic_a, conic_b, conic_c, log_opacity


def ray_rows(screen_u, screen_v):
    image_width = 1.0 * SIDE * IMG_TX
    image_height = 1.0 * SIDE * IMG_TY
    ray_x = (screen_u - 0.5 * image_width) / image_width
    ray_y = (screen_v - 0.5 * image_height) / image_width
    factor = lax.rsqrt(ray_x * ray_x + ray_y * ray_y + 1.0)
    return ray_x, ray_y, factor


def project_to(param_ref, cam_x, cam_y, out_ref):
    rows = [param_ref[i : i + 1, :] for i in range(7)]
    geo = geometry_rows(*rows, cam_x, cam_y)
    ray_x, ray_y, factor = ray_rows(geo[0], geo[1])
    basis = jnp.concatenate(harmonic_rows(ray_x * factor, ray_y * factor, factor), 0)
    colours = []
    for ch in range(3):
        coef = param_ref[7 + NCOEF * ch : 7 + NCOEF * (ch + 1), :]
        colours.append(0.5 + jnp.sum(coef * basis, axis=0, keepdims=True))
    fields = jnp.concatenate(list(geo) + colours, 0)
    per_field = fields.shape[1] // LANES
    for k in range(per_field):
        out_ref[pl.ds(k, FIELDS, stride=per_field), :] = fields[:, k * LANES : (k + 1) * LANES]


def project_kernel(cam_ref, param_ref, out_ref, *, step):
    project_to(param_ref, cam_ref[step, 0], cam_ref[step, 1], out_ref)


def gradient_to(param_ref, cam_x, cam_y, grad_ref, full_ref):
    count = param_ref.shape[1]
    per_field = count // LANES
    pieces = [grad_ref[pl.ds(k, FIELDS, stride=per_field), :] for k in range(per_field)]
    grads = jnp.concatenate(pieces, 1)
    g = [grads[i : i + 1, :] for i in range(FIELDS)]
    p0, p1, p2, p3, p4, p5, p6 = [param_ref[i : i + 1, :] for i in range(7)]
    inv_z = 1.0 / p2
    screen_u = (p0 - cam_x) / p2
    screen_v = (p1 - cam_y) / p2
    inv_one = p2 * p2 * jnp.exp(-2.0 * p3)
    inv_two = p2 * p2 * jnp.exp(-2.0 * p4)
    cosine = jnp.cos(p5)
    sine = jnp.sin(p5)
    cc = cosine * cosine
    ss = sine * sine
    cs = cosine * sine
    ray_x, ray_y, factor = ray_rows(screen_u, screen_v)
    nx, ny, nz = ray_x * factor, ray_y * factor, factor
    basis_rows, basis_vjp = jax.vjp(lambda a, b, c: tuple(harmonic_rows(a, b, c)), nx, ny, nz)
    basis = jnp.concatenate(basis_rows, 0)
    d_basis = jnp.zeros_like(basis)
    for ch in range(3):
        coef = param_ref[7 + NCOEF * ch : 7 + NCOEF * (ch + 1), :]
        full_ref[7 + NCOEF * ch : 7 + NCOEF * (ch + 1), :] = g[6 + ch] * basis
        d_basis = d_basis + g[6 + ch] * coef
    d_nx, d_ny, d_nz = basis_vjp(tuple(d_basis[i : i + 1, :] for i in range(NCOEF)))
    dot = d_nx * nx + d_ny * ny + d_nz * nz
    image_width = 1.0 * SIDE * IMG_TX
    d_u = g[0] + factor * (d_nx - nx * dot) / image_width
    d_v = g[1] + factor * (d_ny - ny * dot) / image_width
    d_one = g[2] * cc + g[3] * cs + g[4] * ss
    d_two = g[2] * ss - g[3] * cs + g[4] * cc
    diff = inv_one - inv_two
    d_angle = diff * (2.0 * cs * (g[4] - g[2]) + (cc - ss) * g[3])
    d_x = d_u * inv_z
    d_y = d_v * inv_z
    d_z = 2.0 * (d_one * inv_one + d_two * inv_two) * inv_z - d_x * screen_u - d_y * screen_v
    full_ref[0:1, :] = d_x
    full_ref[1:2, :] = d_y
    full_ref[2:3, :] = d_z
    full_ref[3:4, :] = -2.0 * inv_one * d_one
    full_ref[4:5, :] = -2.0 * inv_two * d_two
    full_ref[5:6, :] = d_angle
    full_ref[6:7, :] = g[5] / (1.0 + jnp.exp(p6))


def update_kernel(
    cam_ref, param_ref, first_ref, second_ref, grad_ref, *refs, step, project_next, pixel_count
):
    if project_next:
        new_param, new_first, new_second, field_ref, full_ref = refs
    else:
        before, (new_param, new_first, new_second, loss_ref, full_ref) = refs[:step], refs[step:]
        tail = grad_ref.shape[0] - ROWSUB
        for i, one in enumerate(before + (grad_ref,)):
            loss_ref[i] = jnp.max(one[tail : tail + 1, :]) / pixel_count
    gradient_to(param_ref, cam_ref[step, 0], cam_ref[step, 1], grad_ref, full_ref)
    step_count = adam_start + step + 1
    gradient = full_ref[...]
    first = beta_one * first_ref[...] + (1.0 - beta_one) * gradient
    second = beta_two * second_ref[...] + (1.0 - beta_two) * gradient * gradient
    scaled_first = first / (1.0 - beta_one**step_count)
    scaled_second = second / (1.0 - beta_two**step_count)
    new_first[...] = first
    new_second[...] = second
    new_param[...] = param_ref[...] - learn_rate * scaled_first / (
        jnp.sqrt(scaled_second) + adam_eps
    )
    if project_next:
        project_to(new_param, cam_ref[step + 1, 0], cam_ref[step + 1, 1], field_ref)


def split_two(values):
    high = values.astype(jnp.bfloat16)
    rest = (values - high.astype(jnp.float32)).astype(jnp.bfloat16)
    return high, rest


def pixel_basis(rows):
    pix = lax.broadcasted_iota(jnp.int32, (rows, SIDE * SIDE), 1)
    which = lax.broadcasted_iota(jnp.int32, (rows, SIDE * SIDE), 0)
    x = (pix % SIDE).astype(jnp.float32) + (0.5 - 0.5 * SIDE)
    y = (pix // SIDE).astype(jnp.float32) + (0.5 - 0.5 * SIDE)
    which = which % 8
    out = jnp.where(which == 0, 1.0, 0.0)
    for index, value in enumerate((x, y, x * x, x * y, y * y)):
        out = jnp.where(which == index + 1, value, out)
    return out


def dot_nn(a, b):
    return jnp.dot(a, b, preferred_element_type=jnp.float32)


def render_kernel(
    rows_ref,
    group_ref,
    middle_ref,
    target_ref,
    *refs,
    devices,
    per_owner,
    groups,
    depth,
    streams,
    step_index,
):
    table_parts, refs = refs[:PARTS], refs[PARTS:]
    picture_ref, refs = refs[0], refs[1:]
    grad_parts, refs = refs[:PARTS], refs[PARTS:]
    (
        fresh,
        placed,
        fields,
        factors,
        residual,
        across,
        w_high,
        w_rest,
        g_high,
        g_rest,
        sums,
        in_sem,
        out_sem,
        row_sem,
        *scratch,
    ) = refs
    planes_in = FIELDS * per_owner
    planes_out = planes_in + ROWSUB
    halves = per_owner // ROWSUB
    total = groups * ROWSUB * depth
    row_lists, scratch = scratch[:streams], scratch[streams:]
    blocks = depth * ROWSUB // LANES
    per_block = LANES // ROWSUB
    pixels = SIDE * SIDE
    wide = pixels // LANES
    near = devices // 2
    quarter = PARTS // 2
    part = near // quarter
    w_planes, a_planes, tables = scratch[:wide], scratch[wide : 2 * wide], scratch[2 * wide :]
    table = tables[0]

    loads = [
        pltpu.make_async_copy(
            ref,
            w_planes[i // quarter].at[pl.ds(i % quarter * part * planes_in, part * planes_in)],
            in_sem.at[i],
        )
        for i, ref in enumerate(table_parts)
    ]
    lists = [
        pltpu.make_async_copy(rows_ref.at[step_index, i], one, row_sem.at[i])
        for i, one in enumerate(row_lists)
    ]
    for copy in loads + lists:
        copy.start()

    tall = jnp.zeros((LANES, LANES), jnp.float32)

    def clear(some, index, carry):
        at = pl.multiple_of(index * LANES, LANES)
        for one in some:
            one[pl.ds(at, LANES), :] = tall
        return carry

    lax.fori_loop(0, devices * halves, functools.partial(clear, tables[1:]), 0)

    pad = jnp.zeros((LANES - FIELDS * ROWSUB, LANES), jnp.float32)

    for side in range(2):
        for load in loads[side * quarter : (side + 1) * quarter]:
            load.wait()
        stage = w_planes[side]

        def build(owner, carry, stage=stage, side=side):
            start = pl.multiple_of(owner * planes_in, 8)
            for half in range(halves):
                parts = [
                    stage[pl.ds(start + f * per_owner + half * ROWSUB, ROWSUB), :]
                    for f in range(FIELDS)
                ]
                block = jnp.concatenate(parts + [pad], 0)
                at = pl.multiple_of(((side * near + owner) * halves + half) * LANES, LANES)
                table[pl.ds(at, LANES), :] = block.T
            return carry

        lax.fori_loop(0, near, build, 0, unroll=2)
    for copy in lists:
        copy.wait()

    turns = LANES // streams

    def gather(step):
        for group in range(groups):
            for turn in range(turns):
                place = (group * blocks + step) * turns + turn
                for q in range(streams):
                    at = group * LANES + turn * streams + q
                    fresh[at : at + 1, :] = table[pl.ds(row_lists[q][place], 1), :]

    def scatter(step):
        for group in range(groups):
            for turn in range(turns):
                place = (group * blocks + step) * turns + turn
                for q in range(streams):
                    at = group * LANES + turn * streams + q
                    one = tables[at % len(tables)]
                    row = pl.ds(row_lists[q][place], 1)
                    one[row, :] = one[row, :] + placed[at : at + 1, :]

    sub = lax.broadcasted_iota(jnp.int32, (ROWSUB, LANES), 0)
    lane = lax.broadcasted_iota(jnp.int32, (ROWSUB, LANES), 1)
    own_tile = sub == lane % ROWSUB
    basis_in = jnp.where(
        lax.broadcasted_iota(jnp.int32, (LANES, pixels), 0) < 24, pixel_basis(LANES), 0.0
    ).astype(jnp.bfloat16)
    lit = lax.broadcasted_iota(jnp.int32, (LANES, 3 * LANES), 0) - 32
    lit = jnp.where(lit < 0, -1, lit % 48)
    shown = lax.broadcasted_iota(jnp.int32, (LANES, 3 * LANES), 1) // LANES
    colour_in = jnp.where((lit >= 0) & (lit < 24) & (lit // ROWSUB == shown), 1.0, 0.0)
    colour_in = colour_in.astype(jnp.bfloat16)

    def field_mask(block):
        return sub == group_ref[step_index, pl.ds(block, 1), :]

    def prepare(block, group):
        at = pl.multiple_of(block * LANES, LANES)
        mask = field_mask(block)
        raw = fresh[group * LANES : (group + 1) * LANES, :].T
        rows = []
        for f in range(FIELDS):
            part = jnp.where(mask, raw[f * ROWSUB : (f + 1) * ROWSUB, :], 0.0)
            rows.append(jnp.sum(part, axis=0, keepdims=True))
        u = rows[0] - middle_ref[step_index, 2 * group : 2 * group + 1, :]
        v = rows[1] - middle_ref[step_index, 2 * group + 1 : 2 * group + 2, :]
        rows[0], rows[1] = u, v
        a, b, c = rows[2], rows[3], rows[4]
        for f in range(5):
            fields[pl.ds(block * ROWSUB + f, 1), :] = rows[f]
        au = a * u + b * v
        bv = b * u + c * v
        coefs = (
            LOG2E * (rows[5] - 0.5 * (u * au + v * bv)),
            LOG2E * au,
            LOG2E * bv,
            (-0.5 * LOG2E) * a,
            -LOG2E * b,
            (-0.5 * LOG2E) * c,
        )
        coef = jnp.zeros((ROWSUB, LANES), jnp.float32)
        for i, row in enumerate(coefs):
            coef = jnp.where(sub == i, row, coef)
        high = coef.astype(jnp.bfloat16).astype(jnp.float32)
        rest = coef - high
        mid = rest.astype(jnp.bfloat16).astype(jnp.float32)
        low = rest - mid
        full = [jnp.where(own_tile, rows[6 + ch], 0.0) for ch in range(3)]
        c_high = [part.astype(jnp.bfloat16).astype(jnp.float32) for part in full]
        c_rest = [part - top for part, top in zip(full, c_high)]
        stacked = jnp.concatenate(
            [high, mid, low, jnp.zeros_like(low)] + c_high + c_high + c_rest + c_rest, 0
        )
        factors[pl.ds(at, LANES), :] = stacked.T.astype(jnp.bfloat16)

    def store_split(high_ref, rest_ref, at, values):
        for h in range(wide):
            high, rest = split_two(jnp.concatenate(values[h], 0))
            span = pl.ds(at, high.shape[0])
            high_ref[span, h * LANES : (h + 1) * LANES] = high
            rest_ref[span, h * LANES : (h + 1) * LANES] = rest

    gather(0)
    for group in range(groups):
        prepare(group * blocks, group)
    gather(min(1, blocks - 1))

    def forward(step, carry):
        out = []
        for group in range(groups):
            at = pl.multiple_of((group * blocks + step) * LANES, LANES)
            left = factors[pl.ds(at, LANES), :]
            exponent = dot_nn(left, basis_in)
            tones = dot_nn(left, colour_in)
            trans, sums = list(carry[group][0]), [list(x) for x in carry[group][1]]
            kept = [[] for _ in range(wide)]
            for s in range(per_block):
                span = pl.ds(at + s * ROWSUB, ROWSUB)
                tone = tones[s * ROWSUB : (s + 1) * ROWSUB, :]
                for h in range(wide):
                    e = exponent[s * ROWSUB : (s + 1) * ROWSUB, h * LANES : (h + 1) * LANES]
                    alpha = jnp.exp2(jnp.minimum(e, LOG2E * LOG_CAP))
                    w = trans[h] * alpha
                    trans[h] = trans[h] - w
                    a_planes[h][span, :] = alpha
                    w_planes[h][span, :] = w
                    for ch in range(3):
                        sums[ch][h] = sums[ch][h] + w * tone[:, ch * LANES : (ch + 1) * LANES]
                    kept[h].append(w)
                if s % 2:
                    where = pl.multiple_of(at + (s - 1) * ROWSUB, 2 * ROWSUB)
                    store_split(w_high, w_rest, where, kept)
                    kept = [[] for _ in range(wide)]
            out.append((tuple(trans), tuple(tuple(x) for x in sums)))
        ahead = jnp.minimum(step + 1, blocks - 1)
        for group in range(groups):
            prepare(group * blocks + ahead, group)
        gather(jnp.minimum(step + 2, blocks - 1))
        return tuple(out)

    ones = jnp.ones((ROWSUB, LANES), jnp.float32)
    zeros = jnp.zeros((ROWSUB, LANES), jnp.float32)
    begin = (tuple(ones for _ in range(wide)), tuple((zeros,) * wide for _ in range(3)))
    done = lax.fori_loop(0, blocks, forward, (begin,) * groups)

    loss = jnp.zeros((1, 1), jnp.float32)
    for group in range(groups):
        parts = []
        for ch in range(3):
            pair = []
            for h in range(wide):
                where = pl.ds((group * ROWSUB * 3 + ch) * wide + h, ROWSUB, stride=3 * wide)
                shade = done[group][1][ch][h]
                picture_ref[where, :] = shade
                pair.append(shade - target_ref[step_index, where, :])
            parts.append(jnp.concatenate(pair, 1))
        left = jnp.concatenate(parts, 0)
        square = left * left
        loss = loss + 0.5 * jnp.sum(
            jnp.sum(square, axis=0, keepdims=True), axis=1, keepdims=True
        )
        high = left.astype(jnp.bfloat16).astype(jnp.float32)
        rest = left - high
        none = jnp.zeros((32, pixels), jnp.float32)
        stacked = jnp.concatenate([none, high, rest, high, rest], 0)
        residual[group] = stacked.astype(jnp.bfloat16)
        stacked = jnp.concatenate([none, high, rest, jnp.zeros((48, pixels), jnp.float32)], 0)
        across[group] = stacked.T.astype(jnp.bfloat16)
    basis_out = jnp.where(
        lax.broadcasted_iota(jnp.int32, (LANES, pixels), 0) < 8, pixel_basis(LANES), 0.0
    )
    across[groups] = basis_out.T.astype(jnp.bfloat16)

    def sum_slopes(step):
        both = [g_high[group] for group in range(groups)]
        both += [g_rest[group] for group in range(groups)]
        shape_sums = dot_nn(jnp.concatenate(both, 0), across[groups])
        for group in range(groups):
            span = pl.ds(pl.multiple_of((group * blocks + step) * LANES, LANES), LANES)
            tone_sums = dot_nn(
                jnp.concatenate([w_high[span, :], w_rest[span, :]], 0), across[group]
            )
            first, second = group * LANES, (groups + group) * LANES
            sums[group] = (
                shape_sums[first : first + LANES]
                + shape_sums[second : second + LANES]
                + tone_sums[:LANES]
                + tone_sums[LANES:]
            ).T

    def place_slopes(step, skip):
        for group in range(groups):
            block = group * blocks + step
            mask = sub == group_ref[step_index, pl.ds(block, 1), :] + skip
            m = [sums[group, i : i + 1, :] for i in range(6)]
            u, v, a, b, c = [fields[pl.ds(block * ROWSUB + f, 1), :] for f in range(5)]
            m_x = m[1] - u * m[0]
            m_y = m[2] - v * m[0]
            rows = [
                a * m_x + b * m_y,
                b * m_x + c * m_y,
                -0.5 * (m[3] - u * (m[1] + m_x)),
                -(m[4] - u * m[2] - v * m_x),
                -0.5 * (m[5] - v * (m[2] + m_y)),
                m[0],
            ]
            for ch in range(3):
                low = 32 + ch * ROWSUB
                tint = (
                    sums[group, low : low + ROWSUB, :]
                    + sums[group, low + 24 : low + 24 + ROWSUB, :]
                )
                rows.append(jnp.sum(jnp.where(own_tile, tint, 0.0), axis=0, keepdims=True))
            rows = [jnp.where(mask, row, 0.0) for row in rows] + [pad]
            placed[group * LANES : (group + 1) * LANES, :] = jnp.concatenate(rows, 0).T

    for group in range(groups):
        placed[group * LANES : (group + 1) * LANES, :] = tall

    lax.fori_loop(0, devices * halves, functools.partial(clear, tables[:1]), 0)

    def backward(index, carry):
        newest = blocks - 1 - index
        later = [jnp.clip(newest + i, 0, blocks - 1) for i in range(4)]
        step = later[0]
        scatter(later[3])
        place_slopes(later[2], jnp.where(newest + 2 < blocks, 0, ROWSUB))
        sum_slopes(later[1])
        out = []
        for group in range(groups):
            at = pl.multiple_of((group * blocks + step) * LANES, LANES)
            q = dot_nn(factors[pl.ds(at, LANES), :], residual[group])
            behind = list(carry[group])
            kept = [[] for _ in range(wide)]
            for s in reversed(range(per_block)):
                span = pl.ds(at + s * ROWSUB, ROWSUB)
                for h in range(wide):
                    w = w_planes[h][span, :]
                    alpha = a_planes[h][span, :]
                    d = q[s * ROWSUB : (s + 1) * ROWSUB, h * LANES : (h + 1) * LANES] - behind[h]
                    kept[h].insert(0, w * d)
                    behind[h] = behind[h] + alpha * d
                if s % 2 == 0:
                    store_split(g_high.at[group], g_rest.at[group], s * ROWSUB, kept)
                    kept = [[] for _ in range(wide)]
            out.append(tuple(behind))
        return tuple(out)

    lax.fori_loop(0, blocks + 3, backward, ((zeros,) * wide,) * groups)

    loss_rows = jnp.broadcast_to(loss, (ROWSUB, LANES))
    stores = []
    for side, skip in ((1, 0), (1, near // 2), (0, 0), (0, near // 2)):
        stage = w_planes[side]

        def collect(owner, carry, side=side, stage=stage):
            start = pl.multiple_of(owner * planes_out, 8)
            turned = []
            for half in range(halves):
                at = pl.multiple_of(((side * near + owner) * halves + half) * LANES, LANES)
                block = tables[0][pl.ds(at, LANES), :]
                for one in tables[1:]:
                    block = block + one[pl.ds(at, LANES), :]
                turned.append(block.T)
            for half in range(halves):
                for f in range(FIELDS):
                    stage[pl.ds(start + f * per_owner + half * ROWSUB, ROWSUB), :] = turned[
                        half
                    ][f * ROWSUB : (f + 1) * ROWSUB, :]
            stage[pl.ds(start + planes_in, ROWSUB), :] = loss_rows
            return carry

        lax.fori_loop(skip, skip + near // 2, collect, 0)
        for first in range(skip, skip + near // 2, part):
            index = side * quarter + first // part
            store = pltpu.make_async_copy(
                stage.at[pl.ds(first * planes_out, part * planes_out)],
                grad_parts[index],
                out_sem.at[index],
            )
            store.start()
            stores.append(store)
    for store in stores:
        store.wait()


def exchange_flips(gy_size):
    bits = list(range(1, gy_size.bit_length() - 1))
    cut = (len(bits) + 1) // 2
    low, high = bits[:cut], bits[cut:]
    return list(zip(low + high, high + low))


def swap(values, devices, even, odd=None):
    flips = (even, even if odd is None else odd)
    pairs = [(i, i ^ flips[i & 1]) for i in range(devices)]
    return lax.ppermute(values, AXES, pairs)


def spread(values, gx_size, gy_size, hold):
    devices = gx_size * gy_size
    order = exchange_flips(gy_size)
    blocks = [values] + [swap(values, devices, z * gy_size) for z in range(1, gx_size)]
    own, other = [], []
    for chunk in range(2):
        values = jnp.concatenate(blocks[chunk * gx_size // 2 : (chunk + 1) * gx_size // 2], 0)
        if chunk == 0:
            values, hold = lax.optimization_barrier((values, hold))
        for even, odd in order[:-1]:
            values = jnp.concatenate([values, swap(values, devices, 1 << even, 1 << odd)], 0)
        even, odd = order[-1]
        last = swap(values, devices, 1 << even, 1 << odd)
        own += [values, last]
        other += [swap(values, devices, 1), swap(last, devices, 1)]
    return own + other, hold


def fold(parts, gx_size, gy_size):
    devices = gx_size * gy_size
    order = exchange_flips(gy_size)
    own, other = parts[: PARTS // 2], parts[PARTS // 2 :]
    chunks = [None, None]
    for chunk in (1, 0):
        high = own[2 * chunk + 1] + swap(other[2 * chunk + 1], devices, 1)
        low = own[2 * chunk] + swap(other[2 * chunk], devices, 1)
        even, odd = order[-1]
        values = low + swap(high, devices, 1 << even, 1 << odd)
        for even, odd in reversed(order[:-1]):
            half = values.shape[0] // 2
            values = values[:half] + swap(values[half:], devices, 1 << even, 1 << odd)
        chunks[chunk] = values
    size = 2 * chunks[0].shape[0] // gx_size
    total = chunks[0][:size]
    for z in range(1, gx_size):
        at = z % (gx_size // 2) * size
        block = chunks[z // (gx_size // 2)][at : at + size]
        total = total + swap(block, devices, z * gy_size)
    return total


def per_device(gauss_params, first_moment, second_moment, splat_lists, tile_ids, targets, camera):
    gx_size = lax.axis_size("gx")
    gy_size = lax.axis_size("gy")
    devices = gx_size * gy_size
    params_rows, count = gauss_params.shape
    tiles, depth = splat_lists.shape[1:]
    per_owner = count // LANES
    groups = tiles // ROWSUB
    planes_in = FIELDS * per_owner
    planes_out = planes_in + ROWSUB
    total = tiles * depth
    pixels = SIDE * SIDE

    me = lax.axis_index("gx") * gy_size + lax.axis_index("gy")
    owner = splat_lists // count
    apart = owner ^ me
    local = splat_lists % count
    lows = gx_size // 2
    apart_gx = apart // gy_size
    place = (apart & 1) * (devices // 2) + apart_gx // lows * (devices // 4) + apart_gx % lows
    for bit, (even, odd) in enumerate(exchange_flips(gy_size)):
        taken = jnp.where(owner & 1 == 0, apart >> even, apart >> odd)
        place = place + (taken & 1) * (lows << bit)
    rows = place * (count // ROWSUB) + (local // (ROWSUB * LANES)) * LANES + local % LANES
    which = (local // LANES) % ROWSUB

    def interleave(values):
        return (
            values.reshape(STEPS, groups, ROWSUB, depth)
            .transpose(0, 1, 3, 2)
            .reshape(STEPS, total)
        )

    rows = interleave(rows).reshape(STEPS, total // 16, 16).transpose(0, 2, 1)
    which = interleave(which).reshape(STEPS, total // LANES, LANES)
    middle_x = (tile_ids % IMG_TX * SIDE + SIDE // 2).astype(jnp.float32)
    middle_y = (tile_ids // IMG_TX * SIDE + SIDE // 2).astype(jnp.float32)
    middle = jnp.stack([middle_x, middle_y], 1).reshape(STEPS, 2, groups, ROWSUB)
    middle = middle.transpose(0, 2, 1, 3).reshape(STEPS, 2 * groups, ROWSUB)
    middle = jnp.tile(middle, (1, 1, LANES // ROWSUB))
    target_rows = targets.reshape(STEPS, tiles * 3 * pixels // LANES, LANES)

    vmem = pl.BlockSpec(memory_space=pltpu.VMEM)
    smem = pl.BlockSpec(memory_space=pltpu.SMEM)
    hbm = pl.BlockSpec(memory_space=pl.ANY)
    f32, bf16 = jnp.float32, jnp.bfloat16
    state = jax.ShapeDtypeStruct((params_rows, count), f32)
    field_shape = jax.ShapeDtypeStruct((planes_in, LANES), f32)

    streams = 16
    wide = pixels // LANES
    table_rows = devices * count // ROWSUB
    plane_rows = max(total, devices // 2 * planes_out)
    copies = max(1, min(5, (26 << 20) // (table_rows * LANES * 4)))
    render = functools.partial(
        pl.pallas_call,
        out_shape=(jax.ShapeDtypeStruct((tiles * 3 * pixels // LANES, LANES), f32),)
        + (jax.ShapeDtypeStruct((devices // PARTS * planes_out, LANES), f32),) * PARTS,
        in_specs=[hbm, vmem, vmem, vmem] + [hbm] * PARTS,
        out_specs=(vmem,) + (hbm,) * PARTS,
        scratch_shapes=[
            pltpu.VMEM((groups * LANES, LANES), f32),
            pltpu.VMEM((groups * LANES, LANES), f32),
            pltpu.VMEM((total // LANES * ROWSUB, LANES), f32),
            pltpu.VMEM((total, LANES), bf16),
            pltpu.VMEM((groups, LANES, pixels), bf16),
            pltpu.VMEM((groups + 1, pixels, LANES), bf16),
            pltpu.VMEM((total, pixels), bf16),
            pltpu.VMEM((total, pixels), bf16),
            pltpu.VMEM((groups, LANES, pixels), bf16),
            pltpu.VMEM((groups, LANES, pixels), bf16),
            pltpu.VMEM((groups, LANES, LANES), f32),
            pltpu.SemaphoreType.DMA((PARTS,)),
            pltpu.SemaphoreType.DMA((PARTS,)),
            pltpu.SemaphoreType.DMA((streams,)),
        ]
        + [pltpu.SMEM((total // streams,), jnp.int32)] * streams
        + [pltpu.VMEM((plane_rows, LANES), f32)] * (2 * wide)
        + [pltpu.VMEM((table_rows, LANES), f32)] * copies,
        compiler_params=pltpu.CompilerParams(vmem_limit_bytes=48 << 20),
        name="render",
    )

    params, first, second = gauss_params, first_moment, second_moment
    fields = pl.pallas_call(
        functools.partial(project_kernel, step=0),
        out_shape=field_shape,
        in_specs=[smem, vmem],
        out_specs=vmem,
        name="project",
    )(camera, params)
    settings = (rows, which, middle, target_rows)
    pictures = []
    sums = []
    for step in range(STEPS):
        kernel = functools.partial(
            render_kernel,
            devices=devices,
            per_owner=per_owner,
            groups=groups,
            depth=depth,
            streams=streams,
            step_index=step,
        )
        table, settings = spread(fields, gx_size, gy_size, settings)
        picture, *grads = render(kernel)(*settings, *table)
        pictures.append(picture)
        summed = fold(grads, gx_size, gy_size)
        sums.append(summed)
        more = step + 1 < STEPS
        before = [] if more else sums[:-1]
        result = pl.pallas_call(
            functools.partial(
                update_kernel,
                step=step,
                project_next=more,
                pixel_count=3.0 * pixels * tiles * devices,
            ),
            out_shape=(state, state, state)
            + (field_shape if more else jax.ShapeDtypeStruct((STEPS,), f32),),
            in_specs=[smem] + [vmem] * (4 + len(before)),
            out_specs=(vmem,) * 3 + (vmem if more else smem,),
            scratch_shapes=[pltpu.VMEM((params_rows, count), f32)],
            name="update",
        )(camera, params, first, second, summed, *before)
        params, first, second, fields = result
    rendered = jnp.stack(pictures).reshape(STEPS, tiles, 3, pixels)
    return params, first, second, rendered, fields


def solution(mesh):
    along = P(None, AXES)
    lists = P(None, AXES, None)
    frames = P(None, AXES, None, None)
    return jax.shard_map(
        per_device,
        mesh=mesh,
        in_specs=(along, along, along, lists, along, frames, P()),
        out_specs=(along, along, along, frames, P()),
        check_vma=False,
    )
```

```python
import functools

import jax
import jax.numpy as jnp
from jax import lax
from jax.experimental import pallas as pl
from jax.experimental.pallas import tpu as pltpu
from jax.sharding import PartitionSpec as P

SIDE = 16
NCOEF = 16
STEPS = 2
IMG_TX = 64
IMG_TY = 32

FIELDS = 9
LANES = 128
ROWSUB = 8
PARTS = 8
AXES = ("gx", "gy")

beta_one = 0.9
beta_two = 0.999
adam_eps = 1e-08
learn_rate = 0.01
adam_start = 1000
band_zero = 0.28209479177387814
band_one = 0.4886025119029199
band_two = (
    1.0925484305920792,
    -1.0925484305920792,
    0.31539156525252005,
    -1.0925484305920792,
    0.5462742152960396,
)
band_three = (
    -0.5900435899266435,
    2.890611442640554,
    -0.4570457994644658,
    0.3731763325901154,
    -0.4570457994644658,
    1.445305721320277,
    -0.5900435899266435,
)
LOG2E = 1.4426950408889634
LOG_CAP = -0.01005033585350145


def harmonic_rows(ray_x, ray_y, ray_z):
    sq_x = ray_x * ray_x
    sq_y = ray_y * ray_y
    sq_z = ray_z * ray_z
    return [
        band_zero * jnp.ones_like(ray_x),
        -band_one * ray_y,
        band_one * ray_z,
        -band_one * ray_x,
        band_two[0] * ray_x * ray_y,
        band_two[1] * ray_y * ray_z,
        band_two[2] * (2.0 * sq_z - sq_x - sq_y),
        band_two[3] * ray_x * ray_z,
        band_two[4] * (sq_x - sq_y),
        band_three[0] * ray_y * (3.0 * sq_x - sq_y),
        band_three[1] * ray_x * ray_y * ray_z,
        band_three[2] * ray_y * (4.0 * sq_z - sq_x - sq_y),
        band_three[3] * ray_z * (2.0 * sq_z - 3.0 * sq_x - 3.0 * sq_y),
        band_three[4] * ray_x * (4.0 * sq_z - sq_x - sq_y),
        band_three[5] * ray_z * (sq_x - sq_y),
        band_three[6] * ray_x * (sq_x - 3.0 * sq_y),
    ]


def geometry_rows(p0, p1, p2, p3, p4, p5, p6, cam_x, cam_y):
    screen_u = (p0 - cam_x) / p2
    screen_v = (p1 - cam_y) / p2
    inv_one = p2 * p2 * jnp.exp(-2.0 * p3)
    inv_two = p2 * p2 * jnp.exp(-2.0 * p4)
    cosine = jnp.cos(p5)
    sine = jnp.sin(p5)
    conic_a = cosine * cosine * inv_one + sine * sine * inv_two
    conic_b = cosine * sine * (inv_one - inv_two)
    conic_c = sine * sine * inv_one + cosine * cosine * inv_two
    tail = jnp.log(1.0 + jnp.exp(-jnp.abs(p6)))
    log_opacity = LOG_CAP - (jnp.maximum(-p6, 0.0) + tail)
    return screen_u, screen_v, conic_a, conic_b, conic_c, log_opacity


def ray_rows(screen_u, screen_v):
    image_width = 1.0 * SIDE * IMG_TX
    image_height = 1.0 * SIDE * IMG_TY
    ray_x = (screen_u - 0.5 * image_width) / image_width
    ray_y = (screen_v - 0.5 * image_height) / image_width
    factor = lax.rsqrt(ray_x * ray_x + ray_y * ray_y + 1.0)
    return ray_x, ray_y, factor


def chunk(index):
    return slice(index * LANES, (index + 1) * LANES)


def tiles_of(param_ref, turn):
    size = param_ref.shape[1] // LANES
    for k in range(size):
        turn[pl.ds(k, ROWSUB, stride=size), :] = param_ref[0:ROWSUB, chunk(k)]
    return [turn[i * size : (i + 1) * size, :] for i in range(7)]


def project_to(param_ref, cam_x, cam_y, out_ref, turn, basis_turn):
    size = param_ref.shape[1] // LANES
    geo = geometry_rows(*tiles_of(param_ref, turn), cam_x, cam_y)
    for i, tile in enumerate(geo):
        out_ref[i * size : (i + 1) * size, :] = tile
    ray_x, ray_y, factor = ray_rows(geo[0], geo[1])
    for i, tile in enumerate(harmonic_rows(ray_x * factor, ray_y * factor, factor)):
        basis_turn[i * size : (i + 1) * size, :] = tile
    for k in range(size):
        basis = basis_turn[pl.ds(k, NCOEF, stride=size), :]
        for ch in range(3):
            coef = param_ref[7 + NCOEF * ch : 7 + NCOEF * (ch + 1), chunk(k)]
            at = (6 + ch) * size + k
            out_ref[at : at + 1, :] = 0.5 + jnp.sum(coef * basis, axis=0, keepdims=True)


def project_kernel(cam_ref, param_ref, out_ref, turn, basis_turn, *, step):
    project_to(param_ref, cam_ref[step, 0], cam_ref[step, 1], out_ref, turn, basis_turn)


def gradient_to(param_ref, cam_x, cam_y, grad_ref, full_ref, turn, basis_turn):
    size = param_ref.shape[1] // LANES
    g = [grad_ref[i * size : (i + 1) * size, :] for i in range(6)]
    p0, p1, p2, p3, p4, p5, p6 = tiles_of(param_ref, turn)
    inv_z = 1.0 / p2
    screen_u = (p0 - cam_x) / p2
    screen_v = (p1 - cam_y) / p2
    inv_one = p2 * p2 * jnp.exp(-2.0 * p3)
    inv_two = p2 * p2 * jnp.exp(-2.0 * p4)
    cosine = jnp.cos(p5)
    sine = jnp.sin(p5)
    cc = cosine * cosine
    ss = sine * sine
    cs = cosine * sine
    ray_x, ray_y, factor = ray_rows(screen_u, screen_v)
    nx, ny, nz = ray_x * factor, ray_y * factor, factor
    basis_rows, basis_vjp = jax.vjp(lambda a, b, c: tuple(harmonic_rows(a, b, c)), nx, ny, nz)
    for i, tile in enumerate(basis_rows):
        basis_turn[i * size : (i + 1) * size, :] = tile
    for k in range(size):
        where = pl.ds(k, NCOEF, stride=size)
        basis = basis_turn[where, :]
        d_basis = jnp.zeros_like(basis)
        for ch in range(3):
            rows = slice(7 + NCOEF * ch, 7 + NCOEF * (ch + 1))
            at = (6 + ch) * size + k
            tone = grad_ref[at : at + 1, :]
            full_ref[rows, chunk(k)] = tone * basis
            d_basis = d_basis + tone * param_ref[rows, chunk(k)]
        basis_turn[where, :] = d_basis
    d_nx, d_ny, d_nz = basis_vjp(
        tuple(basis_turn[i * size : (i + 1) * size, :] for i in range(NCOEF))
    )
    dot = d_nx * nx + d_ny * ny + d_nz * nz
    image_width = 1.0 * SIDE * IMG_TX
    d_u = g[0] + factor * (d_nx - nx * dot) / image_width
    d_v = g[1] + factor * (d_ny - ny * dot) / image_width
    d_one = g[2] * cc + g[3] * cs + g[4] * ss
    d_two = g[2] * ss - g[3] * cs + g[4] * cc
    diff = inv_one - inv_two
    d_x = d_u * inv_z
    d_y = d_v * inv_z
    slopes = (
        d_x,
        d_y,
        2.0 * (d_one * inv_one + d_two * inv_two) * inv_z - d_x * screen_u - d_y * screen_v,
        -2.0 * inv_one * d_one,
        -2.0 * inv_two * d_two,
        diff * (2.0 * cs * (g[4] - g[2]) + (cc - ss) * g[3]),
        g[5] / (1.0 + jnp.exp(p6)),
    )
    for i, tile in enumerate(slopes):
        turn[i * size : (i + 1) * size, :] = tile
    for k in range(size):
        full_ref[0:7, chunk(k)] = turn[pl.ds(k, 7, stride=size), :]


def update_kernel(
    cam_ref, param_ref, first_ref, second_ref, grad_ref, *refs, step, project_next, pixel_count
):
    refs, (full_ref, turn, basis_turn) = refs[:-3], refs[-3:]
    if project_next:
        new_param, new_first, new_second, field_ref = refs
    else:
        before, (new_param, new_first, new_second, loss_ref) = refs[:step], refs[step:]
        tail = grad_ref.shape[0] - ROWSUB
        for i, one in enumerate(before + (grad_ref,)):
            loss_ref[i] = jnp.max(one[tail : tail + 1, :]) / pixel_count
    camera = cam_ref[step, 0], cam_ref[step, 1]
    gradient_to(param_ref, *camera, grad_ref, full_ref, turn, basis_turn)
    step_count = adam_start + step + 1
    gradient = full_ref[...]
    first = beta_one * first_ref[...] + (1.0 - beta_one) * gradient
    second = beta_two * second_ref[...] + (1.0 - beta_two) * gradient * gradient
    scaled_first = first / (1.0 - beta_one**step_count)
    scaled_second = second / (1.0 - beta_two**step_count)
    new_first[...] = first
    new_second[...] = second
    new_param[...] = param_ref[...] - learn_rate * scaled_first / (
        jnp.sqrt(scaled_second) + adam_eps
    )
    if project_next:
        camera = cam_ref[step + 1, 0], cam_ref[step + 1, 1]
        project_to(new_param, *camera, field_ref, turn, basis_turn)


def split_two(values):
    high = values.astype(jnp.bfloat16)
    rest = (values - high.astype(jnp.float32)).astype(jnp.bfloat16)
    return high, rest


def pixel_basis(rows):
    pix = lax.broadcasted_iota(jnp.int32, (rows, SIDE * SIDE), 1)
    which = lax.broadcasted_iota(jnp.int32, (rows, SIDE * SIDE), 0)
    x = (pix % SIDE).astype(jnp.float32) + (0.5 - 0.5 * SIDE)
    y = (pix // SIDE).astype(jnp.float32) + (0.5 - 0.5 * SIDE)
    which = which % 8
    out = jnp.where(which == 0, 1.0, 0.0)
    for index, value in enumerate((x, y, x * x, x * y, y * y)):
        out = jnp.where(which == index + 1, value, out)
    return out


def dot_nn(a, b):
    return jnp.dot(a, b, preferred_element_type=jnp.float32)


def render_kernel(
    rows_ref,
    group_ref,
    middle_ref,
    target_ref,
    *refs,
    devices,
    per_owner,
    groups,
    depth,
    streams,
    step_index,
):
    table_parts, refs = refs[:PARTS], refs[PARTS:]
    picture_ref, refs = refs[0], refs[1:]
    grad_parts, refs = refs[:PARTS], refs[PARTS:]
    (
        fresh,
        placed,
        fields,
        factors,
        residual,
        across,
        w_high,
        w_rest,
        g_high,
        g_rest,
        sums,
        in_sem,
        out_sem,
        row_sem,
        *scratch,
    ) = refs
    planes_in = FIELDS * per_owner
    planes_out = planes_in + ROWSUB
    halves = per_owner // ROWSUB
    total = groups * ROWSUB * depth
    row_lists, scratch = scratch[:streams], scratch[streams:]
    blocks = depth * ROWSUB // LANES
    per_block = LANES // ROWSUB
    pixels = SIDE * SIDE
    wide = pixels // LANES
    near = devices // 2
    quarter = PARTS // 2
    part = near // quarter
    w_planes, a_planes, tables = scratch[:wide], scratch[wide : 2 * wide], scratch[2 * wide :]
    table = tables[0]

    loads = [
        pltpu.make_async_copy(
            ref,
            w_planes[i // quarter].at[pl.ds(i % quarter * part * planes_in, part * planes_in)],
            in_sem.at[i],
        )
        for i, ref in enumerate(table_parts)
    ]
    lists = [
        pltpu.make_async_copy(rows_ref.at[step_index, i], one, row_sem.at[i])
        for i, one in enumerate(row_lists)
    ]
    for copy in loads + lists:
        copy.start()

    tall = jnp.zeros((LANES, LANES), jnp.float32)

    def clear(some, index, carry):
        at = pl.multiple_of(index * LANES, LANES)
        for one in some:
            one[pl.ds(at, LANES), :] = tall
        return carry

    lax.fori_loop(0, devices * halves, functools.partial(clear, tables[1:]), 0)

    pad = jnp.zeros((LANES - FIELDS * ROWSUB, LANES), jnp.float32)

    for side in range(2):
        for load in loads[side * quarter : (side + 1) * quarter]:
            load.wait()
        stage = w_planes[side]

        def build(owner, carry, stage=stage, side=side):
            start = pl.multiple_of(owner * planes_in, 8)
            for half in range(halves):
                parts = [
                    stage[pl.ds(start + f * per_owner + half * ROWSUB, ROWSUB), :]
                    for f in range(FIELDS)
                ]
                block = jnp.concatenate(parts + [pad], 0)
                at = pl.multiple_of(((side * near + owner) * halves + half) * LANES, LANES)
                table[pl.ds(at, LANES), :] = block.T
            return carry

        lax.fori_loop(0, near, build, 0, unroll=2)
    for copy in lists:
        copy.wait()

    turns = LANES // streams

    def gather(step):
        for group in range(groups):
            for turn in range(turns):
                place = (group * blocks + step) * turns + turn
                for q in range(streams):
                    at = group * LANES + turn * streams + q
                    fresh[at : at + 1, :] = table[pl.ds(row_lists[q][place], 1), :]

    def scatter(step):
        for group in range(groups):
            for turn in range(turns):
                place = (group * blocks + step) * turns + turn
                for q in range(streams):
                    at = group * LANES + turn * streams + q
                    one = tables[at % len(tables)]
                    row = pl.ds(row_lists[q][place], 1)
                    one[row, :] = one[row, :] + placed[at : at + 1, :]

    sub = lax.broadcasted_iota(jnp.int32, (ROWSUB, LANES), 0)
    lane = lax.broadcasted_iota(jnp.int32, (ROWSUB, LANES), 1)
    own_tile = sub == lane % ROWSUB
    basis_in = jnp.where(
        lax.broadcasted_iota(jnp.int32, (LANES, pixels), 0) < 24, pixel_basis(LANES), 0.0
    ).astype(jnp.bfloat16)
    lit = lax.broadcasted_iota(jnp.int32, (LANES, 3 * LANES), 0) - 32
    lit = jnp.where(lit < 0, -1, lit % 48)
    shown = lax.broadcasted_iota(jnp.int32, (LANES, 3 * LANES), 1) // LANES
    colour_in = jnp.where((lit >= 0) & (lit < 24) & (lit // ROWSUB == shown), 1.0, 0.0)
    colour_in = colour_in.astype(jnp.bfloat16)

    def field_mask(block):
        return sub == group_ref[step_index, pl.ds(block, 1), :]

    def prepare(block, group):
        at = pl.multiple_of(block * LANES, LANES)
        mask = field_mask(block)
        raw = fresh[group * LANES : (group + 1) * LANES, :].T
        rows = []
        for f in range(FIELDS):
            part = jnp.where(mask, raw[f * ROWSUB : (f + 1) * ROWSUB, :], 0.0)
            rows.append(jnp.sum(part, axis=0, keepdims=True))
        u = rows[0] - middle_ref[step_index, 2 * group : 2 * group + 1, :]
        v = rows[1] - middle_ref[step_index, 2 * group + 1 : 2 * group + 2, :]
        rows[0], rows[1] = u, v
        a, b, c = rows[2], rows[3], rows[4]
        for f in range(5):
            fields[pl.ds(block * ROWSUB + f, 1), :] = rows[f]
        au = a * u + b * v
        bv = b * u + c * v
        coefs = (
            LOG2E * (rows[5] - 0.5 * (u * au + v * bv)),
            LOG2E * au,
            LOG2E * bv,
            (-0.5 * LOG2E) * a,
            -LOG2E * b,
            (-0.5 * LOG2E) * c,
        )
        coef = jnp.zeros((ROWSUB, LANES), jnp.float32)
        for i, row in enumerate(coefs):
            coef = jnp.where(sub == i, row, coef)
        high = coef.astype(jnp.bfloat16).astype(jnp.float32)
        rest = coef - high
        mid = rest.astype(jnp.bfloat16).astype(jnp.float32)
        low = rest - mid
        full = [jnp.where(own_tile, rows[6 + ch], 0.0) for ch in range(3)]
        c_high = [part.astype(jnp.bfloat16).astype(jnp.float32) for part in full]
        c_rest = [part - top for part, top in zip(full, c_high)]
        stacked = jnp.concatenate(
            [high, mid, low, jnp.zeros_like(low)] + c_high + c_high + c_rest + c_rest, 0
        )
        factors[pl.ds(at, LANES), :] = stacked.T.astype(jnp.bfloat16)

    def store_split(high_ref, rest_ref, at, values):
        for h in range(wide):
            high, rest = split_two(jnp.concatenate(values[h], 0))
            span = pl.ds(at, high.shape[0])
            high_ref[span, h * LANES : (h + 1) * LANES] = high
            rest_ref[span, h * LANES : (h + 1) * LANES] = rest

    gather(0)
    for group in range(groups):
        prepare(group * blocks, group)
    gather(min(1, blocks - 1))

    def forward(step, carry):
        out = []
        for group in range(groups):
            at = pl.multiple_of((group * blocks + step) * LANES, LANES)
            left = factors[pl.ds(at, LANES), :]
            exponent = dot_nn(left, basis_in)
            tones = dot_nn(left, colour_in)
            trans, sums = list(carry[group][0]), [list(x) for x in carry[group][1]]
            kept = [[] for _ in range(wide)]
            for s in range(per_block):
                span = pl.ds(at + s * ROWSUB, ROWSUB)
                tone = tones[s * ROWSUB : (s + 1) * ROWSUB, :]
                for h in range(wide):
                    e = exponent[s * ROWSUB : (s + 1) * ROWSUB, h * LANES : (h + 1) * LANES]
                    alpha = jnp.exp2(jnp.minimum(e, LOG2E * LOG_CAP))
                    w = trans[h] * alpha
                    trans[h] = trans[h] - w
                    a_planes[h][span, :] = alpha
                    w_planes[h][span, :] = w
                    for ch in range(3):
                        sums[ch][h] = sums[ch][h] + w * tone[:, ch * LANES : (ch + 1) * LANES]
                    kept[h].append(w)
                if s % 2:
                    where = pl.multiple_of(at + (s - 1) * ROWSUB, 2 * ROWSUB)
                    store_split(w_high, w_rest, where, kept)
                    kept = [[] for _ in range(wide)]
            out.append((tuple(trans), tuple(tuple(x) for x in sums)))
        ahead = jnp.minimum(step + 1, blocks - 1)
        for group in range(groups):
            prepare(group * blocks + ahead, group)
        gather(jnp.minimum(step + 2, blocks - 1))
        return tuple(out)

    ones = jnp.ones((ROWSUB, LANES), jnp.float32)
    zeros = jnp.zeros((ROWSUB, LANES), jnp.float32)
    begin = (tuple(ones for _ in range(wide)), tuple((zeros,) * wide for _ in range(3)))
    done = lax.fori_loop(0, blocks, forward, (begin,) * groups)

    loss = jnp.zeros((1, 1), jnp.float32)
    for group in range(groups):
        parts = []
        for ch in range(3):
            pair = []
            for h in range(wide):
                where = pl.ds((group * ROWSUB * 3 + ch) * wide + h, ROWSUB, stride=3 * wide)
                shade = done[group][1][ch][h]
                picture_ref[where, :] = shade
                pair.append(shade - target_ref[step_index, where, :])
            parts.append(jnp.concatenate(pair, 1))
        left = jnp.concatenate(parts, 0)
        square = left * left
        loss = loss + 0.5 * jnp.sum(
            jnp.sum(square, axis=0, keepdims=True), axis=1, keepdims=True
        )
        high = left.astype(jnp.bfloat16).astype(jnp.float32)
        rest = left - high
        none = jnp.zeros((32, pixels), jnp.float32)
        stacked = jnp.concatenate([none, high, rest, high, rest], 0)
        residual[group] = stacked.astype(jnp.bfloat16)
        stacked = jnp.concatenate([none, high, rest, jnp.zeros((48, pixels), jnp.float32)], 0)
        across[group] = stacked.T.astype(jnp.bfloat16)
    basis_out = jnp.where(
        lax.broadcasted_iota(jnp.int32, (LANES, pixels), 0) < 8, pixel_basis(LANES), 0.0
    )
    across[groups] = basis_out.T.astype(jnp.bfloat16)

    def sum_slopes(step):
        both = [g_high[group] for group in range(groups)]
        both += [g_rest[group] for group in range(groups)]
        shape_sums = dot_nn(jnp.concatenate(both, 0), across[groups])
        for group in range(groups):
            span = pl.ds(pl.multiple_of((group * blocks + step) * LANES, LANES), LANES)
            tone_sums = dot_nn(
                jnp.concatenate([w_high[span, :], w_rest[span, :]], 0), across[group]
            )
            first, second = group * LANES, (groups + group) * LANES
            sums[group] = (
                shape_sums[first : first + LANES]
                + shape_sums[second : second + LANES]
                + tone_sums[:LANES]
                + tone_sums[LANES:]
            ).T

    def place_slopes(step, skip):
        for group in range(groups):
            block = group * blocks + step
            mask = sub == group_ref[step_index, pl.ds(block, 1), :] + skip
            m = [sums[group, i : i + 1, :] for i in range(6)]
            u, v, a, b, c = [fields[pl.ds(block * ROWSUB + f, 1), :] for f in range(5)]
            m_x = m[1] - u * m[0]
            m_y = m[2] - v * m[0]
            rows = [
                a * m_x + b * m_y,
                b * m_x + c * m_y,
                -0.5 * (m[3] - u * (m[1] + m_x)),
                -(m[4] - u * m[2] - v * m_x),
                -0.5 * (m[5] - v * (m[2] + m_y)),
                m[0],
            ]
            for ch in range(3):
                low = 32 + ch * ROWSUB
                tint = (
                    sums[group, low : low + ROWSUB, :]
                    + sums[group, low + 24 : low + 24 + ROWSUB, :]
                )
                rows.append(jnp.sum(jnp.where(own_tile, tint, 0.0), axis=0, keepdims=True))
            rows = [jnp.where(mask, row, 0.0) for row in rows] + [pad]
            placed[group * LANES : (group + 1) * LANES, :] = jnp.concatenate(rows, 0).T

    for group in range(groups):
        placed[group * LANES : (group + 1) * LANES, :] = tall

    lax.fori_loop(0, devices * halves, functools.partial(clear, tables[:1]), 0)

    def backward(index, carry):
        newest = blocks - 1 - index
        later = [jnp.clip(newest + i, 0, blocks - 1) for i in range(4)]
        step = later[0]
        scatter(later[3])
        place_slopes(later[2], jnp.where(newest + 2 < blocks, 0, ROWSUB))
        sum_slopes(later[1])
        out = []
        for group in range(groups):
            at = pl.multiple_of((group * blocks + step) * LANES, LANES)
            q = dot_nn(factors[pl.ds(at, LANES), :], residual[group])
            behind = list(carry[group])
            kept = [[] for _ in range(wide)]
            for s in reversed(range(per_block)):
                span = pl.ds(at + s * ROWSUB, ROWSUB)
                for h in range(wide):
                    w = w_planes[h][span, :]
                    alpha = a_planes[h][span, :]
                    d = q[s * ROWSUB : (s + 1) * ROWSUB, h * LANES : (h + 1) * LANES] - behind[h]
                    kept[h].insert(0, w * d)
                    behind[h] = behind[h] + alpha * d
                if s % 2 == 0:
                    store_split(g_high.at[group], g_rest.at[group], s * ROWSUB, kept)
                    kept = [[] for _ in range(wide)]
            out.append(tuple(behind))
        return tuple(out)

    lax.fori_loop(0, blocks + 3, backward, ((zeros,) * wide,) * groups)

    loss_rows = jnp.broadcast_to(loss, (ROWSUB, LANES))
    stores = []
    for side, skip in ((1, 0), (1, near // 2), (0, 0), (0, near // 2)):
        stage = w_planes[side]

        def collect(owner, carry, side=side, stage=stage):
            start = pl.multiple_of(owner * planes_out, 8)
            turned = []
            for half in range(halves):
                at = pl.multiple_of(((side * near + owner) * halves + half) * LANES, LANES)
                block = tables[0][pl.ds(at, LANES), :]
                for one in tables[1:]:
                    block = block + one[pl.ds(at, LANES), :]
                turned.append(block.T)
            for half in range(halves):
                for f in range(FIELDS):
                    stage[pl.ds(start + f * per_owner + half * ROWSUB, ROWSUB), :] = turned[
                        half
                    ][f * ROWSUB : (f + 1) * ROWSUB, :]
            stage[pl.ds(start + planes_in, ROWSUB), :] = loss_rows
            return carry

        lax.fori_loop(skip, skip + near // 2, collect, 0)
        for first in range(skip, skip + near // 2, part):
            index = side * quarter + first // part
            store = pltpu.make_async_copy(
                stage.at[pl.ds(first * planes_out, part * planes_out)],
                grad_parts[index],
                out_sem.at[index],
            )
            store.start()
            stores.append(store)
    for store in stores:
        store.wait()


def exchange_flips(gy_size):
    bits = list(range(1, gy_size.bit_length() - 1))
    cut = (len(bits) + 1) // 2
    low, high = bits[:cut], bits[cut:]
    return list(zip(low + high, high + low))


def swap(values, devices, even, odd=None):
    flips = (even, even if odd is None else odd)
    pairs = [(i, i ^ flips[i & 1]) for i in range(devices)]
    return lax.ppermute(values, AXES, pairs)


def spread(values, gx_size, gy_size, hold):
    devices = gx_size * gy_size
    order = exchange_flips(gy_size)
    blocks = [values] + [swap(values, devices, z * gy_size) for z in range(1, gx_size)]
    own, other = [], []
    for chunk in range(2):
        values = jnp.concatenate(blocks[chunk * gx_size // 2 : (chunk + 1) * gx_size // 2], 0)
        if chunk == 0:
            values, hold = lax.optimization_barrier((values, hold))
        for even, odd in order[:-1]:
            values = jnp.concatenate([values, swap(values, devices, 1 << even, 1 << odd)], 0)
        even, odd = order[-1]
        last = swap(values, devices, 1 << even, 1 << odd)
        own += [values, last]
        other += [swap(values, devices, 1), swap(last, devices, 1)]
    return own + other, hold


def fold(parts, gx_size, gy_size):
    devices = gx_size * gy_size
    order = exchange_flips(gy_size)
    own, other = parts[: PARTS // 2], parts[PARTS // 2 :]
    chunks = [None, None]
    for chunk in (1, 0):
        high = own[2 * chunk + 1] + swap(other[2 * chunk + 1], devices, 1)
        low = own[2 * chunk] + swap(other[2 * chunk], devices, 1)
        even, odd = order[-1]
        values = low + swap(high, devices, 1 << even, 1 << odd)
        for even, odd in reversed(order[:-1]):
            half = values.shape[0] // 2
            values = values[:half] + swap(values[half:], devices, 1 << even, 1 << odd)
        chunks[chunk] = values
    size = 2 * chunks[0].shape[0] // gx_size
    total = chunks[0][:size]
    for z in range(1, gx_size):
        at = z % (gx_size // 2) * size
        block = chunks[z // (gx_size // 2)][at : at + size]
        total = total + swap(block, devices, z * gy_size)
    return total


def per_device(gauss_params, first_moment, second_moment, splat_lists, tile_ids, targets, camera):
    gx_size = lax.axis_size("gx")
    gy_size = lax.axis_size("gy")
    devices = gx_size * gy_size
    params_rows, count = gauss_params.shape
    tiles, depth = splat_lists.shape[1:]
    per_owner = count // LANES
    groups = tiles // ROWSUB
    planes_in = FIELDS * per_owner
    planes_out = planes_in + ROWSUB
    total = tiles * depth
    pixels = SIDE * SIDE

    me = lax.axis_index("gx") * gy_size + lax.axis_index("gy")
    owner = splat_lists // count
    apart = owner ^ me
    local = splat_lists % count
    lows = gx_size // 2
    apart_gx = apart // gy_size
    place = (apart & 1) * (devices // 2) + apart_gx // lows * (devices // 4) + apart_gx % lows
    for bit, (even, odd) in enumerate(exchange_flips(gy_size)):
        taken = jnp.where(owner & 1 == 0, apart >> even, apart >> odd)
        place = place + (taken & 1) * (lows << bit)
    rows = place * (count // ROWSUB) + (local // (ROWSUB * LANES)) * LANES + local % LANES
    which = (local // LANES) % ROWSUB

    def interleave(values):
        return (
            values.reshape(STEPS, groups, ROWSUB, depth)
            .transpose(0, 1, 3, 2)
            .reshape(STEPS, total)
        )

    rows = interleave(rows).reshape(STEPS, total // 16, 16).transpose(0, 2, 1)
    which = interleave(which).reshape(STEPS, total // LANES, LANES)
    middle_x = (tile_ids % IMG_TX * SIDE + SIDE // 2).astype(jnp.float32)
    middle_y = (tile_ids // IMG_TX * SIDE + SIDE // 2).astype(jnp.float32)
    middle = jnp.stack([middle_x, middle_y], 1).reshape(STEPS, 2, groups, ROWSUB)
    middle = middle.transpose(0, 2, 1, 3).reshape(STEPS, 2 * groups, ROWSUB)
    middle = jnp.tile(middle, (1, 1, LANES // ROWSUB))
    target_rows = targets.reshape(STEPS, tiles * 3 * pixels // LANES, LANES)

    vmem = pl.BlockSpec(memory_space=pltpu.VMEM)
    smem = pl.BlockSpec(memory_space=pltpu.SMEM)
    hbm = pl.BlockSpec(memory_space=pl.ANY)
    f32, bf16 = jnp.float32, jnp.bfloat16
    state = jax.ShapeDtypeStruct((params_rows, count), f32)
    field_shape = jax.ShapeDtypeStruct((planes_in, LANES), f32)

    streams = 16
    wide = pixels // LANES
    table_rows = devices * count // ROWSUB
    plane_rows = max(total, devices // 2 * planes_out)
    copies = max(1, min(5, (26 << 20) // (table_rows * LANES * 4)))
    render = functools.partial(
        pl.pallas_call,
        out_shape=(jax.ShapeDtypeStruct((tiles * 3 * pixels // LANES, LANES), f32),)
        + (jax.ShapeDtypeStruct((devices // PARTS * planes_out, LANES), f32),) * PARTS,
        in_specs=[hbm, vmem, vmem, vmem] + [hbm] * PARTS,
        out_specs=(vmem,) + (hbm,) * PARTS,
        scratch_shapes=[
            pltpu.VMEM((groups * LANES, LANES), f32),
            pltpu.VMEM((groups * LANES, LANES), f32),
            pltpu.VMEM((total // LANES * ROWSUB, LANES), f32),
            pltpu.VMEM((total, LANES), bf16),
            pltpu.VMEM((groups, LANES, pixels), bf16),
            pltpu.VMEM((groups + 1, pixels, LANES), bf16),
            pltpu.VMEM((total, pixels), bf16),
            pltpu.VMEM((total, pixels), bf16),
            pltpu.VMEM((groups, LANES, pixels), bf16),
            pltpu.VMEM((groups, LANES, pixels), bf16),
            pltpu.VMEM((groups, LANES, LANES), f32),
            pltpu.SemaphoreType.DMA((PARTS,)),
            pltpu.SemaphoreType.DMA((PARTS,)),
            pltpu.SemaphoreType.DMA((streams,)),
        ]
        + [pltpu.SMEM((total // streams,), jnp.int32)] * streams
        + [pltpu.VMEM((plane_rows, LANES), f32)] * (2 * wide)
        + [pltpu.VMEM((table_rows, LANES), f32)] * copies,
        compiler_params=pltpu.CompilerParams(vmem_limit_bytes=48 << 20),
        name="render",
    )

    turns = [
        pltpu.VMEM((ROWSUB * per_owner, LANES), f32),
        pltpu.VMEM((NCOEF * per_owner, LANES), f32),
    ]
    params, first, second = gauss_params, first_moment, second_moment
    fields = pl.pallas_call(
        functools.partial(project_kernel, step=0),
        out_shape=field_shape,
        in_specs=[smem, vmem],
        out_specs=vmem,
        scratch_shapes=turns,
        name="project",
    )(camera, params)
    settings = (rows, which, middle, target_rows)
    pictures = []
    sums = []
    for step in range(STEPS):
        kernel = functools.partial(
            render_kernel,
            devices=devices,
            per_owner=per_owner,
            groups=groups,
            depth=depth,
            streams=streams,
            step_index=step,
        )
        table, settings = spread(fields, gx_size, gy_size, settings)
        picture, *grads = render(kernel)(*settings, *table)
        pictures.append(picture)
        summed = fold(grads, gx_size, gy_size)
        sums.append(summed)
        more = step + 1 < STEPS
        before = [] if more else sums[:-1]
        result = pl.pallas_call(
            functools.partial(
                update_kernel,
                step=step,
                project_next=more,
                pixel_count=3.0 * pixels * tiles * devices,
            ),
            out_shape=(state, state, state)
            + (field_shape if more else jax.ShapeDtypeStruct((STEPS,), f32),),
            in_specs=[smem] + [vmem] * (4 + len(before)),
            out_specs=(vmem,) * 3 + (vmem if more else smem,),
            scratch_shapes=[pltpu.VMEM((params_rows, count), f32)] + turns,
            name="update",
        )(camera, params, first, second, summed, *before)
        params, first, second, fields = result
    rendered = jnp.stack(pictures).reshape(STEPS, tiles, 3, pixels)
    return params, first, second, rendered, fields


def solution(mesh):
    along = P(None, AXES)
    lists = P(None, AXES, None)
    frames = P(None, AXES, None, None)
    return jax.shard_map(
        per_device,
        mesh=mesh,
        in_specs=(along, along, along, lists, along, frames, P()),
        out_specs=(along, along, along, frames, P()),
        check_vma=False,
    )
```

```python
import functools

import jax
import jax.numpy as jnp
from jax import lax
from jax.experimental import pallas as pl
from jax.experimental.pallas import tpu as pltpu
from jax.sharding import PartitionSpec as P

SIDE = 16
NCOEF = 16
STEPS = 2
IMG_TX = 64
IMG_TY = 32

FIELDS = 9
LANES = 128
ROWSUB = 8
PARTS = 8
AXES = ("gx", "gy")

beta_one = 0.9
beta_two = 0.999
adam_eps = 1e-08
learn_rate = 0.01
adam_start = 1000
band_zero = 0.28209479177387814
band_one = 0.4886025119029199
band_two = (
    1.0925484305920792,
    -1.0925484305920792,
    0.31539156525252005,
    -1.0925484305920792,
    0.5462742152960396,
)
band_three = (
    -0.5900435899266435,
    2.890611442640554,
    -0.4570457994644658,
    0.3731763325901154,
    -0.4570457994644658,
    1.445305721320277,
    -0.5900435899266435,
)
LOG2E = 1.4426950408889634
LOG_CAP = -0.01005033585350145


def harmonic_rows(ray_x, ray_y, ray_z):
    sq_x = ray_x * ray_x
    sq_y = ray_y * ray_y
    sq_z = ray_z * ray_z
    return [
        band_zero * jnp.ones_like(ray_x),
        -band_one * ray_y,
        band_one * ray_z,
        -band_one * ray_x,
        band_two[0] * ray_x * ray_y,
        band_two[1] * ray_y * ray_z,
        band_two[2] * (2.0 * sq_z - sq_x - sq_y),
        band_two[3] * ray_x * ray_z,
        band_two[4] * (sq_x - sq_y),
        band_three[0] * ray_y * (3.0 * sq_x - sq_y),
        band_three[1] * ray_x * ray_y * ray_z,
        band_three[2] * ray_y * (4.0 * sq_z - sq_x - sq_y),
        band_three[3] * ray_z * (2.0 * sq_z - 3.0 * sq_x - 3.0 * sq_y),
        band_three[4] * ray_x * (4.0 * sq_z - sq_x - sq_y),
        band_three[5] * ray_z * (sq_x - sq_y),
        band_three[6] * ray_x * (sq_x - 3.0 * sq_y),
    ]


def geometry_rows(p0, p1, p2, p3, p4, p5, p6, cam_x, cam_y):
    screen_u = (p0 - cam_x) / p2
    screen_v = (p1 - cam_y) / p2
    inv_one = p2 * p2 * jnp.exp(-2.0 * p3)
    inv_two = p2 * p2 * jnp.exp(-2.0 * p4)
    cosine = jnp.cos(p5)
    sine = jnp.sin(p5)
    conic_a = cosine * cosine * inv_one + sine * sine * inv_two
    conic_b = cosine * sine * (inv_one - inv_two)
    conic_c = sine * sine * inv_one + cosine * cosine * inv_two
    tail = jnp.log(1.0 + jnp.exp(-jnp.abs(p6)))
    log_opacity = LOG_CAP - (jnp.maximum(-p6, 0.0) + tail)
    return screen_u, screen_v, conic_a, conic_b, conic_c, log_opacity


def ray_rows(screen_u, screen_v):
    image_width = 1.0 * SIDE * IMG_TX
    image_height = 1.0 * SIDE * IMG_TY
    ray_x = (screen_u - 0.5 * image_width) / image_width
    ray_y = (screen_v - 0.5 * image_height) / image_width
    factor = lax.rsqrt(ray_x * ray_x + ray_y * ray_y + 1.0)
    return ray_x, ray_y, factor


def chunk(index):
    return slice(index * LANES, (index + 1) * LANES)


def tiles_of(param_ref, turn):
    size = param_ref.shape[1] // LANES
    for k in range(size):
        turn[pl.ds(k, ROWSUB, stride=size), :] = param_ref[0:ROWSUB, chunk(k)]
    return [turn[i * size : (i + 1) * size, :] for i in range(7)]


def project_to(param_ref, cam_x, cam_y, out_ref, turn, basis_turn):
    size = param_ref.shape[1] // LANES
    geo = geometry_rows(*tiles_of(param_ref, turn), cam_x, cam_y)
    for i, tile in enumerate(geo):
        out_ref[i * size : (i + 1) * size, :] = tile
    ray_x, ray_y, factor = ray_rows(geo[0], geo[1])
    for i, tile in enumerate(harmonic_rows(ray_x * factor, ray_y * factor, factor)):
        basis_turn[i * size : (i + 1) * size, :] = tile
    for k in range(size):
        basis = basis_turn[pl.ds(k, NCOEF, stride=size), :]
        for ch in range(3):
            coef = param_ref[7 + NCOEF * ch : 7 + NCOEF * (ch + 1), chunk(k)]
            at = (6 + ch) * size + k
            out_ref[at : at + 1, :] = 0.5 + jnp.sum(coef * basis, axis=0, keepdims=True)


def project_kernel(cam_ref, param_ref, out_ref, turn, basis_turn, *, step):
    project_to(param_ref, cam_ref[step, 0], cam_ref[step, 1], out_ref, turn, basis_turn)


def gradient_to(param_ref, cam_x, cam_y, grad_ref, full_ref, turn, basis_turn):
    size = param_ref.shape[1] // LANES
    g = [grad_ref[i * size : (i + 1) * size, :] for i in range(6)]
    p0, p1, p2, p3, p4, p5, p6 = tiles_of(param_ref, turn)
    inv_z = 1.0 / p2
    screen_u = (p0 - cam_x) / p2
    screen_v = (p1 - cam_y) / p2
    inv_one = p2 * p2 * jnp.exp(-2.0 * p3)
    inv_two = p2 * p2 * jnp.exp(-2.0 * p4)
    cosine = jnp.cos(p5)
    sine = jnp.sin(p5)
    cc = cosine * cosine
    ss = sine * sine
    cs = cosine * sine
    ray_x, ray_y, factor = ray_rows(screen_u, screen_v)
    nx, ny, nz = ray_x * factor, ray_y * factor, factor
    basis_rows, basis_vjp = jax.vjp(lambda a, b, c: tuple(harmonic_rows(a, b, c)), nx, ny, nz)
    for i, tile in enumerate(basis_rows):
        basis_turn[i * size : (i + 1) * size, :] = tile
    for k in range(size):
        where = pl.ds(k, NCOEF, stride=size)
        basis = basis_turn[where, :]
        d_basis = jnp.zeros_like(basis)
        for ch in range(3):
            rows = slice(7 + NCOEF * ch, 7 + NCOEF * (ch + 1))
            at = (6 + ch) * size + k
            tone = grad_ref[at : at + 1, :]
            full_ref[rows, chunk(k)] = tone * basis
            d_basis = d_basis + tone * param_ref[rows, chunk(k)]
        basis_turn[where, :] = d_basis
    d_nx, d_ny, d_nz = basis_vjp(
        tuple(basis_turn[i * size : (i + 1) * size, :] for i in range(NCOEF))
    )
    dot = d_nx * nx + d_ny * ny + d_nz * nz
    image_width = 1.0 * SIDE * IMG_TX
    d_u = g[0] + factor * (d_nx - nx * dot) / image_width
    d_v = g[1] + factor * (d_ny - ny * dot) / image_width
    d_one = g[2] * cc + g[3] * cs + g[4] * ss
    d_two = g[2] * ss - g[3] * cs + g[4] * cc
    diff = inv_one - inv_two
    d_x = d_u * inv_z
    d_y = d_v * inv_z
    slopes = (
        d_x,
        d_y,
        2.0 * (d_one * inv_one + d_two * inv_two) * inv_z - d_x * screen_u - d_y * screen_v,
        -2.0 * inv_one * d_one,
        -2.0 * inv_two * d_two,
        diff * (2.0 * cs * (g[4] - g[2]) + (cc - ss) * g[3]),
        g[5] / (1.0 + jnp.exp(p6)),
    )
    for i, tile in enumerate(slopes):
        turn[i * size : (i + 1) * size, :] = tile
    for k in range(size):
        full_ref[0:7, chunk(k)] = turn[pl.ds(k, 7, stride=size), :]


def update_kernel(
    cam_ref, param_ref, first_ref, second_ref, grad_ref, *refs, step, project_next, pixel_count
):
    refs, (full_ref, turn, basis_turn) = refs[:-3], refs[-3:]
    if project_next:
        new_param, new_first, new_second, field_ref = refs
    else:
        before, (new_param, new_first, new_second, loss_ref) = refs[:step], refs[step:]
        tail = grad_ref.shape[0] - ROWSUB
        for i, one in enumerate(before + (grad_ref,)):
            loss_ref[i] = jnp.max(one[tail : tail + 1, :]) / pixel_count
    camera = cam_ref[step, 0], cam_ref[step, 1]
    gradient_to(param_ref, *camera, grad_ref, full_ref, turn, basis_turn)
    step_count = adam_start + step + 1
    gradient = full_ref[...]
    first = beta_one * first_ref[...] + (1.0 - beta_one) * gradient
    second = beta_two * second_ref[...] + (1.0 - beta_two) * gradient * gradient
    scaled_first = first / (1.0 - beta_one**step_count)
    scaled_second = second / (1.0 - beta_two**step_count)
    new_first[...] = first
    new_second[...] = second
    new_param[...] = param_ref[...] - learn_rate * scaled_first / (
        jnp.sqrt(scaled_second) + adam_eps
    )
    if project_next:
        camera = cam_ref[step + 1, 0], cam_ref[step + 1, 1]
        project_to(new_param, *camera, field_ref, turn, basis_turn)


def split_two(values):
    high = values.astype(jnp.bfloat16)
    rest = (values - high.astype(jnp.float32)).astype(jnp.bfloat16)
    return high, rest


def pixel_basis(rows):
    pix = lax.broadcasted_iota(jnp.int32, (rows, SIDE * SIDE), 1)
    which = lax.broadcasted_iota(jnp.int32, (rows, SIDE * SIDE), 0)
    x = (pix % SIDE).astype(jnp.float32) + (0.5 - 0.5 * SIDE)
    y = (pix // SIDE).astype(jnp.float32) + (0.5 - 0.5 * SIDE)
    which = which % 8
    out = jnp.where(which == 0, 1.0, 0.0)
    for index, value in enumerate((x, y, x * x, x * y, y * y)):
        out = jnp.where(which == index + 1, value, out)
    return out


def dot_nn(a, b):
    return jnp.dot(a, b, preferred_element_type=jnp.float32)


def render_kernel(
    rows_ref,
    group_ref,
    middle_ref,
    target_ref,
    *refs,
    devices,
    per_owner,
    groups,
    depth,
    streams,
    step_index,
):
    table_parts, refs = refs[:PARTS], refs[PARTS:]
    picture_ref, refs = refs[0], refs[1:]
    grad_parts, refs = refs[:PARTS], refs[PARTS:]
    (
        fresh,
        placed,
        fields,
        factors,
        residual,
        across,
        w_high,
        w_rest,
        g_high,
        g_rest,
        sums,
        in_sem,
        out_sem,
        row_sem,
        *scratch,
    ) = refs
    planes_in = FIELDS * per_owner
    planes_out = planes_in + ROWSUB
    halves = per_owner // ROWSUB
    total = groups * ROWSUB * depth
    row_lists, scratch = scratch[:streams], scratch[streams:]
    blocks = depth * ROWSUB // LANES
    per_block = LANES // ROWSUB
    pixels = SIDE * SIDE
    wide = pixels // LANES
    near = devices // 2
    quarter = PARTS // 2
    part = near // quarter
    w_planes, a_planes, tables = scratch[:wide], scratch[wide : 2 * wide], scratch[2 * wide :]
    table = tables[0]

    loads = [
        pltpu.make_async_copy(
            ref,
            w_planes[i // quarter].at[pl.ds(i % quarter * part * planes_in, part * planes_in)],
            in_sem.at[i],
        )
        for i, ref in enumerate(table_parts)
    ]
    lists = [
        pltpu.make_async_copy(rows_ref.at[step_index, i], one, row_sem.at[i])
        for i, one in enumerate(row_lists)
    ]
    for copy in loads + lists:
        copy.start()

    tall = jnp.zeros((LANES, LANES), jnp.float32)

    def clear(some, index, carry):
        at = pl.multiple_of(index * LANES, LANES)
        for one in some:
            one[pl.ds(at, LANES), :] = tall
        return carry

    lax.fori_loop(0, devices * halves, functools.partial(clear, tables[1:]), 0)

    pad = jnp.zeros((LANES - FIELDS * ROWSUB, LANES), jnp.float32)

    for side in range(2):
        for load in loads[side * quarter : (side + 1) * quarter]:
            load.wait()
        stage = w_planes[side]

        def build(owner, carry, stage=stage, side=side):
            start = pl.multiple_of(owner * planes_in, 8)
            for half in range(halves):
                parts = [
                    stage[pl.ds(start + f * per_owner + half * ROWSUB, ROWSUB), :]
                    for f in range(FIELDS)
                ]
                block = jnp.concatenate(parts + [pad], 0)
                at = pl.multiple_of(((side * near + owner) * halves + half) * LANES, LANES)
                table[pl.ds(at, LANES), :] = block.T
            return carry

        lax.fori_loop(0, near, build, 0, unroll=4)
    for copy in lists:
        copy.wait()

    turns = LANES // streams

    def gather(step):
        for group in range(groups):
            for turn in range(turns):
                place = (group * blocks + step) * turns + turn
                for q in range(streams):
                    at = group * LANES + turn * streams + q
                    fresh[at : at + 1, :] = table[pl.ds(row_lists[q][place], 1), :]

    def scatter(step):
        for group in range(groups):
            for turn in range(turns):
                place = (group * blocks + step) * turns + turn
                for q in range(streams):
                    at = group * LANES + turn * streams + q
                    one = tables[at % len(tables)]
                    row = pl.ds(row_lists[q][place], 1)
                    one[row, :] = one[row, :] + placed[at : at + 1, :]

    sub = lax.broadcasted_iota(jnp.int32, (ROWSUB, LANES), 0)
    lane = lax.broadcasted_iota(jnp.int32, (ROWSUB, LANES), 1)
    own_tile = sub == lane % ROWSUB
    basis_in = jnp.where(
        lax.broadcasted_iota(jnp.int32, (LANES, pixels), 0) < 24, pixel_basis(LANES), 0.0
    ).astype(jnp.bfloat16)
    lit = lax.broadcasted_iota(jnp.int32, (LANES, 3 * LANES), 0) - 32
    lit = jnp.where(lit < 0, -1, lit % 48)
    shown = lax.broadcasted_iota(jnp.int32, (LANES, 3 * LANES), 1) // LANES
    colour_in = jnp.where((lit >= 0) & (lit < 24) & (lit // ROWSUB == shown), 1.0, 0.0)
    colour_in = colour_in.astype(jnp.bfloat16)

    def field_mask(block):
        return sub == group_ref[step_index, pl.ds(block, 1), :]

    def prepare(block, group):
        at = pl.multiple_of(block * LANES, LANES)
        mask = field_mask(block)
        raw = fresh[group * LANES : (group + 1) * LANES, :].T
        rows = []
        for f in range(FIELDS):
            part = jnp.where(mask, raw[f * ROWSUB : (f + 1) * ROWSUB, :], 0.0)
            rows.append(jnp.sum(part, axis=0, keepdims=True))
        u = rows[0] - middle_ref[step_index, 2 * group : 2 * group + 1, :]
        v = rows[1] - middle_ref[step_index, 2 * group + 1 : 2 * group + 2, :]
        rows[0], rows[1] = u, v
        a, b, c = rows[2], rows[3], rows[4]
        for f in range(5):
            fields[pl.ds(block * ROWSUB + f, 1), :] = rows[f]
        au = a * u + b * v
        bv = b * u + c * v
        coefs = (
            LOG2E * (rows[5] - 0.5 * (u * au + v * bv)),
            LOG2E * au,
            LOG2E * bv,
            (-0.5 * LOG2E) * a,
            -LOG2E * b,
            (-0.5 * LOG2E) * c,
        )
        coef = jnp.zeros((ROWSUB, LANES), jnp.float32)
        for i, row in enumerate(coefs):
            coef = jnp.where(sub == i, row, coef)
        high = coef.astype(jnp.bfloat16).astype(jnp.float32)
        rest = coef - high
        mid = rest.astype(jnp.bfloat16).astype(jnp.float32)
        low = rest - mid
        full = [jnp.where(own_tile, rows[6 + ch], 0.0) for ch in range(3)]
        c_high = [part.astype(jnp.bfloat16).astype(jnp.float32) for part in full]
        c_rest = [part - top for part, top in zip(full, c_high)]
        stacked = jnp.concatenate(
            [high, mid, low, jnp.zeros_like(low)] + c_high + c_high + c_rest + c_rest, 0
        )
        factors[pl.ds(at, LANES), :] = stacked.T.astype(jnp.bfloat16)

    def store_split(high_ref, rest_ref, at, values):
        for h in range(wide):
            high, rest = split_two(jnp.concatenate(values[h], 0))
            span = pl.ds(at, high.shape[0])
            high_ref[span, h * LANES : (h + 1) * LANES] = high
            rest_ref[span, h * LANES : (h + 1) * LANES] = rest

    gather(0)
    for group in range(groups):
        prepare(group * blocks, group)
    gather(min(1, blocks - 1))

    def forward(step, carry):
        out = []
        for group in range(groups):
            at = pl.multiple_of((group * blocks + step) * LANES, LANES)
            left = factors[pl.ds(at, LANES), :]
            exponent = dot_nn(left, basis_in)
            tones = dot_nn(left, colour_in)
            trans, sums = list(carry[group][0]), [list(x) for x in carry[group][1]]
            kept = [[] for _ in range(wide)]
            for s in range(per_block):
                span = pl.ds(at + s * ROWSUB, ROWSUB)
                tone = tones[s * ROWSUB : (s + 1) * ROWSUB, :]
                for h in range(wide):
                    e = exponent[s * ROWSUB : (s + 1) * ROWSUB, h * LANES : (h + 1) * LANES]
                    alpha = jnp.exp2(jnp.minimum(e, LOG2E * LOG_CAP))
                    w = trans[h] * alpha
                    trans[h] = trans[h] - w
                    a_planes[h][span, :] = alpha
                    w_planes[h][span, :] = w
                    for ch in range(3):
                        sums[ch][h] = sums[ch][h] + w * tone[:, ch * LANES : (ch + 1) * LANES]
                    kept[h].append(w)
                if s % 2:
                    where = pl.multiple_of(at + (s - 1) * ROWSUB, 2 * ROWSUB)
                    store_split(w_high, w_rest, where, kept)
                    kept = [[] for _ in range(wide)]
            out.append((tuple(trans), tuple(tuple(x) for x in sums)))
        ahead = jnp.minimum(step + 1, blocks - 1)
        for group in range(groups):
            prepare(group * blocks + ahead, group)
        gather(jnp.minimum(step + 2, blocks - 1))
        return tuple(out)

    ones = jnp.ones((ROWSUB, LANES), jnp.float32)
    zeros = jnp.zeros((ROWSUB, LANES), jnp.float32)
    begin = (tuple(ones for _ in range(wide)), tuple((zeros,) * wide for _ in range(3)))
    done = lax.fori_loop(0, blocks, forward, (begin,) * groups)

    loss = jnp.zeros((1, 1), jnp.float32)
    for group in range(groups):
        parts = []
        for ch in range(3):
            pair = []
            for h in range(wide):
                where = pl.ds((group * ROWSUB * 3 + ch) * wide + h, ROWSUB, stride=3 * wide)
                shade = done[group][1][ch][h]
                picture_ref[where, :] = shade
                pair.append(shade - target_ref[step_index, where, :])
            parts.append(jnp.concatenate(pair, 1))
        left = jnp.concatenate(parts, 0)
        square = left * left
        loss = loss + 0.5 * jnp.sum(
            jnp.sum(square, axis=0, keepdims=True), axis=1, keepdims=True
        )
        high = left.astype(jnp.bfloat16).astype(jnp.float32)
        rest = left - high
        none = jnp.zeros((32, pixels), jnp.float32)
        stacked = jnp.concatenate([none, high, rest, high, rest], 0)
        residual[group] = stacked.astype(jnp.bfloat16)
        stacked = jnp.concatenate([none, high, rest, jnp.zeros((48, pixels), jnp.float32)], 0)
        across[group] = stacked.T.astype(jnp.bfloat16)
    basis_out = jnp.where(
        lax.broadcasted_iota(jnp.int32, (LANES, pixels), 0) < 8, pixel_basis(LANES), 0.0
    )
    across[groups] = basis_out.T.astype(jnp.bfloat16)

    def sum_slopes(step):
        both = [g_high[group] for group in range(groups)]
        both += [g_rest[group] for group in range(groups)]
        shape_sums = dot_nn(jnp.concatenate(both, 0), across[groups])
        for group in range(groups):
            span = pl.ds(pl.multiple_of((group * blocks + step) * LANES, LANES), LANES)
            tone_sums = dot_nn(
                jnp.concatenate([w_high[span, :], w_rest[span, :]], 0), across[group]
            )
            first, second = group * LANES, (groups + group) * LANES
            sums[group] = (
                shape_sums[first : first + LANES]
                + shape_sums[second : second + LANES]
                + tone_sums[:LANES]
                + tone_sums[LANES:]
            ).T

    def place_slopes(step, skip):
        for group in range(groups):
            block = group * blocks + step
            mask = sub == group_ref[step_index, pl.ds(block, 1), :] + skip
            m = [sums[group, i : i + 1, :] for i in range(6)]
            u, v, a, b, c = [fields[pl.ds(block * ROWSUB + f, 1), :] for f in range(5)]
            m_x = m[1] - u * m[0]
            m_y = m[2] - v * m[0]
            rows = [
                a * m_x + b * m_y,
                b * m_x + c * m_y,
                -0.5 * (m[3] - u * (m[1] + m_x)),
                -(m[4] - u * m[2] - v * m_x),
                -0.5 * (m[5] - v * (m[2] + m_y)),
                m[0],
            ]
            for ch in range(3):
                low = 32 + ch * ROWSUB
                tint = (
                    sums[group, low : low + ROWSUB, :]
                    + sums[group, low + 24 : low + 24 + ROWSUB, :]
                )
                rows.append(jnp.sum(jnp.where(own_tile, tint, 0.0), axis=0, keepdims=True))
            rows = [jnp.where(mask, row, 0.0) for row in rows] + [pad]
            placed[group * LANES : (group + 1) * LANES, :] = jnp.concatenate(rows, 0).T

    for group in range(groups):
        placed[group * LANES : (group + 1) * LANES, :] = tall

    lax.fori_loop(0, devices * halves, functools.partial(clear, tables[:1]), 0)

    def backward(index, carry):
        newest = blocks - 1 - index
        later = [jnp.clip(newest + i, 0, blocks - 1) for i in range(4)]
        step = later[0]
        scatter(later[3])
        place_slopes(later[2], jnp.where(newest + 2 < blocks, 0, ROWSUB))
        sum_slopes(later[1])
        out = []
        for group in range(groups):
            at = pl.multiple_of((group * blocks + step) * LANES, LANES)
            q = dot_nn(factors[pl.ds(at, LANES), :], residual[group])
            behind = list(carry[group])
            kept = [[] for _ in range(wide)]
            for s in reversed(range(per_block)):
                span = pl.ds(at + s * ROWSUB, ROWSUB)
                for h in range(wide):
                    w = w_planes[h][span, :]
                    alpha = a_planes[h][span, :]
                    d = q[s * ROWSUB : (s + 1) * ROWSUB, h * LANES : (h + 1) * LANES] - behind[h]
                    kept[h].insert(0, w * d)
                    behind[h] = behind[h] + alpha * d
                if s % 2 == 0:
                    store_split(g_high.at[group], g_rest.at[group], s * ROWSUB, kept)
                    kept = [[] for _ in range(wide)]
            out.append(tuple(behind))
        return tuple(out)

    lax.fori_loop(0, blocks + 3, backward, ((zeros,) * wide,) * groups)

    loss_rows = jnp.broadcast_to(loss, (ROWSUB, LANES))
    stores = []
    for side, skip in ((1, 0), (1, near // 2), (0, 0), (0, near // 2)):
        stage = w_planes[side]

        def collect(owner, carry, side=side, stage=stage):
            start = pl.multiple_of(owner * planes_out, 8)
            turned = []
            for half in range(halves):
                at = pl.multiple_of(((side * near + owner) * halves + half) * LANES, LANES)
                block = tables[0][pl.ds(at, LANES), :]
                for one in tables[1:]:
                    block = block + one[pl.ds(at, LANES), :]
                turned.append(block.T)
            for half in range(halves):
                for f in range(FIELDS):
                    stage[pl.ds(start + f * per_owner + half * ROWSUB, ROWSUB), :] = turned[
                        half
                    ][f * ROWSUB : (f + 1) * ROWSUB, :]
            stage[pl.ds(start + planes_in, ROWSUB), :] = loss_rows
            return carry

        lax.fori_loop(skip, skip + near // 2, collect, 0, unroll=2)
        for first in range(skip, skip + near // 2, part):
            index = side * quarter + first // part
            store = pltpu.make_async_copy(
                stage.at[pl.ds(first * planes_out, part * planes_out)],
                grad_parts[index],
                out_sem.at[index],
            )
            store.start()
            stores.append(store)
    for store in stores:
        store.wait()


def exchange_flips(gy_size):
    bits = list(range(1, gy_size.bit_length() - 1))
    cut = (len(bits) + 1) // 2
    low, high = bits[:cut], bits[cut:]
    return list(zip(low + high, high + low))


def swap(values, devices, even, odd=None):
    flips = (even, even if odd is None else odd)
    pairs = [(i, i ^ flips[i & 1]) for i in range(devices)]
    return lax.ppermute(values, AXES, pairs)


def spread(values, gx_size, gy_size, hold):
    devices = gx_size * gy_size
    order = exchange_flips(gy_size)
    blocks = [values] + [swap(values, devices, z * gy_size) for z in range(1, gx_size)]
    own, other = [], []
    for chunk in range(2):
        values = jnp.concatenate(blocks[chunk * gx_size // 2 : (chunk + 1) * gx_size // 2], 0)
        if chunk == 0:
            values, hold = lax.optimization_barrier((values, hold))
        for even, odd in order[:-1]:
            values = jnp.concatenate([values, swap(values, devices, 1 << even, 1 << odd)], 0)
        even, odd = order[-1]
        last = swap(values, devices, 1 << even, 1 << odd)
        own += [values, last]
        other += [swap(values, devices, 1), swap(last, devices, 1)]
    return own + other, hold


def fold(parts, gx_size, gy_size):
    devices = gx_size * gy_size
    order = exchange_flips(gy_size)
    own, other = parts[: PARTS // 2], parts[PARTS // 2 :]
    chunks = [None, None]
    for chunk in (1, 0):
        high = own[2 * chunk + 1] + swap(other[2 * chunk + 1], devices, 1)
        low = own[2 * chunk] + swap(other[2 * chunk], devices, 1)
        even, odd = order[-1]
        values = low + swap(high, devices, 1 << even, 1 << odd)
        for even, odd in reversed(order[:-1]):
            half = values.shape[0] // 2
            values = values[:half] + swap(values[half:], devices, 1 << even, 1 << odd)
        chunks[chunk] = values
    size = 2 * chunks[0].shape[0] // gx_size
    total = chunks[0][:size]
    for z in range(1, gx_size):
        at = z % (gx_size // 2) * size
        block = chunks[z // (gx_size // 2)][at : at + size]
        total = total + swap(block, devices, z * gy_size)
    return total


def per_device(gauss_params, first_moment, second_moment, splat_lists, tile_ids, targets, camera):
    gx_size = lax.axis_size("gx")
    gy_size = lax.axis_size("gy")
    devices = gx_size * gy_size
    params_rows, count = gauss_params.shape
    tiles, depth = splat_lists.shape[1:]
    per_owner = count // LANES
    groups = tiles // ROWSUB
    planes_in = FIELDS * per_owner
    planes_out = planes_in + ROWSUB
    total = tiles * depth
    pixels = SIDE * SIDE

    me = lax.axis_index("gx") * gy_size + lax.axis_index("gy")
    owner = splat_lists // count
    apart = owner ^ me
    local = splat_lists % count
    lows = gx_size // 2
    apart_gx = apart // gy_size
    place = (apart & 1) * (devices // 2) + apart_gx // lows * (devices // 4) + apart_gx % lows
    for bit, (even, odd) in enumerate(exchange_flips(gy_size)):
        taken = jnp.where(owner & 1 == 0, apart >> even, apart >> odd)
        place = place + (taken & 1) * (lows << bit)
    rows = place * (count // ROWSUB) + (local // (ROWSUB * LANES)) * LANES + local % LANES
    which = (local // LANES) % ROWSUB

    def interleave(values):
        return (
            values.reshape(STEPS, groups, ROWSUB, depth)
            .transpose(0, 1, 3, 2)
            .reshape(STEPS, total)
        )

    rows = interleave(rows).reshape(STEPS, total // 16, 16).transpose(0, 2, 1)
    which = interleave(which).reshape(STEPS, total // LANES, LANES)
    middle_x = (tile_ids % IMG_TX * SIDE + SIDE // 2).astype(jnp.float32)
    middle_y = (tile_ids // IMG_TX * SIDE + SIDE // 2).astype(jnp.float32)
    middle = jnp.stack([middle_x, middle_y], 1).reshape(STEPS, 2, groups, ROWSUB)
    middle = middle.transpose(0, 2, 1, 3).reshape(STEPS, 2 * groups, ROWSUB)
    middle = jnp.tile(middle, (1, 1, LANES // ROWSUB))
    target_rows = targets.reshape(STEPS, tiles * 3 * pixels // LANES, LANES)

    vmem = pl.BlockSpec(memory_space=pltpu.VMEM)
    smem = pl.BlockSpec(memory_space=pltpu.SMEM)
    hbm = pl.BlockSpec(memory_space=pl.ANY)
    f32, bf16 = jnp.float32, jnp.bfloat16
    state = jax.ShapeDtypeStruct((params_rows, count), f32)
    field_shape = jax.ShapeDtypeStruct((planes_in, LANES), f32)

    streams = 16
    wide = pixels // LANES
    table_rows = devices * count // ROWSUB
    plane_rows = max(total, devices // 2 * planes_out)
    copies = max(1, min(5, (26 << 20) // (table_rows * LANES * 4)))
    render = functools.partial(
        pl.pallas_call,
        out_shape=(jax.ShapeDtypeStruct((tiles * 3 * pixels // LANES, LANES), f32),)
        + (jax.ShapeDtypeStruct((devices // PARTS * planes_out, LANES), f32),) * PARTS,
        in_specs=[hbm, vmem, vmem, vmem] + [hbm] * PARTS,
        out_specs=(vmem,) + (hbm,) * PARTS,
        scratch_shapes=[
            pltpu.VMEM((groups * LANES, LANES), f32),
            pltpu.VMEM((groups * LANES, LANES), f32),
            pltpu.VMEM((total // LANES * ROWSUB, LANES), f32),
            pltpu.VMEM((total, LANES), bf16),
            pltpu.VMEM((groups, LANES, pixels), bf16),
            pltpu.VMEM((groups + 1, pixels, LANES), bf16),
            pltpu.VMEM((total, pixels), bf16),
            pltpu.VMEM((total, pixels), bf16),
            pltpu.VMEM((groups, LANES, pixels), bf16),
            pltpu.VMEM((groups, LANES, pixels), bf16),
            pltpu.VMEM((groups, LANES, LANES), f32),
            pltpu.SemaphoreType.DMA((PARTS,)),
            pltpu.SemaphoreType.DMA((PARTS,)),
            pltpu.SemaphoreType.DMA((streams,)),
        ]
        + [pltpu.SMEM((total // streams,), jnp.int32)] * streams
        + [pltpu.VMEM((plane_rows, LANES), f32)] * (2 * wide)
        + [pltpu.VMEM((table_rows, LANES), f32)] * copies,
        compiler_params=pltpu.CompilerParams(vmem_limit_bytes=48 << 20),
        name="render",
    )

    turns = [
        pltpu.VMEM((ROWSUB * per_owner, LANES), f32),
        pltpu.VMEM((NCOEF * per_owner, LANES), f32),
    ]
    params, first, second = gauss_params, first_moment, second_moment
    fields = pl.pallas_call(
        functools.partial(project_kernel, step=0),
        out_shape=field_shape,
        in_specs=[smem, vmem],
        out_specs=vmem,
        scratch_shapes=turns,
        name="project",
    )(camera, params)
    settings = (rows, which, middle, target_rows)
    pictures = []
    sums = []
    for step in range(STEPS):
        kernel = functools.partial(
            render_kernel,
            devices=devices,
            per_owner=per_owner,
            groups=groups,
            depth=depth,
            streams=streams,
            step_index=step,
        )
        table, settings = spread(fields, gx_size, gy_size, settings)
        picture, *grads = render(kernel)(*settings, *table)
        pictures.append(picture)
        summed = fold(grads, gx_size, gy_size)
        sums.append(summed)
        more = step + 1 < STEPS
        before = [] if more else sums[:-1]
        result = pl.pallas_call(
            functools.partial(
                update_kernel,
                step=step,
                project_next=more,
                pixel_count=3.0 * pixels * tiles * devices,
            ),
            out_shape=(state, state, state)
            + (field_shape if more else jax.ShapeDtypeStruct((STEPS,), f32),),
            in_specs=[smem] + [vmem] * (4 + len(before)),
            out_specs=(vmem,) * 3 + (vmem if more else smem,),
            scratch_shapes=[pltpu.VMEM((params_rows, count), f32)] + turns,
            name="update",
        )(camera, params, first, second, summed, *before)
        params, first, second, fields = result
    rendered = jnp.stack(pictures).reshape(STEPS, tiles, 3, pixels)
    return params, first, second, rendered, fields


def solution(mesh):
    along = P(None, AXES)
    lists = P(None, AXES, None)
    frames = P(None, AXES, None, None)
    return jax.shard_map(
        per_device,
        mesh=mesh,
        in_specs=(along, along, along, lists, along, frames, P()),
        out_specs=(along, along, along, frames, P()),
        check_vma=False,
    )
```

```python
import functools

import jax
import jax.numpy as jnp
from jax import lax
from jax.experimental import pallas as pl
from jax.experimental.pallas import tpu as pltpu
from jax.sharding import PartitionSpec as P

SIDE = 16
NCOEF = 16
STEPS = 2
IMG_TX = 64
IMG_TY = 32

FIELDS = 9
LANES = 128
ROWSUB = 8
PARTS = 8
AXES = ("gx", "gy")

beta_one = 0.9
beta_two = 0.999
adam_eps = 1e-08
learn_rate = 0.01
adam_start = 1000
band_zero = 0.28209479177387814
band_one = 0.4886025119029199
band_two = (
    1.0925484305920792,
    -1.0925484305920792,
    0.31539156525252005,
    -1.0925484305920792,
    0.5462742152960396,
)
band_three = (
    -0.5900435899266435,
    2.890611442640554,
    -0.4570457994644658,
    0.3731763325901154,
    -0.4570457994644658,
    1.445305721320277,
    -0.5900435899266435,
)
LOG2E = 1.4426950408889634
LOG_CAP = -0.01005033585350145


def harmonic_rows(ray_x, ray_y, ray_z):
    sq_x = ray_x * ray_x
    sq_y = ray_y * ray_y
    sq_z = ray_z * ray_z
    return [
        band_zero * jnp.ones_like(ray_x),
        -band_one * ray_y,
        band_one * ray_z,
        -band_one * ray_x,
        band_two[0] * ray_x * ray_y,
        band_two[1] * ray_y * ray_z,
        band_two[2] * (2.0 * sq_z - sq_x - sq_y),
        band_two[3] * ray_x * ray_z,
        band_two[4] * (sq_x - sq_y),
        band_three[0] * ray_y * (3.0 * sq_x - sq_y),
        band_three[1] * ray_x * ray_y * ray_z,
        band_three[2] * ray_y * (4.0 * sq_z - sq_x - sq_y),
        band_three[3] * ray_z * (2.0 * sq_z - 3.0 * sq_x - 3.0 * sq_y),
        band_three[4] * ray_x * (4.0 * sq_z - sq_x - sq_y),
        band_three[5] * ray_z * (sq_x - sq_y),
        band_three[6] * ray_x * (sq_x - 3.0 * sq_y),
    ]


def geometry_rows(p0, p1, p2, p3, p4, p5, p6, cam_x, cam_y):
    screen_u = (p0 - cam_x) / p2
    screen_v = (p1 - cam_y) / p2
    inv_one = p2 * p2 * jnp.exp(-2.0 * p3)
    inv_two = p2 * p2 * jnp.exp(-2.0 * p4)
    cosine = jnp.cos(p5)
    sine = jnp.sin(p5)
    conic_a = cosine * cosine * inv_one + sine * sine * inv_two
    conic_b = cosine * sine * (inv_one - inv_two)
    conic_c = sine * sine * inv_one + cosine * cosine * inv_two
    tail = jnp.log(1.0 + jnp.exp(-jnp.abs(p6)))
    log_opacity = LOG_CAP - (jnp.maximum(-p6, 0.0) + tail)
    return screen_u, screen_v, conic_a, conic_b, conic_c, log_opacity


def ray_rows(screen_u, screen_v):
    image_width = 1.0 * SIDE * IMG_TX
    image_height = 1.0 * SIDE * IMG_TY
    ray_x = (screen_u - 0.5 * image_width) / image_width
    ray_y = (screen_v - 0.5 * image_height) / image_width
    factor = lax.rsqrt(ray_x * ray_x + ray_y * ray_y + 1.0)
    return ray_x, ray_y, factor


def chunk(index):
    return slice(index * LANES, (index + 1) * LANES)


def tiles_of(param_ref, turn):
    size = param_ref.shape[1] // LANES
    for k in range(size):
        turn[pl.ds(k, ROWSUB, stride=size), :] = param_ref[0:ROWSUB, chunk(k)]
    return [turn[i * size : (i + 1) * size, :] for i in range(7)]


def project_to(param_ref, cam_x, cam_y, out_ref, turn, basis_turn):
    size = param_ref.shape[1] // LANES
    geo = geometry_rows(*tiles_of(param_ref, turn), cam_x, cam_y)
    for i, tile in enumerate(geo):
        out_ref[i * size : (i + 1) * size, :] = tile
    ray_x, ray_y, factor = ray_rows(geo[0], geo[1])
    for i, tile in enumerate(harmonic_rows(ray_x * factor, ray_y * factor, factor)):
        basis_turn[i * size : (i + 1) * size, :] = tile
    for k in range(size):
        basis = basis_turn[pl.ds(k, NCOEF, stride=size), :]
        for ch in range(3):
            coef = param_ref[7 + NCOEF * ch : 7 + NCOEF * (ch + 1), chunk(k)]
            at = (6 + ch) * size + k
            out_ref[at : at + 1, :] = 0.5 + jnp.sum(coef * basis, axis=0, keepdims=True)


def project_kernel(cam_ref, param_ref, out_ref, turn, basis_turn, *, step):
    project_to(param_ref, cam_ref[step, 0], cam_ref[step, 1], out_ref, turn, basis_turn)


def gradient_to(param_ref, cam_x, cam_y, grad_ref, full_ref, turn, basis_turn):
    size = param_ref.shape[1] // LANES
    g = [grad_ref[i * size : (i + 1) * size, :] for i in range(6)]
    p0, p1, p2, p3, p4, p5, p6 = tiles_of(param_ref, turn)
    inv_z = 1.0 / p2
    screen_u = (p0 - cam_x) / p2
    screen_v = (p1 - cam_y) / p2
    inv_one = p2 * p2 * jnp.exp(-2.0 * p3)
    inv_two = p2 * p2 * jnp.exp(-2.0 * p4)
    cosine = jnp.cos(p5)
    sine = jnp.sin(p5)
    cc = cosine * cosine
    ss = sine * sine
    cs = cosine * sine
    ray_x, ray_y, factor = ray_rows(screen_u, screen_v)
    nx, ny, nz = ray_x * factor, ray_y * factor, factor
    basis_rows, basis_vjp = jax.vjp(lambda a, b, c: tuple(harmonic_rows(a, b, c)), nx, ny, nz)
    for i, tile in enumerate(basis_rows):
        basis_turn[i * size : (i + 1) * size, :] = tile
    for k in range(size):
        where = pl.ds(k, NCOEF, stride=size)
        basis = basis_turn[where, :]
        d_basis = jnp.zeros_like(basis)
        for ch in range(3):
            rows = slice(7 + NCOEF * ch, 7 + NCOEF * (ch + 1))
            at = (6 + ch) * size + k
            tone = grad_ref[at : at + 1, :]
            full_ref[rows, chunk(k)] = tone * basis
            d_basis = d_basis + tone * param_ref[rows, chunk(k)]
        basis_turn[where, :] = d_basis
    d_nx, d_ny, d_nz = basis_vjp(
        tuple(basis_turn[i * size : (i + 1) * size, :] for i in range(NCOEF))
    )
    dot = d_nx * nx + d_ny * ny + d_nz * nz
    image_width = 1.0 * SIDE * IMG_TX
    d_u = g[0] + factor * (d_nx - nx * dot) / image_width
    d_v = g[1] + factor * (d_ny - ny * dot) / image_width
    d_one = g[2] * cc + g[3] * cs + g[4] * ss
    d_two = g[2] * ss - g[3] * cs + g[4] * cc
    diff = inv_one - inv_two
    d_x = d_u * inv_z
    d_y = d_v * inv_z
    slopes = (
        d_x,
        d_y,
        2.0 * (d_one * inv_one + d_two * inv_two) * inv_z - d_x * screen_u - d_y * screen_v,
        -2.0 * inv_one * d_one,
        -2.0 * inv_two * d_two,
        diff * (2.0 * cs * (g[4] - g[2]) + (cc - ss) * g[3]),
        g[5] / (1.0 + jnp.exp(p6)),
    )
    for i, tile in enumerate(slopes):
        turn[i * size : (i + 1) * size, :] = tile
    for k in range(size):
        full_ref[0:7, chunk(k)] = turn[pl.ds(k, 7, stride=size), :]


def update_kernel(
    cam_ref, param_ref, first_ref, second_ref, grad_ref, *refs, step, project_next, pixel_count
):
    refs, (full_ref, turn, basis_turn) = refs[:-3], refs[-3:]
    if project_next:
        new_param, new_first, new_second, field_ref = refs
    else:
        before, (new_param, new_first, new_second, loss_ref) = refs[:step], refs[step:]
        tail = grad_ref.shape[0] - ROWSUB
        for i, one in enumerate(before + (grad_ref,)):
            loss_ref[i] = jnp.max(one[tail : tail + 1, :]) / pixel_count
    camera = cam_ref[step, 0], cam_ref[step, 1]
    gradient_to(param_ref, *camera, grad_ref, full_ref, turn, basis_turn)
    step_count = adam_start + step + 1
    gradient = full_ref[...]
    first = beta_one * first_ref[...] + (1.0 - beta_one) * gradient
    second = beta_two * second_ref[...] + (1.0 - beta_two) * gradient * gradient
    scaled_first = first / (1.0 - beta_one**step_count)
    scaled_second = second / (1.0 - beta_two**step_count)
    new_first[...] = first
    new_second[...] = second
    new_param[...] = param_ref[...] - learn_rate * scaled_first / (
        jnp.sqrt(scaled_second) + adam_eps
    )
    if project_next:
        camera = cam_ref[step + 1, 0], cam_ref[step + 1, 1]
        project_to(new_param, *camera, field_ref, turn, basis_turn)


def split_two(values):
    high = values.astype(jnp.bfloat16)
    rest = (values - high.astype(jnp.float32)).astype(jnp.bfloat16)
    return high, rest


def pixel_basis(rows):
    pix = lax.broadcasted_iota(jnp.int32, (rows, SIDE * SIDE), 1)
    which = lax.broadcasted_iota(jnp.int32, (rows, SIDE * SIDE), 0)
    x = (pix % SIDE).astype(jnp.float32) + (0.5 - 0.5 * SIDE)
    y = (pix // SIDE).astype(jnp.float32) + (0.5 - 0.5 * SIDE)
    which = which % 8
    out = jnp.where(which == 0, 1.0, 0.0)
    for index, value in enumerate((x, y, x * x, x * y, y * y)):
        out = jnp.where(which == index + 1, value, out)
    return out


def dot_nn(a, b):
    return jnp.dot(a, b, preferred_element_type=jnp.float32)


def render_kernel(
    rows_ref,
    group_ref,
    middle_ref,
    target_ref,
    *refs,
    devices,
    per_owner,
    groups,
    depth,
    streams,
    step_index,
):
    table_parts, refs = refs[:PARTS], refs[PARTS:]
    picture_ref, refs = refs[0], refs[1:]
    grad_parts, refs = refs[:PARTS], refs[PARTS:]
    (
        fresh,
        placed,
        fields,
        factors,
        residual,
        across,
        w_high,
        w_rest,
        g_high,
        g_rest,
        sums,
        in_sem,
        out_sem,
        row_sem,
        *scratch,
    ) = refs
    planes_in = FIELDS * per_owner
    planes_out = planes_in + ROWSUB
    halves = per_owner // ROWSUB
    total = groups * ROWSUB * depth
    row_lists, scratch = scratch[:streams], scratch[streams:]
    blocks = depth * ROWSUB // LANES
    per_block = LANES // ROWSUB
    pixels = SIDE * SIDE
    wide = pixels // LANES
    near = devices // 2
    quarter = PARTS // 2
    part = near // quarter
    w_planes, a_planes, tables = scratch[:wide], scratch[wide : 2 * wide], scratch[2 * wide :]
    table = tables[0]

    loads = [
        pltpu.make_async_copy(
            ref,
            w_planes[i // quarter].at[pl.ds(i % quarter * part * planes_in, part * planes_in)],
            in_sem.at[i],
        )
        for i, ref in enumerate(table_parts)
    ]
    lists = [
        pltpu.make_async_copy(rows_ref.at[step_index, i], one, row_sem.at[i])
        for i, one in enumerate(row_lists)
    ]
    for copy in loads + lists:
        copy.start()

    tall = jnp.zeros((LANES, LANES), jnp.float32)

    def clear(some, index, carry):
        at = pl.multiple_of(index * LANES, LANES)
        for one in some:
            one[pl.ds(at, LANES), :] = tall
        return carry

    lax.fori_loop(0, devices * halves, functools.partial(clear, tables[1:]), 0)

    pad = jnp.zeros((LANES - FIELDS * ROWSUB, LANES), jnp.float32)

    for side in range(2):
        for load in loads[side * quarter : (side + 1) * quarter]:
            load.wait()
        stage = w_planes[side]

        def build(owner, carry, stage=stage, side=side):
            start = pl.multiple_of(owner * planes_in, 8)
            for half in range(halves):
                parts = [
                    stage[pl.ds(start + f * per_owner + half * ROWSUB, ROWSUB), :]
                    for f in range(FIELDS)
                ]
                block = jnp.concatenate(parts + [pad], 0)
                at = pl.multiple_of(((side * near + owner) * halves + half) * LANES, LANES)
                table[pl.ds(at, LANES), :] = block.T
            return carry

        lax.fori_loop(0, near, build, 0, unroll=4)
    for copy in lists:
        copy.wait()

    turns = LANES // streams

    def gather(step):
        for group in range(groups):
            for turn in range(turns):
                place = (group * blocks + step) * turns + turn
                for q in range(streams):
                    at = group * LANES + turn * streams + q
                    fresh[at : at + 1, :] = table[pl.ds(row_lists[q][place], 1), :]

    def scatter(step):
        for group in range(groups):
            for turn in range(turns):
                place = (group * blocks + step) * turns + turn
                for q in range(streams):
                    at = group * LANES + turn * streams + q
                    one = tables[at % len(tables)]
                    row = pl.ds(row_lists[q][place], 1)
                    one[row, :] = one[row, :] + placed[at : at + 1, :]

    sub = lax.broadcasted_iota(jnp.int32, (ROWSUB, LANES), 0)
    lane = lax.broadcasted_iota(jnp.int32, (ROWSUB, LANES), 1)
    own_tile = sub == lane % ROWSUB
    basis_in = jnp.where(
        lax.broadcasted_iota(jnp.int32, (LANES, pixels), 0) < 24, pixel_basis(LANES), 0.0
    ).astype(jnp.bfloat16)
    lit = lax.broadcasted_iota(jnp.int32, (LANES, 3 * LANES), 0) - 32
    lit = jnp.where(lit < 0, -1, lit % 48)
    shown = lax.broadcasted_iota(jnp.int32, (LANES, 3 * LANES), 1) // LANES
    colour_in = jnp.where((lit >= 0) & (lit < 24) & (lit // ROWSUB == shown), 1.0, 0.0)
    colour_in = colour_in.astype(jnp.bfloat16)

    def field_mask(block):
        return sub == group_ref[step_index, pl.ds(block, 1), :]

    def prepare(block, group):
        at = pl.multiple_of(block * LANES, LANES)
        mask = field_mask(block)
        raw = fresh[group * LANES : (group + 1) * LANES, :].T
        rows = []
        for f in range(FIELDS):
            part = jnp.where(mask, raw[f * ROWSUB : (f + 1) * ROWSUB, :], 0.0)
            rows.append(jnp.sum(part, axis=0, keepdims=True))
        u = rows[0] - middle_ref[step_index, 2 * group : 2 * group + 1, :]
        v = rows[1] - middle_ref[step_index, 2 * group + 1 : 2 * group + 2, :]
        rows[0], rows[1] = u, v
        a, b, c = rows[2], rows[3], rows[4]
        for f in range(5):
            fields[pl.ds(block * ROWSUB + f, 1), :] = rows[f]
        au = a * u + b * v
        bv = b * u + c * v
        coefs = (
            LOG2E * (rows[5] - 0.5 * (u * au + v * bv)),
            LOG2E * au,
            LOG2E * bv,
            (-0.5 * LOG2E) * a,
            -LOG2E * b,
            (-0.5 * LOG2E) * c,
        )
        coef = jnp.zeros((ROWSUB, LANES), jnp.float32)
        for i, row in enumerate(coefs):
            coef = jnp.where(sub == i, row, coef)
        high = coef.astype(jnp.bfloat16).astype(jnp.float32)
        rest = coef - high
        mid = rest.astype(jnp.bfloat16).astype(jnp.float32)
        low = rest - mid
        full = [jnp.where(own_tile, rows[6 + ch], 0.0) for ch in range(3)]
        c_high = [part.astype(jnp.bfloat16).astype(jnp.float32) for part in full]
        c_rest = [part - top for part, top in zip(full, c_high)]
        stacked = jnp.concatenate(
            [high, mid, low, jnp.zeros_like(low)] + c_high + c_high + c_rest + c_rest, 0
        )
        factors[pl.ds(at, LANES), :] = stacked.T.astype(jnp.bfloat16)

    def store_split(high_ref, rest_ref, at, values):
        for h in range(wide):
            high, rest = split_two(jnp.concatenate(values[h], 0))
            span = pl.ds(at, high.shape[0])
            high_ref[span, h * LANES : (h + 1) * LANES] = high
            rest_ref[span, h * LANES : (h + 1) * LANES] = rest

    gather(0)
    for group in range(groups):
        prepare(group * blocks, group)
    gather(min(1, blocks - 1))

    def forward(step, carry):
        out = []
        for group in range(groups):
            at = pl.multiple_of((group * blocks + step) * LANES, LANES)
            left = factors[pl.ds(at, LANES), :]
            exponent = dot_nn(left, basis_in)
            tones = dot_nn(left, colour_in)
            trans, sums = list(carry[group][0]), [list(x) for x in carry[group][1]]
            kept = [[] for _ in range(wide)]
            for s in range(per_block):
                span = pl.ds(at + s * ROWSUB, ROWSUB)
                tone = tones[s * ROWSUB : (s + 1) * ROWSUB, :]
                for h in range(wide):
                    e = exponent[s * ROWSUB : (s + 1) * ROWSUB, h * LANES : (h + 1) * LANES]
                    alpha = jnp.exp2(jnp.minimum(e, LOG2E * LOG_CAP))
                    w = trans[h] * alpha
                    trans[h] = trans[h] - w
                    a_planes[h][span, :] = alpha
                    w_planes[h][span, :] = w
                    for ch in range(3):
                        sums[ch][h] = sums[ch][h] + w * tone[:, ch * LANES : (ch + 1) * LANES]
                    kept[h].append(w)
                if s % 2:
                    where = pl.multiple_of(at + (s - 1) * ROWSUB, 2 * ROWSUB)
                    store_split(w_high, w_rest, where, kept)
                    kept = [[] for _ in range(wide)]
            out.append((tuple(trans), tuple(tuple(x) for x in sums)))
        ahead = jnp.minimum(step + 1, blocks - 1)
        for group in range(groups):
            prepare(group * blocks + ahead, group)
        gather(jnp.minimum(step + 2, blocks - 1))
        return tuple(out)

    ones = jnp.ones((ROWSUB, LANES), jnp.float32)
    zeros = jnp.zeros((ROWSUB, LANES), jnp.float32)
    begin = (tuple(ones for _ in range(wide)), tuple((zeros,) * wide for _ in range(3)))
    done = lax.fori_loop(0, blocks, forward, (begin,) * groups)

    loss = jnp.zeros((1, 1), jnp.float32)
    for group in range(groups):
        parts = []
        for ch in range(3):
            pair = []
            for h in range(wide):
                where = pl.ds((group * ROWSUB * 3 + ch) * wide + h, ROWSUB, stride=3 * wide)
                shade = done[group][1][ch][h]
                picture_ref[where, :] = shade
                pair.append(shade - target_ref[step_index, where, :])
            parts.append(jnp.concatenate(pair, 1))
        left = jnp.concatenate(parts, 0)
        square = left * left
        loss = loss + 0.5 * jnp.sum(
            jnp.sum(square, axis=0, keepdims=True), axis=1, keepdims=True
        )
        high = left.astype(jnp.bfloat16).astype(jnp.float32)
        rest = left - high
        none = jnp.zeros((32, pixels), jnp.float32)
        stacked = jnp.concatenate([none, high, rest, high, rest], 0)
        residual[group] = stacked.astype(jnp.bfloat16)
        stacked = jnp.concatenate([none, high, rest, jnp.zeros((48, pixels), jnp.float32)], 0)
        across[group] = stacked.T.astype(jnp.bfloat16)
    basis_out = jnp.where(
        lax.broadcasted_iota(jnp.int32, (LANES, pixels), 0) < 8, pixel_basis(LANES), 0.0
    )
    across[groups] = basis_out.T.astype(jnp.bfloat16)

    def sum_slopes(step):
        both = [g_high[group] for group in range(groups)]
        both += [g_rest[group] for group in range(groups)]
        shape_sums = dot_nn(jnp.concatenate(both, 0), across[groups])
        for group in range(groups):
            span = pl.ds(pl.multiple_of((group * blocks + step) * LANES, LANES), LANES)
            tone_sums = dot_nn(
                jnp.concatenate([w_high[span, :], w_rest[span, :]], 0), across[group]
            )
            first, second = group * LANES, (groups + group) * LANES
            sums[group] = (
                shape_sums[first : first + LANES]
                + shape_sums[second : second + LANES]
                + tone_sums[:LANES]
                + tone_sums[LANES:]
            ).T

    def place_slopes(step, skip):
        for group in range(groups):
            block = group * blocks + step
            mask = sub == group_ref[step_index, pl.ds(block, 1), :] + skip
            m = [sums[group, i : i + 1, :] for i in range(6)]
            u, v, a, b, c = [fields[pl.ds(block * ROWSUB + f, 1), :] for f in range(5)]
            m_x = m[1] - u * m[0]
            m_y = m[2] - v * m[0]
            rows = [
                a * m_x + b * m_y,
                b * m_x + c * m_y,
                -0.5 * (m[3] - u * (m[1] + m_x)),
                -(m[4] - u * m[2] - v * m_x),
                -0.5 * (m[5] - v * (m[2] + m_y)),
                m[0],
            ]
            for ch in range(3):
                low = 32 + ch * ROWSUB
                tint = (
                    sums[group, low : low + ROWSUB, :]
                    + sums[group, low + 24 : low + 24 + ROWSUB, :]
                )
                rows.append(jnp.sum(jnp.where(own_tile, tint, 0.0), axis=0, keepdims=True))
            rows = [jnp.where(mask, row, 0.0) for row in rows] + [pad]
            placed[group * LANES : (group + 1) * LANES, :] = jnp.concatenate(rows, 0).T

    for group in range(groups):
        placed[group * LANES : (group + 1) * LANES, :] = tall

    lax.fori_loop(0, devices * halves, functools.partial(clear, tables[:1]), 0, unroll=4)

    def backward(index, carry):
        newest = blocks - 1 - index
        later = [jnp.clip(newest + i, 0, blocks - 1) for i in range(4)]
        step = later[0]
        scatter(later[3])
        place_slopes(later[2], jnp.where(newest + 2 < blocks, 0, ROWSUB))
        sum_slopes(later[1])
        out = []
        for group in range(groups):
            at = pl.multiple_of((group * blocks + step) * LANES, LANES)
            q = dot_nn(factors[pl.ds(at, LANES), :], residual[group])
            behind = list(carry[group])
            kept = [[] for _ in range(wide)]
            for s in reversed(range(per_block)):
                span = pl.ds(at + s * ROWSUB, ROWSUB)
                for h in range(wide):
                    w = w_planes[h][span, :]
                    alpha = a_planes[h][span, :]
                    d = q[s * ROWSUB : (s + 1) * ROWSUB, h * LANES : (h + 1) * LANES] - behind[h]
                    kept[h].insert(0, w * d)
                    behind[h] = behind[h] + alpha * d
                if s % 2 == 0:
                    store_split(g_high.at[group], g_rest.at[group], s * ROWSUB, kept)
                    kept = [[] for _ in range(wide)]
            out.append(tuple(behind))
        return tuple(out)

    lax.fori_loop(0, blocks + 3, backward, ((zeros,) * wide,) * groups)

    loss_rows = jnp.broadcast_to(loss, (ROWSUB, LANES))
    stores = []
    for side, skip in ((1, 0), (1, near // 2), (0, 0), (0, near // 2)):
        stage = w_planes[side]

        def collect(owner, carry, side=side, stage=stage):
            start = pl.multiple_of(owner * planes_out, 8)
            turned = []
            for half in range(halves):
                at = pl.multiple_of(((side * near + owner) * halves + half) * LANES, LANES)
                block = tables[0][pl.ds(at, LANES), :]
                for one in tables[1:]:
                    block = block + one[pl.ds(at, LANES), :]
                turned.append(block.T)
            for half in range(halves):
                for f in range(FIELDS):
                    stage[pl.ds(start + f * per_owner + half * ROWSUB, ROWSUB), :] = turned[
                        half
                    ][f * ROWSUB : (f + 1) * ROWSUB, :]
            stage[pl.ds(start + planes_in, ROWSUB), :] = loss_rows
            return carry

        lax.fori_loop(skip, skip + near // 2, collect, 0, unroll=4)
        for first in range(skip, skip + near // 2, part):
            index = side * quarter + first // part
            store = pltpu.make_async_copy(
                stage.at[pl.ds(first * planes_out, part * planes_out)],
                grad_parts[index],
                out_sem.at[index],
            )
            store.start()
            stores.append(store)
    for store in stores:
        store.wait()


def exchange_flips(gy_size):
    bits = list(range(1, gy_size.bit_length() - 1))
    cut = (len(bits) + 1) // 2
    low, high = bits[:cut], bits[cut:]
    return list(zip(low + high, high + low))


def swap(values, devices, even, odd=None):
    flips = (even, even if odd is None else odd)
    pairs = [(i, i ^ flips[i & 1]) for i in range(devices)]
    return lax.ppermute(values, AXES, pairs)


def spread(values, gx_size, gy_size, hold):
    devices = gx_size * gy_size
    order = exchange_flips(gy_size)
    blocks = [values] + [swap(values, devices, z * gy_size) for z in range(1, gx_size)]
    own, other = [], []
    for chunk in range(2):
        values = jnp.concatenate(blocks[chunk * gx_size // 2 : (chunk + 1) * gx_size // 2], 0)
        if chunk == 0:
            values, hold = lax.optimization_barrier((values, hold))
        for even, odd in order[:-1]:
            values = jnp.concatenate([values, swap(values, devices, 1 << even, 1 << odd)], 0)
        even, odd = order[-1]
        last = swap(values, devices, 1 << even, 1 << odd)
        own += [values, last]
        other += [swap(values, devices, 1), swap(last, devices, 1)]
    return own + other, hold


def fold(parts, gx_size, gy_size):
    devices = gx_size * gy_size
    order = exchange_flips(gy_size)
    own, other = parts[: PARTS // 2], parts[PARTS // 2 :]
    chunks = [None, None]
    for chunk in (1, 0):
        high = own[2 * chunk + 1] + swap(other[2 * chunk + 1], devices, 1)
        low = own[2 * chunk] + swap(other[2 * chunk], devices, 1)
        even, odd = order[-1]
        values = low + swap(high, devices, 1 << even, 1 << odd)
        for even, odd in reversed(order[:-1]):
            half = values.shape[0] // 2
            values = values[:half] + swap(values[half:], devices, 1 << even, 1 << odd)
        chunks[chunk] = values
    size = 2 * chunks[0].shape[0] // gx_size
    total = chunks[0][:size]
    for z in range(1, gx_size):
        at = z % (gx_size // 2) * size
        block = chunks[z // (gx_size // 2)][at : at + size]
        total = total + swap(block, devices, z * gy_size)
    return total


def per_device(gauss_params, first_moment, second_moment, splat_lists, tile_ids, targets, camera):
    gx_size = lax.axis_size("gx")
    gy_size = lax.axis_size("gy")
    devices = gx_size * gy_size
    params_rows, count = gauss_params.shape
    tiles, depth = splat_lists.shape[1:]
    per_owner = count // LANES
    groups = tiles // ROWSUB
    planes_in = FIELDS * per_owner
    planes_out = planes_in + ROWSUB
    total = tiles * depth
    pixels = SIDE * SIDE

    me = lax.axis_index("gx") * gy_size + lax.axis_index("gy")
    owner = splat_lists // count
    apart = owner ^ me
    local = splat_lists % count
    lows = gx_size // 2
    apart_gx = apart // gy_size
    place = (apart & 1) * (devices // 2) + apart_gx // lows * (devices // 4) + apart_gx % lows
    for bit, (even, odd) in enumerate(exchange_flips(gy_size)):
        taken = jnp.where(owner & 1 == 0, apart >> even, apart >> odd)
        place = place + (taken & 1) * (lows << bit)
    rows = place * (count // ROWSUB) + (local // (ROWSUB * LANES)) * LANES + local % LANES
    which = (local // LANES) % ROWSUB

    def interleave(values):
        return (
            values.reshape(STEPS, groups, ROWSUB, depth)
            .transpose(0, 1, 3, 2)
            .reshape(STEPS, total)
        )

    rows = interleave(rows).reshape(STEPS, total // 16, 16).transpose(0, 2, 1)
    which = interleave(which).reshape(STEPS, total // LANES, LANES)
    middle_x = (tile_ids % IMG_TX * SIDE + SIDE // 2).astype(jnp.float32)
    middle_y = (tile_ids // IMG_TX * SIDE + SIDE // 2).astype(jnp.float32)
    middle = jnp.stack([middle_x, middle_y], 1).reshape(STEPS, 2, groups, ROWSUB)
    middle = middle.transpose(0, 2, 1, 3).reshape(STEPS, 2 * groups, ROWSUB)
    middle = jnp.tile(middle, (1, 1, LANES // ROWSUB))
    target_rows = targets.reshape(STEPS, tiles * 3 * pixels // LANES, LANES)

    vmem = pl.BlockSpec(memory_space=pltpu.VMEM)
    smem = pl.BlockSpec(memory_space=pltpu.SMEM)
    hbm = pl.BlockSpec(memory_space=pl.ANY)
    f32, bf16 = jnp.float32, jnp.bfloat16
    state = jax.ShapeDtypeStruct((params_rows, count), f32)
    field_shape = jax.ShapeDtypeStruct((planes_in, LANES), f32)

    streams = 16
    wide = pixels // LANES
    table_rows = devices * count // ROWSUB
    plane_rows = max(total, devices // 2 * planes_out)
    copies = max(1, min(5, (26 << 20) // (table_rows * LANES * 4)))
    render = functools.partial(
        pl.pallas_call,
        out_shape=(jax.ShapeDtypeStruct((tiles * 3 * pixels // LANES, LANES), f32),)
        + (jax.ShapeDtypeStruct((devices // PARTS * planes_out, LANES), f32),) * PARTS,
        in_specs=[hbm, vmem, vmem, vmem] + [hbm] * PARTS,
        out_specs=(vmem,) + (hbm,) * PARTS,
        scratch_shapes=[
            pltpu.VMEM((groups * LANES, LANES), f32),
            pltpu.VMEM((groups * LANES, LANES), f32),
            pltpu.VMEM((total // LANES * ROWSUB, LANES), f32),
            pltpu.VMEM((total, LANES), bf16),
            pltpu.VMEM((groups, LANES, pixels), bf16),
            pltpu.VMEM((groups + 1, pixels, LANES), bf16),
            pltpu.VMEM((total, pixels), bf16),
            pltpu.VMEM((total, pixels), bf16),
            pltpu.VMEM((groups, LANES, pixels), bf16),
            pltpu.VMEM((groups, LANES, pixels), bf16),
            pltpu.VMEM((groups, LANES, LANES), f32),
            pltpu.SemaphoreType.DMA((PARTS,)),
            pltpu.SemaphoreType.DMA((PARTS,)),
            pltpu.SemaphoreType.DMA((streams,)),
        ]
        + [pltpu.SMEM((total // streams,), jnp.int32)] * streams
        + [pltpu.VMEM((plane_rows, LANES), f32)] * (2 * wide)
        + [pltpu.VMEM((table_rows, LANES), f32)] * copies,
        compiler_params=pltpu.CompilerParams(vmem_limit_bytes=48 << 20),
        name="render",
    )

    turns = [
        pltpu.VMEM((ROWSUB * per_owner, LANES), f32),
        pltpu.VMEM((NCOEF * per_owner, LANES), f32),
    ]
    params, first, second = gauss_params, first_moment, second_moment
    fields = pl.pallas_call(
        functools.partial(project_kernel, step=0),
        out_shape=field_shape,
        in_specs=[smem, vmem],
        out_specs=vmem,
        scratch_shapes=turns,
        name="project",
    )(camera, params)
    settings = (rows, which, middle, target_rows)
    pictures = []
    sums = []
    for step in range(STEPS):
        kernel = functools.partial(
            render_kernel,
            devices=devices,
            per_owner=per_owner,
            groups=groups,
            depth=depth,
            streams=streams,
            step_index=step,
        )
        table, settings = spread(fields, gx_size, gy_size, settings)
        picture, *grads = render(kernel)(*settings, *table)
        pictures.append(picture)
        summed = fold(grads, gx_size, gy_size)
        sums.append(summed)
        more = step + 1 < STEPS
        before = [] if more else sums[:-1]
        result = pl.pallas_call(
            functools.partial(
                update_kernel,
                step=step,
                project_next=more,
                pixel_count=3.0 * pixels * tiles * devices,
            ),
            out_shape=(state, state, state)
            + (field_shape if more else jax.ShapeDtypeStruct((STEPS,), f32),),
            in_specs=[smem] + [vmem] * (4 + len(before)),
            out_specs=(vmem,) * 3 + (vmem if more else smem,),
            scratch_shapes=[pltpu.VMEM((params_rows, count), f32)] + turns,
            name="update",
        )(camera, params, first, second, summed, *before)
        params, first, second, fields = result
    rendered = jnp.stack(pictures).reshape(STEPS, tiles, 3, pixels)
    return params, first, second, rendered, fields


def solution(mesh):
    along = P(None, AXES)
    lists = P(None, AXES, None)
    frames = P(None, AXES, None, None)
    return jax.shard_map(
        per_device,
        mesh=mesh,
        in_specs=(along, along, along, lists, along, frames, P()),
        out_specs=(along, along, along, frames, P()),
        check_vma=False,
    )
```
